32 devices in a mesh: fsdp: 16 (over z, y, x), tp: 2 (over core).
Axes of the slice: x: 2, y: 2, z: 4, core: 2. Of those that a mesh axis runs over, the one named last changes fastest.
Arguments:
- tokens: bfloat16 [2, 16384, 512], P(None, ('fsdp', 'tp')), may hold values from -6 to 6
- gain_attn: float32 [512], replicated, may hold values from 0.5 to 1.5
- gain_ffn: float32 [512], replicated, may hold values from 0.5 to 1.5
- w_query: bfloat16 [512, 512], P('fsdp', 'tp'), may hold values from -0.25 to 0.25
- w_key: bfloat16 [512, 512], P('fsdp', 'tp'), may hold values from -0.25 to 0.25
- w_value: bfloat16 [512, 512], P('fsdp', 'tp'), may hold values from -0.25 to 0.25
- w_out: bfloat16 [512, 512], P('tp', 'fsdp'), may hold values from -0.75 to 0.75
- w_in: bfloat16 [512, 2048], P('fsdp', 'tp'), may hold values from -0.25 to 0.25
- w_down: bfloat16 [2048, 512], P('tp', 'fsdp'), may hold values from -0.125 to 0.125
- segment_ids: int32 [2, 512], P(None, 'fsdp'), may hold values from 0 to 4, as said below
- cotangent: bfloat16 [2, 16384, 512], P(None, ('fsdp', 'tp')), may hold values from -6 to 6
Outputs:
- result: bfloat16 [2, 16384, 512], P(None, ('fsdp', 'tp'))
- grad_tokens: bfloat16 [2, 16384, 512], P(None, ('fsdp', 'tp'))
- grad_gain_attn: float32 [512], P(('fsdp', 'tp'))
- grad_gain_ffn: float32 [512], P(('fsdp', 'tp'))
- grad_query: float32 [512, 512], P('fsdp', 'tp')
- grad_key: float32 [512, 512], P('fsdp', 'tp')
- grad_value: float32 [512, 512], P('fsdp', 'tp')
- grad_out: float32 [512, 512], P('tp', 'fsdp')
- grad_in: float32 [512, 2048], P('fsdp', 'tp')
- grad_down: float32 [2048, 512], P('tp', 'fsdp')
The draws below stay inside these ranges and needn't reach their ends.
Inputs may be any that keep to these rules, and one draw needn't show every extreme that they name: `segment_ids`: within each group of 32 blocks of a micro-batch the ids never fall, begin with a prompt of 0s over a quarter to a half of the blocks, and every id 1 to 4 names a run of one block or more.
All inputs are finite; a program needn't handle non-finite values.
Results may differ from the reference program's by a relative error of at most 0.014.
Values may be sent and summed in bfloat16 or wider, within the bound.
A program may use at most 192 MiB of HBM per device.

```python
import math
import jax
import jax.numpy as jnp
from jax import lax

D = 512
HEAD_DIM = 64
FF = 2048
BLK = 32
ITERS = 8
CONT = 4
MB = 2
SEQ = 1024
NB = 32
TOK = 16384
NBALL = 512
N_FSDP = 16


def draw_segment_ids(key, part):
    blocks = SEQ // BLK
    groups = NBALL * MB // blocks
    places = jnp.arange(blocks)

    def one_group(group_key):
        first_key, second_key = jax.random.split(group_key)
        prompt = jax.random.randint(first_key, (), blocks // 4, blocks // 2 + 1)
        remain = blocks - prompt
        scores = jax.random.randint(second_key, (blocks,), 0, 1 << 20) * blocks + places
        usable = (places >= 1) & (places < remain)
        scores = jnp.where(usable, scores, -1 - places)
        cut_points = lax.top_k(scores, CONT - 1)[1]
        offset = places - prompt
        later = jnp.sum((cut_points[None, :] <= offset[:, None]).astype(jnp.int32), axis=1)
        return jnp.where(offset < 0, 0, 1 + later).astype(jnp.int32)
    keys_all = jax.random.split(key, groups)
    return jax.vmap(one_group)(keys_all).reshape(MB, NBALL)


def block_levels(key, shape, cuts, least, largest):
    gain = 1.0
    for position, blocks in cuts:
        draws = jax.random.uniform(jax.random.fold_in(jax.random.fold_in(key, 6), position), (blocks,), jnp.float32, least / len(cuts), largest / len(cuts))
        gain = gain * jnp.repeat(jnp.exp(draws), shape[position] // blocks).reshape((-1,) + (1,) * (len(shape) - 1 - position))
    return gain


def noise(rng, shape, width, reach, cuts=(), kind=jnp.bfloat16):
    loudness = block_levels(rng, shape, cuts, -0.22, 0.18) if cuts else 1.0
    entries = jax.random.normal(rng, shape, jnp.float32) * width * loudness
    return jnp.minimum(jnp.maximum(entries, -reach), reach).astype(kind)


def setup_inputs(seed: int = 0) -> dict:
    splits = jax.random.split(jax.random.key(seed), 12)
    return {
        "tokens": noise(splits[0], (MB, TOK, D), 1.0, 6.0, ((1, 32),)),
        "gain_attn": jnp.clip(1.0 + 0.1 * jax.random.normal(splits[1], (D,), jnp.float32), 0.5, 1.5),
        "gain_ffn": jnp.clip(1.0 + 0.1 * jax.random.normal(splits[2], (D,), jnp.float32), 0.5, 1.5),
        "w_query": noise(splits[3], (D, D), D ** -0.5, 0.25, ((0, 16), (1, 2))),
        "w_key": noise(splits[4], (D, D), D ** -0.5, 0.25, ((0, 16), (1, 2))),
        "w_value": noise(splits[5], (D, D), D ** -0.5, 0.25, ((0, 16), (1, 2))),
        "w_out": noise(splits[6], (D, D), (D // 8) ** -0.5, 0.75, ((0, 2), (1, 16))),
        "w_in": noise(splits[7], (D, FF), D ** -0.5, 0.25, ((0, 16), (1, 2))),
        "w_down": noise(splits[8], (FF, D), FF ** -0.5, 0.125, ((0, 2), (1, 16))),
        "segment_ids": draw_segment_ids(jax.random.fold_in(splits[11], 71), 0),
        "cotangent": noise(splits[10], (MB, TOK, D), 1.0, 6.0, ((1, 32),)),
    }


highest = lax.Precision.HIGHEST
epsilon = 1e-05

@jax.custom_vjp
def lower_bound(v):
    return lax.optimization_barrier(v.astype(jnp.bfloat16)).astype(jnp.float32)

@jax.custom_vjp
def low_back(v):
    return v

def low_keep(v):
    return (lower_bound(v), None)

def low_pass(kept, grad):
    return (grad,)

def back_keep(v):
    return (v, None)

def back_low(kept, grad):
    return (lower_bound(grad),)
lower_bound.defvjp(low_keep, low_pass)
low_back.defvjp(back_keep, back_low)

def layer_norm(values, gain_vec):
    center = values - lax.optimization_barrier(jnp.mean(values, axis=-1, keepdims=True))
    spread = lax.optimization_barrier(jnp.mean(center * center, axis=-1, keepdims=True))
    return center * lax.rsqrt(spread + epsilon) * gain_vec

def block_mask(segment):
    blocks = segment.shape[0]
    rows_at = jnp.arange(blocks)[:, None]
    cols_at = jnp.arange(blocks)[None, :]
    within = (segment[:, None] == segment[None, :]) & (cols_at <= rows_at)
    prompt = (segment[None, :] == 0) & (segment[:, None] > 0)
    return within | prompt

def balanced_transport_kernel(query_rows, incoming_keys, incoming_values, permitted_mask, quantize_helper):
    head_count, length, head_width = query_rows.shape
    blocks = length // BLK
    query_b = query_rows.reshape(head_count, blocks, BLK, head_width)
    keys_b = incoming_keys.reshape(head_count, blocks, BLK, head_width)
    values_b = incoming_values.reshape(head_count, blocks, BLK, head_width)
    query_mean = lax.optimization_barrier(jnp.mean(query_b, axis=2))
    keys_mean = lax.optimization_barrier(jnp.mean(keys_b, axis=2))
    logits = jnp.einsum('hid,hjd->hij', query_mean, keys_mean, precision=highest) * (BLK / math.sqrt(head_width))
    logits = jnp.where(permitted_mask[None], logits, -1000000000.0)
    for sweep in range(ITERS):
        logits = logits - jax.nn.logsumexp(logits, axis=2, keepdims=True)
        logits = logits - jax.nn.logsumexp(logits, axis=1, keepdims=True)
    sorter = quantize_helper(jnp.exp(logits))
    keys_sorted = quantize_helper(jnp.einsum('hij,hjrd->hird', sorter, keys_b, precision=highest))
    values_sorted = quantize_helper(jnp.einsum('hij,hjrd->hird', sorter, values_b, precision=highest))
    score_scale = 1.0 / math.sqrt(head_width)
    causal = jnp.arange(BLK)[:, None] >= jnp.arange(BLK)[None, :]
    local_scores = jnp.einsum('hird,hisd->hirs', query_b, keys_b, precision=highest) * score_scale
    local_scores = jnp.where(causal, local_scores, -1000000000.0)
    sorted_scores = jnp.einsum('hird,hisd->hirs', query_b, keys_sorted, precision=highest) * score_scale
    scores = jnp.concatenate([local_scores, sorted_scores], axis=3)
    probs = quantize_helper(jax.nn.softmax(scores, axis=3))
    blended_values = jnp.einsum('hirs,hisd->hird', probs[..., :BLK], values_b, precision=highest)
    blended_values = blended_values + jnp.einsum('hirs,hisd->hird', probs[..., BLK:], values_sorted, precision=highest)
    return blended_values.reshape(head_count, length, head_width)

def matmul(left_arg, right_arg):
    return jnp.dot(left_arg, right_arg, precision=highest)

def divide_into_heads(values):
    return values.reshape(values.shape[0], -1, HEAD_DIM).transpose(1, 0, 2)

def merge_head_columns(values):
    return values.transpose(1, 0, 2).reshape(values.shape[1], -1)

def forward(tokens, gain_attn, gain_ffn, w_query, w_key, w_value, w_out, w_in, w_down, permitted_mask):
    normed = lower_bound(layer_norm(tokens, gain_attn))
    query_rows = lower_bound(low_back(matmul(normed, w_query)))
    incoming_keys = lower_bound(low_back(matmul(normed, w_key)))
    incoming_values = lower_bound(low_back(matmul(normed, w_value)))
    blended_values = lower_bound(merge_head_columns(balanced_transport_kernel(divide_into_heads(query_rows), divide_into_heads(incoming_keys), divide_into_heads(incoming_values), permitted_mask, lower_bound)))
    attended = low_back(matmul(blended_values, w_out))
    middle = tokens + attended
    normed_ffn = lower_bound(layer_norm(middle, gain_ffn))
    hidden_pre = low_back(matmul(normed_ffn, w_in))
    hidden = lower_bound(jax.nn.gelu(hidden_pre, approximate=True))
    return middle + matmul(hidden, w_down)

def reference(tokens, gain_attn, gain_ffn, w_query, w_key, w_value, w_out, w_in, w_down, segment_ids, cotangent):
    params = tuple((p.astype(jnp.float32) for p in (gain_attn, gain_ffn, w_query, w_key, w_value, w_out, w_in, w_down)))
    groups = MB * N_FSDP
    token_groups = tokens.astype(jnp.float32).reshape(groups, SEQ, D)
    cot_groups = cotangent.astype(jnp.float32).reshape(groups, SEQ, D)
    segment_groups = segment_ids.reshape(groups, NB)

    def one_group(totals, item):
        group_tokens, group_segments, group_cot = item
        permitted_mask = block_mask(group_segments)

        def layer_fn(*inputs):
            return forward(*inputs, permitted_mask)
        outcome, pull = jax.vjp(layer_fn, group_tokens, *params)
        grads = pull(group_cot)
        totals = tuple((a + b for a, b in zip(totals, grads[1:])))
        return (totals, (outcome.astype(jnp.bfloat16), grads[0].astype(jnp.bfloat16)))
    zeros_all = tuple((jnp.zeros_like(p) for p in params))
    totals, (outputs, grad_rows) = lax.scan(one_group, zeros_all, (token_groups, segment_groups, cot_groups))
    return (outputs.reshape(MB, TOK, D), grad_rows.reshape(MB, TOK, D), totals[0], totals[1], totals[2], totals[3], totals[4], totals[5], totals[6], totals[7])
```

```python
import functools, math
import jax, jax.numpy as jnp
from jax import lax
from jax.experimental import pallas as pl
from jax.experimental.pallas import tpu as pltpu
from jax.sharding import PartitionSpec as P

F32, BF = jnp.float32, jnp.bfloat16
HI = lax.Precision.HIGHEST
HD, BLK, ITERS, NB, D, FF, T = 64, 32, 8, 32, 512, 2048, 1024
HALF = D // 2
COLS = 3 * HALF + HALF + FF
QO, KO, VO, OO, IO, DO = 0, 256, 512, 768, 1024, 2048


def nn(a, b, precision=None):
    return lax.dot_general(a, b, (((1,), (0,)), ((), ())), precision=precision, preferred_element_type=F32)


def nt(a, b, precision=None):
    return lax.dot_general(a, b, (((1,), (1,)), ((), ())), precision=precision, preferred_element_type=F32)


def tn(a, b, precision=None):
    return lax.dot_general(a, b, (((0,), (0,)), ((), ())), precision=precision, preferred_element_type=F32)


def iota(shape, dim):
    return lax.broadcasted_iota(jnp.int32, shape, dim)


def order_matrix(inverse):
    n, m = iota((128, 128), 0), iota((128, 128), 1)
    if inverse:
        n, m = m, n
    return (m == (n & 3) * 32 + (n >> 2)).astype(BF)


def norm_rows(x, gain):
    center = x - jnp.mean(x, axis=1, keepdims=True)
    inv = lax.rsqrt(jnp.mean(center * center, axis=1, keepdims=True) + 1e-05)
    xhat = center * inv
    return xhat, inv


def norm_back(xhat, inv, gain, grad):
    gx = grad * gain
    m1 = jnp.mean(gx, axis=1, keepdims=True)
    m2 = jnp.mean(gx * xhat, axis=1, keepdims=True)
    return inv * (gx - m1 - xhat * m2)


def even_lanes(shape):
    return (iota(shape, len(shape) - 1) & 127) < 64


def stack_heads(x):
    ev = even_lanes(x.shape)
    z = jnp.zeros_like(x)
    return jnp.concatenate([jnp.where(ev, x, z), jnp.where(ev, z, x)], axis=0)


def pick_heads(r):
    n = r.shape[0] // 2
    ev = even_lanes((n, r.shape[1]))
    return jnp.where(ev, r[:n], r[n:])


SCRATCH = dict(
    tokp=((T, D), BF), cotp=((T, D), BF), cott=((D, T), BF), nm=((T, D), BF), nmt=((D, T), BF),
    q=((T, D), BF), k=((T, D), BF), v=((T, D), BF), ks=((T, D), BF), vs=((T, D), BF),
    qm=((NB, D), F32), km=((NB, D), F32), sk=((2 * ITERS, 8 * NB, NB), F32), allow=((NB, NB), F32),
    kr=((8, 128, 128), BF), krt=((8, 128, 128), BF), bias=((128, 256), F32),
    pr=((4, 8, 256, 256), BF), mix=((T, D), BF), mid=((T, D), F32), nf=((T, D), BF), nft=((D, T), BF),
    hid=((T, 512), BF), gp=((T, 512), BF), res=((T, D), F32), gnf=((T, D), F32),
    ga=((T, D), BF), gat=((D, T), BF), gmix=((T, D), BF),
    dq=((T, D), F32), dk=((T, D), F32), dv=((T, D), F32), dks=((T, D), BF), dvs=((T, D), BF),
    dqb=((T, D), BF), dkb=((T, D), BF), dvb=((T, D), BF), ds=((8 * NB, NB), F32),
    gg=((8, D), F32),
)


def loop(n, body, unroll=1):
    lax.fori_loop(0, n, lambda i, c: (body(i), c)[1], 0, unroll=unroll)


def rows(i, n):
    return pl.ds(pl.multiple_of(i * n, n), n)


def st_tokens(s, tok, gain_attn):
    pm = order_matrix(False)

    def body(c):
        x = nn(pm, tok[rows(c, 128), :])
        s.tokp[rows(c, 128), :] = x.astype(BF)
        xhat, _ = norm_rows(x, None)
        s.nm[rows(c, 128), :] = (xhat * gain_attn[...]).astype(BF)
    loop(8, body)


def st_cot(s, cot):
    pm = order_matrix(False)

    def body(c):
        s.cotp[rows(c, 128), :] = nn(pm, cot[rows(c, 128), :]).astype(BF)
    loop(8, body)


def transpose_into(dst, src):
    for c in range(4):
        dst[:, c * 256:(c + 1) * 256] = jnp.transpose(src[c * 256:(c + 1) * 256, :], (1, 0))


def block_sums(x):
    y = jnp.sum(x.reshape(16, 8, x.shape[1]), axis=0)
    return y[0:4] + y[4:8]


def st_qkv(s, w):
    def body(m):
        x = s.nm[rows(m, 256), :]
        for t in range(2):
            out = nn(x, w[t, :, 0:768]).astype(BF)
            cs = slice(t * 256, (t + 1) * 256)
            qv, kv = out[:, 0:256], out[:, 256:512]
            s.q[rows(m, 256), cs] = qv
            s.k[rows(m, 256), cs] = kv
            s.v[rows(m, 256), cs] = out[:, 512:768]
            for ref, val in ((s.qm, qv), (s.km, kv)):
                val = val.astype(F32)
                sums = jnp.concatenate([block_sums(val[:128]), block_sums(val[128:])], axis=0)
                ref[rows(m, 8), cs] = sums * (1.0 / BLK)
    loop(4, body)


def st_sinkhorn(s, seg):
    row = jnp.broadcast_to(seg[...], (NB, NB))
    ri, ci = iota((NB, NB), 0), iota((NB, NB), 1)
    col = jnp.sum(jnp.where(ri == ci, row, 0), axis=1, keepdims=True)
    allow = ((row == col) & (ci <= ri)) | ((row == 0) & (col > 0))
    s.allow[...] = allow.astype(F32)
    parts = []
    for p in range(4):
        cs = slice(p * 128, (p + 1) * 128)
        parts.append(nt(stack_heads(s.qm[:, cs]), s.km[:, cs], precision=HI))
    x = jnp.concatenate(parts, axis=0) * (BLK / math.sqrt(HD))
    mask = jnp.concatenate([allow.astype(F32)] * 8, axis=0) > 0
    x = jnp.where(mask, x, -1000000000.0)
    for it in range(ITERS):
        m = jnp.max(x, axis=1, keepdims=True)
        e = jnp.exp(x - m)
        z = jnp.sum(e, axis=1, keepdims=True)
        s.sk[2 * it] = e * (1.0 / z)
        x = x - (m + jnp.log(z))
        y = x.reshape(8, NB, NB)
        m = jnp.max(y, axis=1, keepdims=True)
        e = jnp.exp(y - m)
        z = jnp.sum(e, axis=1, keepdims=True)
        s.sk[2 * it + 1] = (e * (1.0 / z)).reshape(8 * NB, NB)
        x = (y - (m + jnp.log(z))).reshape(8 * NB, NB)
    sorter = s.sk[2 * ITERS - 1].astype(BF)
    n = iota((128, NB), 0)
    e_mat = (((n >> 4) * 4 + (n & 3)) == iota((128, NB), 1)).astype(BF)
    wide = nt(sorter, e_mat).astype(BF)
    a, b = iota((128, 128), 0), iota((128, 128), 1)
    same = ((a >> 2) & 3) == ((b >> 2) & 3)
    for h in range(8):
        kr = jnp.where(same, nn(e_mat, wide[h * NB:(h + 1) * NB]), 0.0)
        s.kr[h] = kr.astype(BF)
        s.krt[h] = jnp.transpose(kr, (1, 0)).astype(BF)


def gather_chunk(ref, rq, cs):
    return jnp.concatenate([ref[pl.ds(pl.multiple_of(i * 128 + rq * 16, 16), 16), cs] for i in range(8)], axis=0)


def split_pair(x):
    return stack_heads(x)


def st_sort(s):
    def body(rq):
        for p in range(4):
            cs = slice(p * 128, (p + 1) * 128)
            kv = jnp.concatenate([gather_chunk(s.k, rq, cs), gather_chunk(s.v, rq, cs)], axis=1)
            lhs = jnp.concatenate([s.kr[2 * p], s.kr[2 * p + 1]], axis=1)
            out = nn(lhs, split_pair(kv)).astype(BF)
            for i in range(8):
                at = pl.ds(pl.multiple_of(i * 128 + rq * 16, 16), 16)
                s.ks[at, cs] = out[i * 16:(i + 1) * 16, 0:128]
                s.vs[at, cs] = out[i * 16:(i + 1) * 16, 128:256]
    loop(8, body)


def st_bias(s):
    n, m = iota((128, 256), 0), iota((128, 256), 1)
    ok = ((n & 3) == (m & 3)) & ((m >= 128) | ((m >> 2) <= (n >> 2)))
    s.bias[...] = jnp.where(ok, 0.0, -1e30)


def st_attend(s):
    scale = 1.0 / math.sqrt(HD)

    def body(c):
        at = rows(c, 128)
        for p in range(4):
            cs = slice(p * 128, (p + 1) * 128)
            qs = stack_heads(s.q[at, cs])
            kk = jnp.concatenate([s.k[at, cs], s.ks[at, cs]], axis=0)
            vv = jnp.concatenate([s.v[at, cs], s.vs[at, cs]], axis=0)
            b = s.bias[...]
            x = nt(qs, kk) * scale + jnp.concatenate([b, b], axis=0)
            m = jnp.max(x, axis=1, keepdims=True)
            e = jnp.exp(x - m)
            z = jnp.sum(e, axis=1, keepdims=True)
            pb = (e * (1.0 / z)).astype(BF)
            s.pr[p, c] = pb
            s.mix[at, cs] = pick_heads(nn(pb, vv)).astype(BF)
    loop(8, body)


def st_out(s, w, gain_ffn):
    def body(m):
        at = rows(m, 256)
        mid = s.tokp[at, :].astype(F32)
        for t in range(2):
            mid = mid + nt(s.mix[at, t * 256:(t + 1) * 256], w[t, :, OO:OO + HALF])
        s.mid[at, :] = mid
        xhat, _ = norm_rows(mid, None)
        s.nf[at, :] = (xhat * gain_ffn[...]).astype(BF)
    loop(4, body)


def gelu_pair(x):
    k0, k1 = math.sqrt(2.0 / math.pi), 0.044715
    x2 = x * x
    th = jnp.tanh(x * (k0 + (k0 * k1) * x2))
    half = 0.5 + 0.5 * th
    val = x * half
    der = half + (0.5 * x) * (1.0 - th * th) * (k0 + (3 * k0 * k1) * x2)
    return val, der


def st_ffn(s, w, g):
    for t in range(2):
        for u in range(2):
            ic = slice(IO + u * 512, IO + (u + 1) * 512)
            dc = slice(DO + u * 512, DO + (u + 1) * 512)
            first = t == 0 and u == 0

            def body(m, t=t, ic=ic, dc=dc, first=first):
                at = rows(m, 256)
                x = nn(s.nf[at, :], w[t, :, ic])
                gh = nn(s.cotp[at, :], w[t, :, dc])
                val, der = gelu_pair(x)
                hid = val.astype(BF)
                gp = (gh * der).astype(BF)
                s.hid[at, :] = hid
                s.gp[at, :] = gp
                add = nt(hid, w[t, :, dc])
                s.res[at, :] = (s.mid[at, :] if first else s.res[at, :]) + add
                add = nt(gp, w[t, :, ic])
                s.gnf[at, :] = add if first else s.gnf[at, :] + add
            loop(4, body)
            g[t, :, ic] = nn(s.nft[...], s.gp[...]).astype(BF)
            g[t, :, dc] = nn(s.cott[...], s.hid[...]).astype(BF)


def st_mid_back(s, w, g, gain_ffn):
    def body(m, acc):
        at = rows(m, 256)
        xhat, inv = norm_rows(s.mid[at, :], None)
        gnf = s.gnf[at, :]
        acc = acc + jnp.sum((gnf * xhat).reshape(32, 8, D), axis=0)
        gm = s.cotp[at, :].astype(F32) + norm_back(xhat, inv, gain_ffn[...], gnf)
        s.mid[at, :] = gm
        ga = gm.astype(BF)
        s.ga[at, :] = ga
        for t in range(2):
            s.gmix[at, t * 256:(t + 1) * 256] = nn(ga, w[t, :, OO:OO + HALF]).astype(BF)
        return acc
    acc = lax.fori_loop(0, 4, body, jnp.zeros((8, D), F32))
    s.gg[1:2, :] = jnp.sum(acc, axis=0, keepdims=True)
    transpose_into(s.gat, s.ga)
    for t in range(2):
        g[t, :, OO:OO + HALF] = nn(s.gat[...], s.mix[:, t * 256:(t + 1) * 256]).astype(BF)


def st_result(s, out, src):
    pm = order_matrix(True)

    def body(c):
        at = rows(c, 128)
        out[at, :] = nn(pm, src[at, :].astype(BF)).astype(BF)
    loop(8, body)


def st_attend_back(s):
    scale = 1.0 / math.sqrt(HD)

    def body(c):
        at = rows(c, 128)
        for p in range(4):
            cs = slice(p * 128, (p + 1) * 128)
            qs = stack_heads(s.q[at, cs])
            gs = stack_heads(s.gmix[at, cs])
            kk = jnp.concatenate([s.k[at, cs], s.ks[at, cs]], axis=0)
            vv = jnp.concatenate([s.v[at, cs], s.vs[at, cs]], axis=0)
            pb = s.pr[p, c]
            pf = pb.astype(F32)
            dp = nt(gs, vv)
            pd = pf * dp
            dl = jnp.sum(pd, axis=1, keepdims=True)
            ds = ((pd - pf * dl) * scale).astype(BF)
            s.dq[at, cs] = pick_heads(nn(ds, kk))
            dkk = tn(ds, qs)
            dvv = tn(pb, gs)
            s.dk[at, cs] = dkk[:128]
            s.dks[at, cs] = dkk[128:].astype(BF)
            s.dv[at, cs] = dvv[:128]
            s.dvs[at, cs] = dvv[128:].astype(BF)
    loop(8, body)


def st_sort_back(s):
    def body(rq, accs):
        new = []
        for p in range(4):
            cs = slice(p * 128, (p + 1) * 128)
            kv = jnp.concatenate([gather_chunk(s.k, rq, cs), gather_chunk(s.v, rq, cs)], axis=1)
            dkv = jnp.concatenate([gather_chunk(s.dks, rq, cs), gather_chunk(s.dvs, rq, cs)], axis=1)
            st = split_pair(dkv)
            new.append(accs[p] + nt(st, kv))
            lhs = jnp.concatenate([s.krt[2 * p], s.krt[2 * p + 1]], axis=1)
            out = nn(lhs, st)
            for i in range(8):
                at = pl.ds(pl.multiple_of(i * 128 + rq * 16, 16), 16)
                s.dk[at, cs] = s.dk[at, cs] + out[i * 16:(i + 1) * 16, 0:128]
                s.dv[at, cs] = s.dv[at, cs] + out[i * 16:(i + 1) * 16, 128:256]
        return tuple(new)
    accs = lax.fori_loop(0, 8, body, tuple(jnp.zeros((256, 128), F32) for _ in range(4)))
    a, b = iota((128, 128), 0), iota((128, 128), 1)
    same = ((a >> 2) & 3) == ((b >> 2) & 3)
    n = iota((128, NB), 0)
    e_mat = (((n >> 4) * 4 + (n & 3)) == iota((128, NB), 1)).astype(F32)
    for p in range(4):
        for e in range(2):
            x = jnp.where(same, accs[p][e * 128:(e + 1) * 128], 0.0)
            y = nn(x, e_mat, precision=HI)
            s.ds[(2 * p + e) * NB:(2 * p + e + 1) * NB, :] = tn(e_mat, y, precision=HI)


def st_sinkhorn_back(s):
    x = s.ds[...] * s.sk[2 * ITERS - 1]
    for it in reversed(range(ITERS)):
        y = x.reshape(8, NB, NB)
        pk = s.sk[2 * it + 1].reshape(8, NB, NB)
        x = (y - pk * jnp.sum(y, axis=1, keepdims=True)).reshape(8 * NB, NB)
        x = x - s.sk[2 * it] * jnp.sum(x, axis=1, keepdims=True)
    mask = jnp.concatenate([s.allow[...]] * 8, axis=0) > 0
    x = jnp.where(mask, x, 0.0) * (BLK / math.sqrt(HD) / BLK)
    for p in range(4):
        cs = slice(p * 128, (p + 1) * 128)
        x0, x1 = x[(2 * p) * NB:(2 * p + 1) * NB], x[(2 * p + 1) * NB:(2 * p + 2) * NB]
        ev = even_lanes((NB, 128))
        km, qm = s.km[:, cs], s.qm[:, cs]
        dqm = jnp.where(ev, nn(x0, km, precision=HI), nn(x1, km, precision=HI))
        dkm = jnp.where(ev, tn(x0, qm, precision=HI), tn(x1, qm, precision=HI))
        for c in range(8):
            for src, ref, dst in ((dqm, s.dq, s.dqb), (dkm, s.dk, s.dkb)):
                four = src[c * 4:(c + 1) * 4]
                eight = jnp.concatenate([four, four], axis=0)
                val = ref[c * 128:(c + 1) * 128, cs].reshape(16, 8, 128) + eight[None]
                dst[c * 128:(c + 1) * 128, cs] = val.reshape(128, 128).astype(BF)
    s.dvb[...] = s.dv[...].astype(BF)


def st_qkv_back(s, w, g, gain_attn):
    for t in range(2):
        cs = slice(t * 256, (t + 1) * 256)
        for off, ref in ((QO, s.dqb), (KO, s.dkb), (VO, s.dvb)):
            g[t, :, off:off + 256] = nn(s.nmt[...], ref[:, cs]).astype(BF)

    def body(m, acc):
        at = rows(m, 256)
        gn = jnp.zeros((256, D), F32)
        for t in range(2):
            cs = slice(t * 256, (t + 1) * 256)
            lhs = jnp.concatenate([s.dqb[at, cs], s.dkb[at, cs], s.dvb[at, cs]], axis=1)
            gn = gn + nt(lhs, w[t, :, 0:768])
        xhat, inv = norm_rows(s.tokp[at, :].astype(F32), None)
        acc = acc + jnp.sum((gn * xhat).reshape(32, 8, D), axis=0)
        s.mid[at, :] = s.mid[at, :] + norm_back(xhat, inv, gain_attn[...], gn)
        return acc
    acc = lax.fori_loop(0, 4, body, jnp.zeros((8, D), F32))
    s.gg[0:1, :] = jnp.sum(acc, axis=0, keepdims=True)


class Names:
    pass


def compute_all(s, tok, cot, gain_attn, gain_ffn, w, seg, result, gtok, g, stop=99):
    steps = [
        lambda: (st_tokens(s, tok, gain_attn), st_cot(s, cot)),
        lambda: (transpose_into(s.cott, s.cotp), transpose_into(s.nmt, s.nm), st_bias(s)),
        lambda: st_qkv(s, w),
        lambda: st_sinkhorn(s, seg),
        lambda: st_sort(s),
        lambda: st_attend(s),
        lambda: (st_out(s, w, gain_ffn), transpose_into(s.nft, s.nf)),
        lambda: st_ffn(s, w, g),
        lambda: st_result(s, result, s.res),
        lambda: st_mid_back(s, w, g, gain_ffn),
        lambda: st_attend_back(s),
        lambda: st_sort_back(s),
        lambda: st_sinkhorn_back(s),
        lambda: st_qkv_back(s, w, g, gain_attn),
        lambda: st_result(s, gtok, s.mid),
    ]
    for st in steps[:stop]:
        st()


def make_call(stop=99, interpret=False):
    names = list(SCRATCH)

    def kernel(tok, cot, ga, gf, w, seg, result, gtok, g, gg, *scr):
        s = Names()
        for n, r in zip(names, scr):
            setattr(s, n, r)
        compute_all(s, tok, cot, ga, gf, w, seg, result, gtok, g, stop)
        gg[...] = s.gg[...]
    vm = pl.BlockSpec(memory_space=pltpu.VMEM)
    return pl.pallas_call(
        kernel,
        out_shape=(jax.ShapeDtypeStruct((T, D), BF), jax.ShapeDtypeStruct((T, D), BF),
                   jax.ShapeDtypeStruct((2, D, COLS), BF), jax.ShapeDtypeStruct((8, D), F32)),
        in_specs=[vm] * 6, out_specs=(vm,) * 4,
        scratch_shapes=[pltpu.VMEM(*v) for v in SCRATCH.values()],
        compiler_params=pltpu.CompilerParams(vmem_limit_bytes=63 << 20),
        interpret=interpret,
    )


def gather_and_call(tokens, gain_attn, gain_ffn, w_query, w_key, w_value, w_out, w_in, w_down, segment_ids, cotangent):
    tp = lax.axis_index("tp")
    tok = lax.all_to_all(tokens, "tp", 0, 0, tiled=True).reshape(T, D)
    cot = lax.all_to_all(cotangent, "tp", 0, 0, tiled=True).reshape(T, D)
    own = jnp.concatenate([w_query, w_key, w_value, w_out.T, w_in, w_down.T], axis=1)
    half = lax.all_gather(own, "fsdp", axis=0, tiled=True)
    w = lax.all_gather(half, "tp", axis=0)
    seg = lax.dynamic_index_in_dim(segment_ids, tp, 0)
    res, gtok, g, gg = make_call()(tok, cot, gain_attn[None], gain_ffn[None], w, seg)
    res = lax.all_to_all(res.reshape(tokens.shape), "tp", 0, 0, tiled=True)
    gtok = lax.all_to_all(gtok.reshape(tokens.shape), "tp", 0, 0, tiled=True)
    gsum = lax.psum_scatter(g.astype(F32), "tp", scatter_dimension=0)
    gsum = lax.psum_scatter(gsum, "fsdp", scatter_dimension=0, tiled=True)
    gains = lax.psum_scatter(gg[:2], ("fsdp", "tp"), scatter_dimension=1, tiled=True)
    return (res, gtok, gains[0], gains[1], gsum[:, QO:KO], gsum[:, KO:VO], gsum[:, VO:OO],
            gsum[:, OO:IO].T, gsum[:, IO:DO], gsum[:, DO:].T)


def solution(mesh):
    return jax.shard_map(
        gather_and_call,
        mesh=mesh,
        in_specs=(P(None, ("fsdp", "tp"), None), P(), P(), P("fsdp", "tp"), P("fsdp", "tp"), P("fsdp", "tp"),
                  P("tp", "fsdp"), P("fsdp", "tp"), P("tp", "fsdp"), P(None, "fsdp"), P(None, ("fsdp", "tp"), None)),
        out_specs=(P(None, ("fsdp", "tp"), None), P(None, ("fsdp", "tp"), None), P(("fsdp", "tp")), P(("fsdp", "tp")),
                   P("fsdp", "tp"), P("fsdp", "tp"), P("fsdp", "tp"), P("tp", "fsdp"), P("fsdp", "tp"), P("tp", "fsdp")),
        check_vma=False,
    )
```

```python
import functools, math
import jax, jax.numpy as jnp
from jax import lax
from jax.experimental import pallas as pl
from jax.experimental.pallas import tpu as pltpu
from jax.sharding import PartitionSpec as P

F32, BF = jnp.float32, jnp.bfloat16
HI = lax.Precision.HIGHEST
HD, BLK, ITERS, NB, D, FF, T = 64, 32, 8, 32, 512, 2048, 1024
HALF = D // 2
COLS = 3 * HALF + HALF + FF
QO, KO, VO, OO, FO = 0, 256, 512, 768, 1024
UNITS = 512


def in_cols(u):
    return slice(FO + 2 * u * UNITS, FO + (2 * u + 1) * UNITS)


def down_cols(u):
    return slice(FO + (2 * u + 1) * UNITS, FO + (2 * u + 2) * UNITS)


def nn(a, b, precision=None):
    return lax.dot_general(a, b, (((1,), (0,)), ((), ())), precision=precision, preferred_element_type=F32)


def nt(a, b, precision=None):
    return lax.dot_general(a, b, (((1,), (1,)), ((), ())), precision=precision, preferred_element_type=F32)


def tn(a, b, precision=None):
    return lax.dot_general(a, b, (((0,), (0,)), ((), ())), precision=precision, preferred_element_type=F32)


def iota(shape, dim):
    return lax.broadcasted_iota(jnp.int32, shape, dim)


def order_matrix(inverse):
    n, m = iota((128, 128), 0), iota((128, 128), 1)
    if inverse:
        n, m = m, n
    return (m == (n & 3) * 32 + (n >> 2)).astype(BF)


def norm_rows(x, gain):
    center = x - jnp.mean(x, axis=1, keepdims=True)
    inv = lax.rsqrt(jnp.mean(center * center, axis=1, keepdims=True) + 1e-05)
    xhat = center * inv
    return xhat, inv


def norm_back(xhat, inv, gain, grad):
    gx = grad * gain
    m1 = jnp.mean(gx, axis=1, keepdims=True)
    m2 = jnp.mean(gx * xhat, axis=1, keepdims=True)
    return inv * (gx - m1 - xhat * m2)


def even_lanes(shape):
    return (iota(shape, len(shape) - 1) & 127) < 64


def stack_heads(x):
    ev = even_lanes(x.shape)
    z = jnp.zeros_like(x)
    return jnp.concatenate([jnp.where(ev, x, z), jnp.where(ev, z, x)], axis=0)


def pick_heads(r):
    n = r.shape[0] // 2
    ev = even_lanes((n, r.shape[1]))
    return jnp.where(ev, r[:n], r[n:])


SCRATCH = dict(
    tokp=((T, D), BF), cotp=((T, D), BF), cott=((D, T), BF), nm=((T, D), BF), nmt=((D, T), BF),
    q=((T, D), BF), k=((T, D), BF), v=((T, D), BF), ks=((T, D), BF), vs=((T, D), BF),
    qm=((NB, D), F32), km=((NB, D), F32), sk=((2 * ITERS, 8 * NB, NB), F32), allow=((NB, NB), F32),
    kr=((8, 128, 128), BF), krt=((8, 128, 128), BF), bias=((128, 256), F32),
    pr=((4, 8, 256, 256), BF), mix=((T, D), BF), mid=((T, D), F32), nf=((T, D), BF), nft=((D, T), BF),
    hid=((T, UNITS), BF), gp=((T, UNITS), BF), res=((T, D), F32), gnf=((T, D), F32),
    ga=((T, D), BF), gat=((D, T), BF), gmix=((T, D), BF), dv=((T, D), F32), ds=((8 * NB, NB), F32),
    gg=((8, D), F32),
)
SHARED = dict(dq="res", dk="gnf", dks="hid", dvs="gp", dqb="ga", dkb="nm", dvb="nf")


def loop(n, body, unroll=1):
    lax.fori_loop(0, n, lambda i, c: (body(i), c)[1], 0, unroll=unroll)


def rows(i, n):
    return pl.ds(pl.multiple_of(i * n, n), n)


def st_tokens(s, tok, gain_attn):
    pm = order_matrix(False)

    def body(c):
        x = nn(pm, tok[rows(c, 128), :])
        s.tokp[rows(c, 128), :] = x.astype(BF)
        xhat, _ = norm_rows(x, None)
        s.nm[rows(c, 128), :] = (xhat * gain_attn[...]).astype(BF)
    loop(8, body)


def st_cot(s, cot):
    pm = order_matrix(False)

    def body(c):
        s.cotp[rows(c, 128), :] = nn(pm, cot[rows(c, 128), :]).astype(BF)
    loop(8, body)


def transpose_into(dst, src):
    for c in range(4):
        dst[:, c * 256:(c + 1) * 256] = jnp.transpose(src[c * 256:(c + 1) * 256, :], (1, 0))


def block_sums(x):
    y = jnp.sum(x.reshape(16, 8, x.shape[1]), axis=0)
    return y[0:4] + y[4:8]


def st_values(s, w):
    def body(m):
        x = s.nm[rows(m, 256), :]
        for t in range(2):
            s.v[rows(m, 256), t * 256:(t + 1) * 256] = nn(x, w[t, :, VO:VO + HALF]).astype(BF)
    loop(4, body)


def st_query_key(s, w):
    def body(m):
        x = s.nm[rows(m, 256), :]
        for t in range(2):
            out = nn(x, w[t, :, 0:512]).astype(BF)
            cs = slice(t * 256, (t + 1) * 256)
            qv, kv = out[:, 0:256], out[:, 256:512]
            s.q[rows(m, 256), cs] = qv
            s.k[rows(m, 256), cs] = kv
            for ref, val in ((s.qm, qv), (s.km, kv)):
                val = val.astype(F32)
                sums = jnp.concatenate([block_sums(val[:128]), block_sums(val[128:])], axis=0)
                ref[rows(m, 8), cs] = sums * (1.0 / BLK)
    loop(4, body)


def st_sinkhorn(s, seg):
    row = jnp.broadcast_to(seg[...], (NB, NB))
    ri, ci = iota((NB, NB), 0), iota((NB, NB), 1)
    col = jnp.sum(jnp.where(ri == ci, row, 0), axis=1, keepdims=True)
    allow = ((row == col) & (ci <= ri)) | ((row == 0) & (col > 0))
    s.allow[...] = allow.astype(F32)
    parts = []
    for p in range(4):
        cs = slice(p * 128, (p + 1) * 128)
        parts.append(nt(stack_heads(s.qm[:, cs]), s.km[:, cs], precision=HI))
    x = jnp.concatenate(parts, axis=0) * (BLK / math.sqrt(HD))
    mask = jnp.concatenate([allow.astype(F32)] * 8, axis=0) > 0
    x = jnp.where(mask, x, -1000000000.0)
    for it in range(ITERS):
        m = jnp.max(x, axis=1, keepdims=True)
        e = jnp.exp(x - m)
        z = jnp.sum(e, axis=1, keepdims=True)
        s.sk[2 * it] = e * (1.0 / z)
        x = x - (m + jnp.log(z))
        y = x.reshape(8, NB, NB)
        m = jnp.max(y, axis=1, keepdims=True)
        e = jnp.exp(y - m)
        z = jnp.sum(e, axis=1, keepdims=True)
        s.sk[2 * it + 1] = (e * (1.0 / z)).reshape(8 * NB, NB)
        x = (y - (m + jnp.log(z))).reshape(8 * NB, NB)
    sorter = s.sk[2 * ITERS - 1].astype(BF)
    n = iota((128, NB), 0)
    e_mat = (((n >> 4) * 4 + (n & 3)) == iota((128, NB), 1)).astype(BF)
    wide = nt(sorter, e_mat).astype(BF)
    a, b = iota((128, 128), 0), iota((128, 128), 1)
    same = ((a >> 2) & 3) == ((b >> 2) & 3)
    for h in range(8):
        kr = jnp.where(same, nn(e_mat, wide[h * NB:(h + 1) * NB]), 0.0)
        s.kr[h] = kr.astype(BF)
        s.krt[h] = jnp.transpose(kr, (1, 0)).astype(BF)


def gather_chunk(ref, rq, cs):
    return jnp.concatenate([ref[pl.ds(pl.multiple_of(i * 128 + rq * 16, 16), 16), cs] for i in range(8)], axis=0)


def split_pair(x):
    return stack_heads(x)


def st_sort(s):
    def body(rq):
        for p in range(4):
            cs = slice(p * 128, (p + 1) * 128)
            kv = jnp.concatenate([gather_chunk(s.k, rq, cs), gather_chunk(s.v, rq, cs)], axis=1)
            lhs = jnp.concatenate([s.kr[2 * p], s.kr[2 * p + 1]], axis=1)
            out = nn(lhs, split_pair(kv)).astype(BF)
            for i in range(8):
                at = pl.ds(pl.multiple_of(i * 128 + rq * 16, 16), 16)
                s.ks[at, cs] = out[i * 16:(i + 1) * 16, 0:128]
                s.vs[at, cs] = out[i * 16:(i + 1) * 16, 128:256]
    loop(8, body)


def st_bias(s):
    n, m = iota((128, 256), 0), iota((128, 256), 1)
    ok = ((n & 3) == (m & 3)) & ((m >= 128) | ((m >> 2) <= (n >> 2)))
    s.bias[...] = jnp.where(ok, 0.0, -1e30)


def st_attend(s):
    scale = 1.0 / math.sqrt(HD)

    def body(c):
        at = rows(c, 128)
        for p in range(4):
            cs = slice(p * 128, (p + 1) * 128)
            qs = stack_heads(s.q[at, cs])
            kk = jnp.concatenate([s.k[at, cs], s.ks[at, cs]], axis=0)
            vv = jnp.concatenate([s.v[at, cs], s.vs[at, cs]], axis=0)
            b = s.bias[...]
            x = nt(qs, kk) * scale + jnp.concatenate([b, b], axis=0)
            m = jnp.max(x, axis=1, keepdims=True)
            e = jnp.exp(x - m)
            z = jnp.sum(e, axis=1, keepdims=True)
            pb = (e * (1.0 / z)).astype(BF)
            s.pr[p, c] = pb
            s.mix[at, cs] = pick_heads(nn(pb, vv)).astype(BF)
    loop(8, body)


def st_out(s, w, gain_ffn):
    def body(m):
        at = rows(m, 256)
        mid = s.tokp[at, :].astype(F32)
        for t in range(2):
            mid = mid + nt(s.mix[at, t * 256:(t + 1) * 256], w[t, :, OO:OO + HALF])
        s.mid[at, :] = mid
        xhat, _ = norm_rows(mid, None)
        s.nf[at, :] = (xhat * gain_ffn[...]).astype(BF)
    loop(4, body)


def gelu_pair(x):
    k0, k1 = math.sqrt(2.0 / math.pi), 0.044715
    x2 = x * x
    th = jnp.tanh(x * (k0 + (k0 * k1) * x2))
    half = 0.5 + 0.5 * th
    val = x * half
    der = half + (0.5 * x) * (1.0 - th * th) * (k0 + (3 * k0 * k1) * x2)
    return val, der


def add_grads(g, other, t, own, cols, val):
    if own:
        val = val + other[:, :, :, cols].reshape(D, val.shape[1]).astype(F32)
    g[t, :, :, :, cols] = val.astype(BF).reshape(4, 4, D // 16, val.shape[1])


def st_ffn(s, w, t, u, first):
    ic, dc = in_cols(u), down_cols(u)

    def body(m):
        at = rows(m, 256)
        x = nn(s.nf[at, :], w[t, :, ic])
        gh = nn(s.cotp[at, :], w[t, :, dc])
        val, der = gelu_pair(x)
        hid = val.astype(BF)
        gp = (gh * der).astype(BF)
        s.hid[at, :] = hid
        s.gp[at, :] = gp
        add = nt(hid, w[t, :, dc])
        s.res[at, :] = (s.mid[at, :] if first else s.res[at, :]) + add
        add = nt(gp, w[t, :, ic])
        s.gnf[at, :] = add if first else s.gnf[at, :] + add
    loop(4, body)


def st_ffn_grads(s, g, other, t, u, own):
    add_grads(g, other, t, own, in_cols(u), nn(s.nft[...], s.gp[...]))
    add_grads(g, other, t, own, down_cols(u), nn(s.cott[...], s.hid[...]))


def st_mid_back(s, w, gain_ffn):
    def body(m, acc):
        at = rows(m, 256)
        xhat, inv = norm_rows(s.mid[at, :], None)
        gnf = s.gnf[at, :]
        acc = acc + jnp.sum((gnf * xhat).reshape(32, 8, D), axis=0)
        gm = s.cotp[at, :].astype(F32) + norm_back(xhat, inv, gain_ffn[...], gnf)
        s.mid[at, :] = gm
        ga = gm.astype(BF)
        s.ga[at, :] = ga
        for t in range(2):
            s.gmix[at, t * 256:(t + 1) * 256] = nn(ga, w[t, :, OO:OO + HALF]).astype(BF)
        return acc
    acc = lax.fori_loop(0, 4, body, jnp.zeros((8, D), F32))
    s.gg[1:2, :] = jnp.sum(acc, axis=0, keepdims=True)
    transpose_into(s.gat, s.ga)


def half_cols(t):
    return pl.ds(pl.multiple_of(t * HALF, HALF), HALF)


def st_out_grads(s, g, other, t, own):
    add_grads(g, other, t, own, slice(OO, OO + HALF), nn(s.gat[...], s.mix[:, half_cols(t)]))


def st_result(s, out, src):
    pm = order_matrix(True)

    def body(c):
        at = rows(c, 128)
        out[at, :] = nn(pm, src[at, :].astype(BF)).astype(BF)
    loop(8, body)


def st_attend_back(s, lo, hi):
    scale = 1.0 / math.sqrt(HD)

    def body(c):
        at = rows(c, 128)
        for p in range(4):
            cs = slice(p * 128, (p + 1) * 128)
            qs = stack_heads(s.q[at, cs])
            gs = stack_heads(s.gmix[at, cs])
            kk = jnp.concatenate([s.k[at, cs], s.ks[at, cs]], axis=0)
            vv = jnp.concatenate([s.v[at, cs], s.vs[at, cs]], axis=0)
            pb = s.pr[p, c]
            pf = pb.astype(F32)
            dp = nt(gs, vv)
            pd = pf * dp
            dl = jnp.sum(pd, axis=1, keepdims=True)
            ds = ((pd - pf * dl) * scale).astype(BF)
            s.dq[at, cs] = pick_heads(nn(ds, kk))
            dkk = tn(ds, qs)
            dvv = tn(pb, gs)
            s.dk[at, cs] = dkk[:128]
            s.dks[at, cs] = dkk[128:].astype(BF)
            s.dv[at, cs] = dvv[:128]
            s.dvs[at, cs] = dvv[128:].astype(BF)
    lax.fori_loop(lo, hi, lambda i, z: (body(i), z)[1], 0)


def st_sort_back(s):
    def body(rq, accs):
        new = []
        for p in range(4):
            cs = slice(p * 128, (p + 1) * 128)
            kv = jnp.concatenate([gather_chunk(s.k, rq, cs), gather_chunk(s.v, rq, cs)], axis=1)
            dkv = jnp.concatenate([gather_chunk(s.dks, rq, cs), gather_chunk(s.dvs, rq, cs)], axis=1)
            st = split_pair(dkv)
            new.append(accs[p] + nt(st, kv))
            lhs = jnp.concatenate([s.krt[2 * p], s.krt[2 * p + 1]], axis=1)
            out = nn(lhs, st)
            for i in range(8):
                at = pl.ds(pl.multiple_of(i * 128 + rq * 16, 16), 16)
                s.dk[at, cs] = s.dk[at, cs] + out[i * 16:(i + 1) * 16, 0:128]
                s.dv[at, cs] = s.dv[at, cs] + out[i * 16:(i + 1) * 16, 128:256]
        return tuple(new)
    accs = lax.fori_loop(0, 8, body, tuple(jnp.zeros((256, 128), F32) for _ in range(4)))
    a, b = iota((128, 128), 0), iota((128, 128), 1)
    same = ((a >> 2) & 3) == ((b >> 2) & 3)
    n = iota((128, NB), 0)
    e_mat = (((n >> 4) * 4 + (n & 3)) == iota((128, NB), 1)).astype(F32)
    for p in range(4):
        for e in range(2):
            x = jnp.where(same, accs[p][e * 128:(e + 1) * 128], 0.0)
            y = nn(x, e_mat, precision=HI)
            s.ds[(2 * p + e) * NB:(2 * p + e + 1) * NB, :] = tn(e_mat, y, precision=HI)


def st_sinkhorn_back(s):
    x = s.ds[...] * s.sk[2 * ITERS - 1]
    for it in reversed(range(ITERS)):
        y = x.reshape(8, NB, NB)
        pk = s.sk[2 * it + 1].reshape(8, NB, NB)
        x = (y - pk * jnp.sum(y, axis=1, keepdims=True)).reshape(8 * NB, NB)
        x = x - s.sk[2 * it] * jnp.sum(x, axis=1, keepdims=True)
    mask = jnp.concatenate([s.allow[...]] * 8, axis=0) > 0
    x = jnp.where(mask, x, 0.0) * (BLK / math.sqrt(HD) / BLK)
    for p in range(4):
        cs = slice(p * 128, (p + 1) * 128)
        x0, x1 = x[(2 * p) * NB:(2 * p + 1) * NB], x[(2 * p + 1) * NB:(2 * p + 2) * NB]
        ev = even_lanes((NB, 128))
        km, qm = s.km[:, cs], s.qm[:, cs]
        dqm = jnp.where(ev, nn(x0, km, precision=HI), nn(x1, km, precision=HI))
        dkm = jnp.where(ev, tn(x0, qm, precision=HI), tn(x1, qm, precision=HI))
        for c in range(8):
            for src, ref, dst in ((dqm, s.dq, s.dqb), (dkm, s.dk, s.dkb)):
                four = src[c * 4:(c + 1) * 4]
                eight = jnp.concatenate([four, four], axis=0)
                val = ref[c * 128:(c + 1) * 128, cs].reshape(16, 8, 128) + eight[None]
                dst[c * 128:(c + 1) * 128, cs] = val.reshape(128, 128).astype(BF)
    s.dvb[...] = s.dv[...].astype(BF)


def st_qkv_grads(s, g, other, t, own):
    for off, ref in ((QO, s.dqb), (KO, s.dkb), (VO, s.dvb)):
        add_grads(g, other, t, own, slice(off, off + HALF), nn(s.nmt[...], ref[:, half_cols(t)]))


def st_qkv_back(s, w, gain_attn):
    def body(m, acc):
        at = rows(m, 256)
        gn = jnp.zeros((256, D), F32)
        for t in range(2):
            cs = slice(t * 256, (t + 1) * 256)
            lhs = jnp.concatenate([s.dqb[at, cs], s.dkb[at, cs], s.dvb[at, cs]], axis=1)
            gn = gn + nt(lhs, w[t, :, 0:768])
        xhat, inv = norm_rows(s.tokp[at, :].astype(F32), None)
        acc = acc + jnp.sum((gn * xhat).reshape(32, 8, D), axis=0)
        s.mid[at, :] = s.mid[at, :] + norm_back(xhat, inv, gain_attn[...], gn)
        return acc
    acc = lax.fori_loop(0, 4, body, jnp.zeros((8, D), F32))
    s.gg[0:1, :] = jnp.sum(acc, axis=0, keepdims=True)


class Names:
    pass


def stage_names(refs):
    s = Names()
    for n, r in zip(SCRATCH, refs):
        setattr(s, n, r)
    for n, o in SHARED.items():
        setattr(s, n, getattr(s, o))
    return s


def layer_kernel(tok, cot, gain_attn, gain_ffn, w, seg, result, gtok, g, gg, *scr):
    s = stage_names(scr)
    st_tokens(s, tok, gain_attn)
    st_cot(s, cot)
    transpose_into(s.cott, s.cotp)
    transpose_into(s.nmt, s.nm)
    st_bias(s)
    st_query_key(s, w)
    st_sinkhorn(s, seg)
    st_values(s, w)
    st_sort(s)
    st_attend(s)
    st_out(s, w, gain_ffn)
    transpose_into(s.nft, s.nf)
    for t in range(2):
        for u in range(2):
            st_ffn(s, w, t, u, t + u == 0)
            st_ffn_grads(s, g, None, t, u, False)
    st_result(s, result, s.res)
    st_mid_back(s, w, gain_ffn)
    for t in range(2):
        st_out_grads(s, g, None, t, False)
    st_attend_back(s, 0, 8)
    st_sort_back(s)
    st_sinkhorn_back(s)
    for t in range(2):
        st_qkv_grads(s, g, None, t, False)
    st_qkv_back(s, w, gain_attn)
    st_result(s, gtok, s.mid)
    gg[...] = s.gg[...]


def layer_call():
    vm = pl.BlockSpec(memory_space=pltpu.VMEM)
    return pl.pallas_call(
        layer_kernel,
        out_shape=(jax.ShapeDtypeStruct((T, D), BF), jax.ShapeDtypeStruct((T, D), BF),
                   jax.ShapeDtypeStruct((2, 4, 4, D // 16, COLS), BF), jax.ShapeDtypeStruct((8, D), F32)),
        in_specs=[vm] * 6, out_specs=(vm,) * 4,
        scratch_shapes=[pltpu.VMEM(*v) for v in SCRATCH.values()],
        compiler_params=pltpu.CompilerParams(vmem_limit_bytes=60 << 20),
    )


def split_cols(x):
    ins = jnp.concatenate([x[:, in_cols(u)] for u in range(2)], axis=1)
    downs = jnp.concatenate([x[:, down_cols(u)] for u in range(2)], axis=1)
    return x[:, QO:KO], x[:, KO:VO], x[:, VO:OO], x[:, OO:FO], ins, downs


def join_cols(q, k, v, o, i, d):
    parts = [q, k, v, o]
    for u in range(2):
        parts += [i[:, u * UNITS:(u + 1) * UNITS], d[:, u * UNITS:(u + 1) * UNITS]]
    return jnp.concatenate(parts, axis=1)


def by_collectives(tokens, gain_attn, gain_ffn, w_query, w_key, w_value, w_out, w_in, w_down, segment_ids, cotangent):
    tp = lax.axis_index("tp")
    tok = lax.all_to_all(tokens, "tp", 0, 0, tiled=True).reshape(T, D)
    cot = lax.all_to_all(cotangent, "tp", 0, 0, tiled=True).reshape(T, D)
    own = join_cols(w_query, w_key, w_value, w_out.T, w_in, w_down.T)
    half = lax.all_gather(own, "fsdp", axis=0, tiled=True)
    w = lax.all_gather(half, "tp", axis=0)
    seg = lax.dynamic_index_in_dim(segment_ids, tp, 0)
    res, gtok, g, gg = layer_call()(tok, cot, gain_attn[None], gain_ffn[None], w, seg)
    res = lax.all_to_all(res.reshape(tokens.shape), "tp", 0, 0, tiled=True)
    gtok = lax.all_to_all(gtok.reshape(tokens.shape), "tp", 0, 0, tiled=True)
    gsum = lax.psum_scatter(g.reshape(2, D, COLS).astype(F32), "tp", scatter_dimension=0)
    gsum = lax.psum_scatter(gsum, "fsdp", scatter_dimension=0, tiled=True)
    gains = lax.psum_scatter(gg[:2], ("fsdp", "tp"), scatter_dimension=1, tiled=True)
    q, k, v, o, i, d = split_cols(gsum)
    return res, gtok, gains[0], gains[1], q, k, v, o.T, i, d.T


PIECES = ((0, 512), (512, 1024), (1024, 2048), (2048, 3072))
GPIECES = ((1024, 2048), (2048, 3072), (768, 1024), (0, 768))
MESH = pl.DeviceIdType.MESH
ROWS = D // 16

EXCHANGE = dict(
    w=((2, D, COLS), BF), g=((2, 4, 4, ROWS, COLS), BF), other=((4, 4, ROWS, COLS), BF),
    rx=((3, 4, ROWS, COLS), BF), zs=((4, ROWS, COLS), BF), rz=((3, ROWS, COLS), BF),
    tok=((T, D), BF), cot=((T, D), BF), gr=((7, 8, D), F32), gs=((3, 8, D), F32),
)


class Links:
    def __init__(self, e, sems):
        self.e = e
        self.sems = sems
        f, self.c = lax.axis_index("fsdp"), lax.axis_index("tp")
        self.zi, self.xy = f // 4, f % 4
        x, y = self.xy % 2, self.xy // 2
        self.f = f
        self.plane = [(1 - x) + 2 * y, x + 2 * (1 - y), (1 - x) + 2 * (1 - y)]
        self.sent = []
        self.copies = {}

    def z_at(self, dz):
        return (self.zi + dz) % 4

    def z_from(self, dz):
        return (self.zi + 4 - dz) % 4

    def everyone(self):
        return ([(self.z_at(d) * 4 + self.xy, self.c) for d in (1, 2, 3)]
                + [(self.zi * 4 + k, self.c) for k in self.plane] + [(self.f, 1 - self.c)])

    def meet(self):
        bar = pltpu.get_barrier_semaphore()
        for dev in self.everyone():
            pl.semaphore_signal(bar, inc=1, device_id=dev, device_id_type=MESH)
        pl.semaphore_wait(bar, 7)

    def send(self, key, src, dst, sem, dev):
        send_sem, recv_sem = self.sems
        copy = pltpu.make_async_remote_copy(src_ref=src, dst_ref=dst, send_sem=send_sem.at[sem], recv_sem=recv_sem.at[sem],
                                            device_id=dev, device_id_type=MESH)
        copy.start()
        self.sent.append(copy)
        self.copies[key] = copy

    def arrived(self, key):
        self.copies[key].wait_recv()

    def finish(self):
        for copy in self.sent:
            copy.wait_send()

    def own_rows(self, piece):
        cols = slice(*PIECES[piece])
        w = self.e.w
        at = w.at[self.c, pl.ds(pl.multiple_of(self.f * ROWS, ROWS), ROWS), cols]
        for d in (1, 2, 3):
            self.send(("z", piece, d), at, at, 19 * piece + d - 1, (self.z_at(d) * 4 + self.xy, self.c))
        for n, k in enumerate(self.plane):
            self.send(("p", piece, 0, n), at, at, 19 * piece + 3 + n, (self.zi * 4 + k, self.c))

    def pass_plane(self, piece):
        cols = slice(*PIECES[piece])
        for d in (1, 2, 3):
            self.arrived(("z", piece, d))
            row = (self.z_from(d) * 4 + self.xy) * ROWS
            at = self.e.w.at[self.c, pl.ds(pl.multiple_of(row, ROWS), ROWS), cols]
            for n, k in enumerate(self.plane):
                self.send(("p", piece, d, n), at, at, 19 * piece + 3 + 3 * d + n, (self.zi * 4 + k, self.c))

    def pass_pair(self, piece):
        cols = slice(*PIECES[piece])
        for d in range(4):
            for n in range(3):
                self.arrived(("p", piece, d, n))
            row = self.z_from(d) * 4 * ROWS
            at = self.e.w.at[self.c, pl.ds(pl.multiple_of(row, 4 * ROWS), 4 * ROWS), cols]
            self.send(("t", piece, d), at, at, 19 * piece + 15 + d, (self.f, 1 - self.c))

    def gathered(self, piece):
        for d in range(4):
            self.arrived(("t", piece, d))

    def grads_pair(self, piece):
        cols = slice(*GPIECES[piece])
        self.send(("gt", piece), self.e.g.at[1 - self.c, :, :, :, cols], self.e.other.at[:, :, :, cols], 76 + 7 * piece,
                  (self.f, 1 - self.c))

    def grads_pair_in(self, piece):
        self.arrived(("gt", piece))

    def grads_plane(self, piece):
        cols = slice(*GPIECES[piece])
        for n, k in enumerate(self.plane):
            self.send(("gp", piece, n), self.e.g.at[self.c, :, k, :, cols], self.e.rx.at[n, :, :, cols], 77 + 7 * piece + n,
                      (self.zi * 4 + k, self.c))

    def grads_line(self, piece, out):
        e = self.e
        cols = slice(*GPIECES[piece])
        for n in range(3):
            self.arrived(("gp", piece, n))
        for d in (1, 2, 3):
            z = self.z_at(d)
            total = e.g[self.c, z, self.xy, :, cols].astype(F32)
            for n in range(3):
                total = total + e.rx[n, z, :, cols].astype(F32)
            e.zs[d, :, cols] = total.astype(BF)
            self.send(("gz", piece, d), e.zs.at[d, :, cols], e.rz.at[d - 1, :, cols], 79 + 7 * piece + d, (z * 4 + self.xy, self.c))
        total = e.g[self.c, self.zi, self.xy, :, cols].astype(F32)
        for n in range(3):
            total = total + e.rx[n, self.zi, :, cols].astype(F32)
        out[:, cols] = total

    def grads_in(self, piece, out):
        cols = slice(*GPIECES[piece])
        for d in (1, 2, 3):
            self.arrived(("gz", piece, d))
        total = out[:, cols]
        for d in range(3):
            total = total + self.e.rz[d, :, cols].astype(F32)
        out[:, cols] = total

    def gains_sum(self, step):
        e = self.e
        if step == 0:
            self.send(("n", 0), e.gs.at[0], e.gr.at[0], 104, (self.f, 1 - self.c))
        if step == 1:
            self.arrived(("n", 0))
            e.gs[1] = e.gs[0] + e.gr[0]
            for n, k in enumerate(self.plane):
                self.send(("n", 1 + n), e.gs.at[1], e.gr.at[1 + n], 105 + n, (self.zi * 4 + k, self.c))
        if step == 2:
            for n in range(3):
                self.arrived(("n", 1 + n))
            e.gs[2] = e.gs[1] + e.gr[1] + e.gr[2] + e.gr[3]
            for d in (1, 2, 3):
                self.send(("n", 3 + d), e.gs.at[2], e.gr.at[3 + d], 107 + d, (self.z_at(d) * 4 + self.xy, self.c))
        if step == 3:
            for d in (1, 2, 3):
                self.arrived(("n", 3 + d))
            return e.gs[2] + e.gr[4] + e.gr[5] + e.gr[6]


NSEM = 116


def step_kernel(tokens, cotangent, gain_attn, gain_ffn, wq, wk, wv, wo, wi, wd, seg, result, gtok, gains, gout, *scr):
    ns, ne = len(SCRATCH), len(EXCHANGE)
    s = stage_names(scr[:ns])
    e = Names()
    for n, r in zip(EXCHANGE, scr[ns:ns + ne]):
        setattr(e, n, r)
    send_sem, recv_sem, local = scr[ns + ne:]
    link = Links(e, (send_sem, recv_sem))
    c, f, w, g = link.c, link.f, e.w, e.g
    half = T // 2
    mine = pl.ds(pl.multiple_of(c * half, half), half)
    theirs = pl.ds(pl.multiple_of((1 - c) * half, half), half)
    pair = (f, 1 - c)

    loads = [pltpu.make_async_copy(tokens.at[c], e.tok.at[mine, :], local.at[0]),
             pltpu.make_async_copy(cotangent.at[c], e.cot.at[mine, :], local.at[1])]
    for cp in loads:
        cp.start()
    own = join_cols(wq[...], wk[...], wv[...], jnp.transpose(wo[...], (1, 0)), wi[...], jnp.transpose(wd[...], (1, 0)))
    w[c, pl.ds(pl.multiple_of(f * ROWS, ROWS), ROWS), :] = own
    link.meet()
    link.own_rows(0)
    link.send("tok", tokens.at[1 - c], e.tok.at[mine, :], 111, pair)
    link.send("cot", cotangent.at[1 - c], e.cot.at[mine, :], 112, pair)
    loads[0].wait()
    link.arrived("tok")
    st_tokens(s, e.tok, gain_attn)
    link.pass_plane(0)
    link.own_rows(1)
    loads[1].wait()
    link.arrived("cot")
    st_cot(s, e.cot)
    transpose_into(s.cott, s.cotp)
    transpose_into(s.nmt, s.nm)
    st_bias(s)
    link.pass_pair(0)
    link.pass_plane(1)
    link.own_rows(2)
    link.gathered(0)
    st_query_key(s, w)
    link.pass_pair(1)
    link.pass_plane(2)
    link.own_rows(3)
    st_sinkhorn(s, seg.at[pl.ds(c, 1), :])
    link.gathered(1)
    st_values(s, w)
    st_sort(s)
    link.pass_pair(2)
    link.pass_plane(3)
    st_attend(s)
    st_out(s, w, gain_ffn)
    transpose_into(s.nft, s.nf)
    link.pass_pair(3)
    link.gathered(2)
    for u in range(2):
        if u == 1:
            link.gathered(3)
        st_ffn(s, w, 1 - c, u, u == 0)
        st_ffn_grads(s, g, None, 1 - c, u, False)
        link.grads_pair(u)
        st_ffn(s, w, c, u, False)
        link.grads_pair_in(u)
        st_ffn_grads(s, g, e.other, c, u, True)
        link.grads_plane(u)
    st_result(s, e.tok, s.res)
    stores = [pltpu.make_async_copy(e.tok.at[mine, :], result.at[c], local.at[2])]
    stores[0].start()
    link.send("res", e.tok.at[theirs, :], result.at[c], 113, pair)
    st_mid_back(s, w, gain_ffn)
    st_out_grads(s, g, None, 1 - c, False)
    link.grads_pair(2)
    link.grads_line(0, gout)
    link.grads_pair_in(2)
    st_out_grads(s, g, e.other, c, True)
    link.grads_plane(2)
    st_attend_back(s, 0, 4)
    link.grads_in(0, gout)
    link.grads_line(1, gout)
    st_attend_back(s, 4, 8)
    link.grads_in(1, gout)
    link.grads_line(2, gout)
    st_sort_back(s)
    st_sinkhorn_back(s)
    st_qkv_grads(s, g, None, 1 - c, False)
    link.grads_pair(3)
    link.grads_in(2, gout)
    st_qkv_back(s, w, gain_attn)
    e.gs[0] = s.gg[...]
    link.gains_sum(0)
    link.grads_pair_in(3)
    st_qkv_grads(s, g, e.other, c, True)
    link.grads_plane(3)
    link.gains_sum(1)
    st_result(s, e.cot, s.mid)
    stores.append(pltpu.make_async_copy(e.cot.at[mine, :], gtok.at[c], local.at[3]))
    stores[1].start()
    link.send("gtok", e.cot.at[theirs, :], gtok.at[c], 114, pair)
    link.gains_sum(2)
    link.grads_line(3, gout)
    total = link.gains_sum(3)
    width = gains.shape[1]
    pick = (iota((D, width), 0) == iota((D, width), 1) + (2 * f + c) * width).astype(F32)
    gains[...] = nn(total, pick, precision=HI)
    link.grads_in(3, gout)
    link.arrived("res")
    link.arrived("gtok")
    for cp in stores:
        cp.wait()
    link.finish()


def by_kernel(tokens, gain_attn, gain_ffn, w_query, w_key, w_value, w_out, w_in, w_down, segment_ids, cotangent):
    vm, hbm = pl.BlockSpec(memory_space=pltpu.VMEM), pl.BlockSpec(memory_space=pl.ANY)
    width = D // 32
    shapes = list(SCRATCH.values()) + list(EXCHANGE.values())
    res, gtok, gains, gout = pl.pallas_call(
        step_kernel,
        out_shape=(jax.ShapeDtypeStruct(tokens.shape, BF), jax.ShapeDtypeStruct(tokens.shape, BF),
                   jax.ShapeDtypeStruct((8, width), F32), jax.ShapeDtypeStruct((ROWS, COLS), F32)),
        in_specs=[hbm] * 2 + [vm] * 9, out_specs=(hbm, hbm, vm, vm),
        scratch_shapes=[pltpu.VMEM(*v) for v in shapes] + [
            pltpu.SemaphoreType.DMA((NSEM,)), pltpu.SemaphoreType.DMA((NSEM,)), pltpu.SemaphoreType.DMA((4,))],
        compiler_params=pltpu.CompilerParams(collective_id=0, has_side_effects=True, vmem_limit_bytes=63 << 20),
    )(tokens, cotangent, gain_attn[None], gain_ffn[None], w_query, w_key, w_value, w_out, w_in, w_down, segment_ids)
    q, k, v, o, i, d = split_cols(gout)
    return res, gtok, gains[0], gains[1], q, k, v, o.T, i, d.T


def solution(mesh):
    body = by_kernel if mesh.shape["fsdp"] == 16 else by_collectives
    return jax.shard_map(
        body,
        mesh=mesh,
        in_specs=(P(None, ("fsdp", "tp"), None), P(), P(), P("fsdp", "tp"), P("fsdp", "tp"), P("fsdp", "tp"),
                  P("tp", "fsdp"), P("fsdp", "tp"), P("tp", "fsdp"), P(None, "fsdp"), P(None, ("fsdp", "tp"), None)),
        out_specs=(P(None, ("fsdp", "tp"), None), P(None, ("fsdp", "tp"), None), P(("fsdp", "tp")), P(("fsdp", "tp")),
                   P("fsdp", "tp"), P("fsdp", "tp"), P("fsdp", "tp"), P("tp", "fsdp"), P("fsdp", "tp"), P("tp", "fsdp")),
        check_vma=False,
    )
```

```python
import collections
import functools
import math
import jax, jax.numpy as jnp
from jax import lax
from jax.experimental import pallas as pl
from jax.experimental.pallas import tpu as pltpu
from jax.sharding import PartitionSpec as P

F32, BF = jnp.float32, jnp.bfloat16
HI = lax.Precision.HIGHEST
HD, BLK, ITERS, NB, D, FF, T = 64, 32, 8, 32, 512, 2048, 1024
HALF = D // 2
COLS = 3 * HALF + HALF + FF
QO, KO, VO, OO, FO = 0, 256, 512, 768, 1024
UNITS = 512


def in_cols(u):
    return slice(FO + 2 * u * UNITS, FO + (2 * u + 1) * UNITS)


def down_cols(u):
    return slice(FO + (2 * u + 1) * UNITS, FO + (2 * u + 2) * UNITS)


def nn(a, b, precision=None):
    return lax.dot_general(a, b, (((1,), (0,)), ((), ())), precision=precision, preferred_element_type=F32)


def nt(a, b, precision=None):
    return lax.dot_general(a, b, (((1,), (1,)), ((), ())), precision=precision, preferred_element_type=F32)


def tn(a, b, precision=None):
    return lax.dot_general(a, b, (((0,), (0,)), ((), ())), precision=precision, preferred_element_type=F32)


def iota(shape, dim):
    return lax.broadcasted_iota(jnp.int32, shape, dim)


def order_matrix(inverse):
    n, m = iota((128, 128), 0), iota((128, 128), 1)
    if inverse:
        n, m = m, n
    return (m == (n & 3) * 32 + (n >> 2)).astype(BF)


def norm_rows(x, gain):
    center = x - jnp.mean(x, axis=1, keepdims=True)
    inv = lax.rsqrt(jnp.mean(center * center, axis=1, keepdims=True) + 1e-05)
    xhat = center * inv
    return xhat, inv


def norm_back(xhat, inv, gain, grad):
    gx = grad * gain
    m1 = jnp.mean(gx, axis=1, keepdims=True)
    m2 = jnp.mean(gx * xhat, axis=1, keepdims=True)
    return inv * (gx - m1 - xhat * m2)


def even_lanes(shape):
    return (iota(shape, len(shape) - 1) & 127) < 64


def stack_heads(x):
    ev = even_lanes(x.shape)
    z = jnp.zeros_like(x)
    return jnp.concatenate([jnp.where(ev, x, z), jnp.where(ev, z, x)], axis=0)


def pick_heads(r):
    n = r.shape[0] // 2
    ev = even_lanes((n, r.shape[1]))
    return jnp.where(ev, r[:n], r[n:])


SCRATCH = dict(
    tokp=((T, D), BF), cotp=((T, D), BF), cott=((D, T), BF), nm=((T, D), BF), nmt=((D, T), BF),
    q=((T, D), BF), k=((T, D), BF), v=((T, D), BF), ks=((T, D), BF), vs=((T, D), BF),
    qm=((NB, D), F32), km=((NB, D), F32), sk=((2 * ITERS, 8 * NB, NB), F32), allow=((NB, NB), F32),
    kr=((8, 128, 128), BF), krt=((8, 128, 128), BF), hidq=((256, 128), BF), hidk=((256, 128), BF),
    pr=((4, 8, 256, 256), BF), mix=((T, D), BF), mid=((T, D), F32), nf=((T, D), BF), nft=((D, T), BF),
    hid=((T, UNITS), BF), gp=((T, UNITS), BF), res=((T, D), F32), gnf=((T, D), F32),
    ga=((T, D), BF), gat=((D, T), BF), gmix=((T, D), BF), dv=((T, D), F32), ds=((8 * NB, NB), F32),
    gg=((8, D), F32), gn=((T, D), F32),
)
SHARED = dict(dq="res", dk="gnf", dks="hid", dvs="gp", dqb="ga", dkb="nm", dvb="nf")


def loop(n, body, unroll=1):
    lax.fori_loop(0, n, lambda i, c: (body(i), c)[1], 0, unroll=unroll)


def rows(i, n):
    return pl.ds(pl.multiple_of(i * n, n), n)


def pipeline(units, stages, lags, after=None):
    vals = [{} for _ in units]
    for step in range(len(units) + lags[-1]):
        for st, lag in reversed(list(zip(stages, lags))):
            if 0 <= step - lag < len(units):
                st(units[step - lag], vals[step - lag])
        if after is not None:
            after(step)


def st_tokens(s, tok, gain_attn):
    pm = order_matrix(False)

    def body(c):
        def order(i, v):
            v["x"] = nn(pm, tok[rows(4 * c + i, 128), :])

        def norm(i, v):
            at = rows(4 * c + i, 128)
            x = v.pop("x")
            s.tokp[at, :] = x.astype(BF)
            xhat, _ = norm_rows(x, None)
            s.nm[at, :] = (xhat * gain_attn[...]).astype(BF)
        pipeline(range(4), (order, norm), (0, 1))
    loop(2, body)


def st_cot(s, cot):
    pm = order_matrix(False)

    def body(c):
        for i in range(4):
            at = rows(4 * c + i, 128)
            s.cotp[at, :] = nn(pm, cot[at, :]).astype(BF)
    loop(2, body)


def transpose_into(dst, src):
    for c in range(4):
        dst[:, c * 256:(c + 1) * 256] = jnp.transpose(src[c * 256:(c + 1) * 256, :], (1, 0))


def block_sums(x):
    y = jnp.sum(x.reshape(16, 8, x.shape[1]), axis=0)
    return y[0:4] + y[4:8]


def st_values(s, w):
    for m in range(4):
        x = s.nm[rows(m, 256), :]
        for t in range(2):
            s.v[rows(m, 256), t * 256:(t + 1) * 256] = nn(x, w[t, :, VO:VO + HALF]).astype(BF)


def st_query_key(s, w, after=None):
    def product(m, v):
        x = s.nm[rows(m, 256), :]
        v["x"] = [nn(x, w[t, :, 0:512]).astype(BF) for t in range(2)]

    def store(m, v):
        at = rows(m, 256)
        for t, out in enumerate(v.pop("x")):
            cs = slice(t * 256, (t + 1) * 256)
            qv, kv = out[:, 0:256].astype(F32), out[:, 256:512].astype(F32)
            s.q[at, cs] = (qv * (1.0 / math.sqrt(HD))).astype(BF)
            s.k[at, cs] = out[:, 256:512]
            for ref, val in ((s.qm, qv), (s.km, kv)):
                sums = jnp.concatenate([block_sums(val[:128]), block_sums(val[128:])], axis=0)
                ref[rows(m, 8), cs] = sums * (1.0 / BLK)
    pipeline(range(4), (product, store), (0, 1), after)


def st_sinkhorn(s, seg, after=None):
    row = jnp.broadcast_to(seg[...], (NB, NB))
    ri, ci = iota((NB, NB), 0), iota((NB, NB), 1)
    col = jnp.sum(jnp.where(ri == ci, row, 0), axis=1, keepdims=True)
    allow = ((row == col) & (ci <= ri)) | ((row == 0) & (col > 0))
    s.allow[...] = allow.astype(F32)
    parts = []
    for p in range(4):
        cs = slice(p * 128, (p + 1) * 128)
        parts.append(nt(stack_heads(s.qm[:, cs]), s.km[:, cs], precision=HI))
    x = jnp.concatenate(parts, axis=0) * (BLK / math.sqrt(HD))
    mask = jnp.concatenate([allow.astype(F32)] * 8, axis=0) > 0
    x = jnp.where(mask, x, -1000000000.0)
    for it in range(ITERS):
        m = jnp.max(x, axis=1, keepdims=True)
        e = jnp.exp(x - m)
        z = jnp.sum(e, axis=1, keepdims=True)
        s.sk[2 * it] = e * (1.0 / z)
        x = x - (m + jnp.log(z))
        y = x.reshape(8, NB, NB)
        m = jnp.max(y, axis=1, keepdims=True)
        e = jnp.exp(y - m)
        z = jnp.sum(e, axis=1, keepdims=True)
        s.sk[2 * it + 1] = (e * (1.0 / z)).reshape(8 * NB, NB)
        x = (y - (m + jnp.log(z))).reshape(8 * NB, NB)
        if after is not None:
            after(it)
    sorter = s.sk[2 * ITERS - 1].astype(BF)
    n = iota((128, NB), 0)
    e_mat = (((n >> 4) * 4 + (n & 3)) == iota((128, NB), 1)).astype(BF)
    wide = nt(sorter, e_mat).astype(BF)
    a, b = iota((128, 128), 0), iota((128, 128), 1)
    same = ((a >> 2) & 3) == ((b >> 2) & 3)
    for h in range(8):
        kr = jnp.where(same, nn(e_mat, wide[h * NB:(h + 1) * NB]), 0.0)
        s.kr[h] = kr.astype(BF)
        s.krt[h] = jnp.transpose(kr, (1, 0)).astype(BF)


def gather_chunk(ref, rq, cs):
    return jnp.concatenate([ref[pl.ds(pl.multiple_of(i * 128 + rq * 16, 16), 16), cs] for i in range(8)], axis=0)


def split_pair(x):
    return stack_heads(x)


def st_sort(s):
    def body(r):
        def mix(unit, v):
            rq, p = 2 * r + unit // 4, unit % 4
            cs = slice(p * 128, (p + 1) * 128)
            kv = jnp.concatenate([gather_chunk(s.k, rq, cs), gather_chunk(s.v, rq, cs)], axis=1)
            lhs = jnp.concatenate([s.kr[2 * p], s.kr[2 * p + 1]], axis=1)
            v["out"] = nn(lhs, split_pair(kv))

        def store(unit, v):
            rq, p = 2 * r + unit // 4, unit % 4
            cs = slice(p * 128, (p + 1) * 128)
            out = v.pop("out").astype(BF)
            for i in range(8):
                at = pl.ds(pl.multiple_of(i * 128 + rq * 16, 16), 16)
                s.ks[at, cs] = out[i * 16:(i + 1) * 16, 0:128]
                s.vs[at, cs] = out[i * 16:(i + 1) * 16, 128:256]
        pipeline(range(8), (mix, store), (0, 2))
    loop(4, body)


def st_bias(s):
    n, a = iota((256, 128), 0), iota((256, 128), 1)
    s.hidq[...] = ((a == (n & 3)) | (a == 4 + ((n & 127) >> 2))).astype(BF)
    other = (a < 4) & (a != (n & 3))
    later = (n < 128) & (a >= 4) & (a < 36) & ((n >> 2) > a - 4)
    s.hidk[...] = jnp.where(other | later, -1e30, 0.0).astype(BF)


def pick_rows(r):
    n = r.shape[1] // 2
    return jnp.concatenate([r[:64, :n], r[64:, n:]], axis=0)


def chunk_pair(c, i):
    p = i % 4
    c = c + i // 4
    return c, p, rows(c, 128), slice(p * 128, (p + 1) * 128)


def st_attend(s, b, after=None):
    def score(i, v):
        c, p, at, cs = chunk_pair(4 * b, i)
        qs = jnp.concatenate([stack_heads(s.q[at, cs]), s.hidq[...]], axis=1)
        kk = jnp.concatenate([jnp.concatenate([s.k[at, cs], s.ks[at, cs]], axis=0), s.hidk[...]], axis=1)
        v["x"] = nt(kk, qs)

    def soften(i, v):
        c, p, at, cs = chunk_pair(4 * b, i)
        x = v.pop("x")
        e = jnp.exp(x - jnp.max(x, axis=0, keepdims=True))
        v["p"] = (e * (1.0 / jnp.sum(e, axis=0, keepdims=True))).astype(BF)
        s.pr[p, c] = v["p"]

    def blend(i, v):
        c, p, at, cs = chunk_pair(4 * b, i)
        vv = jnp.concatenate([s.v[at, cs], s.vs[at, cs]], axis=0)
        v["o"] = pick_rows(nn(jnp.transpose(vv, (1, 0)), v.pop("p")))

    def store(i, v):
        c, p, at, cs = chunk_pair(4 * b, i)
        s.mix[at, cs] = jnp.transpose(v.pop("o"), (1, 0)).astype(BF)
    pipeline(range(16), (score, soften, blend, store), (0, 2, 4, 6), after)


def st_out(s, w, gain_ffn):
    def product(m, v):
        at = rows(m, 256)
        v["x"] = sum(nt(s.mix[at, t * 256:(t + 1) * 256], w[t, :, OO:OO + HALF]) for t in range(2))

    def norm(m, v):
        at = rows(m, 256)
        mid = s.tokp[at, :].astype(F32) + v.pop("x")
        s.mid[at, :] = mid
        xhat, _ = norm_rows(mid, None)
        s.nf[at, :] = (xhat * gain_ffn[...]).astype(BF)
    pipeline(range(4), (product, norm), (0, 1))


def gelu_pair(x):
    k0, k1 = math.sqrt(2.0 / math.pi), 0.044715
    x2 = x * x
    half = 0.5 + 0.5 * jnp.tanh(x * (k0 + (k0 * k1) * x2))
    val = x * half
    der = half + (val - val * half) * (2 * k0 + (6 * k0 * k1) * x2)
    return val, der


def add_grads(g, other, t, own, cols, val):
    if own:
        val = val + other[:, :, :, cols].reshape(D, val.shape[1]).astype(F32)
    g[t, :, :, :, cols] = val.astype(BF).reshape(4, 4, D // 16, val.shape[1])


def st_ffn(s, w, t, u, first, after=None):
    ic, dc = in_cols(u), down_cols(u)

    def into(m, v):
        at = rows(m, 256)
        v["x"] = nn(s.nf[at, :], w[t, :, ic])
        v["g"] = nn(s.cotp[at, :], w[t, :, dc])

    def bend(m, v):
        at = rows(m, 256)
        val, der = gelu_pair(v.pop("x"))
        v["h"] = val.astype(BF)
        v["g"] = (v["g"] * der).astype(BF)
        s.hid[at, :] = v["h"]
        s.gp[at, :] = v["g"]

    def back(m, v):
        at = rows(m, 256)
        add = nt(v.pop("h"), w[t, :, dc])
        s.res[at, :] = (s.mid[at, :] if first else s.res[at, :]) + add
        add = nt(v.pop("g"), w[t, :, ic])
        s.gnf[at, :] = add if first else s.gnf[at, :] + add
    pipeline(range(4), (into, bend, back), (0, 2, 3), after)


def st_ffn_grads(s, g, other, t, u, own):
    add_grads(g, other, t, own, in_cols(u), nn(s.nft[...], s.gp[...]))
    add_grads(g, other, t, own, down_cols(u), nn(s.cott[...], s.hid[...]))


def st_mid_back(s, w, gain_ffn):
    parts = []

    def norm(m, v):
        at = rows(m, 256)
        xhat, inv = norm_rows(s.mid[at, :], None)
        gnf = s.gnf[at, :]
        parts.append(jnp.sum((gnf * xhat).reshape(32, 8, D), axis=0))
        gm = s.cotp[at, :].astype(F32) + norm_back(xhat, inv, gain_ffn[...], gnf)
        s.mid[at, :] = gm
        v["ga"] = gm.astype(BF)
        s.ga[at, :] = v["ga"]

    def product(m, v):
        at = rows(m, 256)
        ga = v.pop("ga")
        for t in range(2):
            s.gmix[at, t * 256:(t + 1) * 256] = nn(ga, w[t, :, OO:OO + HALF]).astype(BF)
        s.gat[:, m * 256:(m + 1) * 256] = jnp.transpose(ga, (1, 0))
    pipeline(range(4), (norm, product), (0, 1))
    s.gg[1:2, :] = jnp.sum(sum(parts), axis=0, keepdims=True)


def half_cols(t):
    return pl.ds(pl.multiple_of(t * HALF, HALF), HALF)


def st_out_grads(s, g, other, t, own):
    add_grads(g, other, t, own, slice(OO, OO + HALF), nn(s.gat[...], s.mix[:, half_cols(t)]))


def st_result(s, out, src):
    pm = order_matrix(True)

    def body(c):
        at = rows(c, 128)
        out[at, :] = nn(pm, src[at, :].astype(BF)).astype(BF)
    loop(8, body)


def pair_cols(t, j):
    return pl.ds(pl.multiple_of(t * HALF + j * 128, 128), 128)


def st_attend_back(s, t, after=None):
    scale = 1.0 / math.sqrt(HD)

    def place(i):
        c, j = i // 2, i % 2
        return c, 2 * t + j, slice(c * 128, (c + 1) * 128), pair_cols(t, j)

    def grad_probs(i, v):
        c, p, at, cs = place(i)
        g = s.gmix[at, cs]
        go = (g.astype(F32) * s.mix[at, cs].astype(F32)).astype(BF)
        vv = jnp.concatenate([s.v[at, cs], s.vs[at, cs]], axis=0)
        v["dp"] = nt(jnp.concatenate([vv, jnp.full_like(vv, -1.0)], axis=1),
                     jnp.concatenate([stack_heads(g), stack_heads(go)], axis=1))

    def grad_scores(i, v):
        c, p, at, cs = place(i)
        v["ds"] = (s.pr[p, c].astype(F32) * v.pop("dp")).astype(BF)

    def products(i, v):
        c, p, at, cs = place(i)
        ds = v.pop("ds")
        dkk = nn(ds, stack_heads(s.q[at, cs]))
        dvv = nn(s.pr[p, c], stack_heads(s.gmix[at, cs]))
        s.dk[at, cs] = dkk[:128]
        s.dks[at, cs] = dkk[128:].astype(BF)
        s.dv[at, cs] = dvv[:128]
        s.dvs[at, cs] = dvv[128:].astype(BF)
        kk = jnp.concatenate([s.k[at, cs], s.ks[at, cs]], axis=0)
        v["dq"] = pick_rows(nn(jnp.transpose(kk, (1, 0)), ds))

    def store(i, v):
        c, p, at, cs = place(i)
        s.dq[at, cs] = jnp.transpose(v.pop("dq"), (1, 0)) * scale
    pipeline(range(16), (grad_probs, grad_scores, products, store), (0, 2, 4, 6), after)


def st_sort_back(s, t):
    a, b = iota((128, 128), 0), iota((128, 128), 1)
    same = ((a >> 2) & 3) == ((b >> 2) & 3)
    accs = [[], []]

    def mix(i, v):
        j, rq = i // 8, i % 8
        cs = pair_cols(t, j)
        kv = jnp.concatenate([gather_chunk(s.k, rq, cs), gather_chunk(s.v, rq, cs)], axis=1)
        st = split_pair(jnp.concatenate([gather_chunk(s.dks, rq, cs), gather_chunk(s.dvs, rq, cs)], axis=1))
        accs[j].append(nt(st, kv))
        h = 4 * t + 2 * j
        v["out"] = nn(jnp.concatenate([s.krt[h], s.krt[h + 1]], axis=1), st)

    def store(i, v):
        j, rq = i // 8, i % 8
        cs = pair_cols(t, j)
        out = v.pop("out")
        for n in range(8):
            at = slice(n * 128 + rq * 16, n * 128 + rq * 16 + 16)
            s.dk[at, cs] = s.dk[at, cs] + out[n * 16:(n + 1) * 16, 0:128]
            s.dvb[at, cs] = (s.dv[at, cs] + out[n * 16:(n + 1) * 16, 128:256]).astype(BF)
    pipeline(range(16), (mix, store), (0, 2))
    x = jnp.concatenate([sum(accs[0]), sum(accs[1])], axis=0)
    x = jnp.where(jnp.concatenate([same] * 4, axis=0), x, 0.0)
    n = iota((128, NB), 0)
    cols_of = (((n >> 4) * 4 + (n & 3)) == iota((128, NB), 1)).astype(BF)
    m, n = iota((4 * NB, 512), 0), iota((4 * NB, 512), 1)
    rows_of = ((m >> 5) == (n >> 7)) & ((m & 31) == ((n >> 4) & 7) * 4 + (n & 3))
    high, low = two_terms(x)
    high, low = two_terms(nn(high, cols_of) + nn(low, cols_of))
    rows_of = rows_of.astype(BF)
    s.ds[pl.ds(pl.multiple_of(t * 4 * NB, 4 * NB), 4 * NB), :] = nn(rows_of, high) + nn(rows_of, low)


def two_terms(x):
    high = x.astype(BF)
    return high, (x - high.astype(F32)).astype(BF)


def sinkhorn_back(s, t):
    hs = pl.ds(pl.multiple_of(t * 4 * NB, 4 * NB), 4 * NB)
    v = {}

    def sweep(it):
        x = v["x"] if it < ITERS - 1 else s.ds[hs, :] * s.sk[2 * ITERS - 1, hs, :]
        y = x.reshape(4, NB, NB)
        pk = s.sk[2 * it + 1, hs, :].reshape(4, NB, NB)
        x = (y - pk * jnp.sum(y, axis=1, keepdims=True)).reshape(4 * NB, NB)
        v["x"] = x - s.sk[2 * it, hs, :] * jnp.sum(x, axis=1, keepdims=True)

    def means():
        mask = jnp.concatenate([s.allow[...]] * 4, axis=0) > 0
        x = jnp.where(mask, v.pop("x"), 0.0) * (1.0 / math.sqrt(HD))
        for j in range(2):
            cs = pair_cols(t, j)
            x0, x1 = x[2 * j * NB:(2 * j + 1) * NB], x[(2 * j + 1) * NB:(2 * j + 2) * NB]
            ev = even_lanes((NB, 128))
            km, qm = s.km[:, cs], s.qm[:, cs]
            v[j] = (jnp.where(ev, nn(x0, km, precision=HI), nn(x1, km, precision=HI)),
                    jnp.where(ev, tn(x0, qm, precision=HI), tn(x1, qm, precision=HI)))

    def spread(j):
        cs = pair_cols(t, j)
        dqm, dkm = v.pop(j)
        for c in range(8):
            at = slice(c * 128, (c + 1) * 128)
            for src, ref, dst in ((dqm, s.dq, s.dqb), (dkm, s.dk, s.dkb)):
                four = src[c * 4:(c + 1) * 4]
                eight = jnp.concatenate([four, four], axis=0)
                val = ref[at, cs].reshape(16, 8, 128) + eight[None]
                dst[at, cs] = val.reshape(128, 128).astype(BF)
    steps = [functools.partial(sweep, it) for it in reversed(range(ITERS))]
    return steps + [means, functools.partial(spread, 0), functools.partial(spread, 1)]


def st_value_grads(s, g, other, t, own):
    add_grads(g, other, t, own, slice(VO, VO + HALF), nn(s.nmt[...], s.dvb[:, half_cols(t)]))


def st_query_key_grads(s, g, other, t, own):
    for off, ref in ((QO, s.dqb), (KO, s.dkb)):
        add_grads(g, other, t, own, slice(off, off + HALF), nn(s.nmt[...], ref[:, half_cols(t)]))


def st_normed_back(s, w, t):
    cs = half_cols(t)

    def product(m):
        at = rows(m, 256)
        return nt(jnp.concatenate([s.dqb[at, cs], s.dkb[at, cs], s.dvb[at, cs]], axis=1), w[t, :, 0:768])
    return product


def st_tokens_back(s, w, t, gain_attn):
    parts = []
    half = st_normed_back(s, w, t)

    def product(m, v):
        v["g"] = half(m)

    def norm(m, v):
        at = rows(m, 256)
        gn = s.gn[at, :] + v.pop("g")
        xhat, inv = norm_rows(s.tokp[at, :].astype(F32), None)
        parts.append(jnp.sum((gn * xhat).reshape(32, 8, D), axis=0))
        s.mid[at, :] = s.mid[at, :] + norm_back(xhat, inv, gain_attn[...], gn)
    pipeline(range(4), (product, norm), (0, 1))
    s.gg[0:1, :] = jnp.sum(sum(parts), axis=0, keepdims=True)


def attention_backward(s, w, g, other, c, gain_attn, hooks):
    st_attend_back(s, 1 - c, hooks["attend0"])
    st_sort_back(s, 1 - c)
    hooks["sort0"]()
    steps = sinkhorn_back(s, 1 - c)

    def between(step):
        if step < len(steps):
            steps[step]()
        hooks["attend1"](step)
    st_attend_back(s, c, between)
    st_value_grads(s, g, None, 1 - c, False)
    st_query_key_grads(s, g, None, 1 - c, False)
    hooks["first"]()
    st_sort_back(s, c)
    hooks["sort1"]()
    st_value_grads(s, g, other, c, other is not None)
    hooks["values"]()
    product = st_normed_back(s, w, 1 - c)
    for n, step in enumerate(sinkhorn_back(s, c)):
        step()
        if n % 2 == 1 and n < 8:
            s.gn[rows(n // 2, 256), :] = product(n // 2)
    st_query_key_grads(s, g, other, c, other is not None)
    hooks["last"]()
    st_tokens_back(s, w, c, gain_attn)


class Names:
    pass


def stage_names(refs):
    s = Names()
    for n, r in zip(SCRATCH, refs):
        setattr(s, n, r)
    for n, o in SHARED.items():
        setattr(s, n, getattr(s, o))
    return s


def layer_kernel(tok, cot, gain_attn, gain_ffn, w, seg, result, gtok, g, gg, *scr):
    s = stage_names(scr)
    st_tokens(s, tok, gain_attn)
    st_cot(s, cot)
    transpose_into(s.cott, s.cotp)
    transpose_into(s.nmt, s.nm)
    st_bias(s)
    st_query_key(s, w)
    st_sinkhorn(s, seg)
    st_values(s, w)
    st_sort(s)
    st_attend(s, 0)
    st_attend(s, 1)
    st_out(s, w, gain_ffn)
    transpose_into(s.nft, s.nf)
    for t in range(2):
        for u in range(2):
            st_ffn(s, w, t, u, t + u == 0)
            st_ffn_grads(s, g, None, t, u, False)
    st_result(s, result, s.res)
    st_mid_back(s, w, gain_ffn)
    for t in range(2):
        st_out_grads(s, g, None, t, False)
    attention_backward(s, w, g, None, 0, gain_attn, collections.defaultdict(lambda: lambda *a: None))
    st_result(s, gtok, s.mid)
    gg[...] = s.gg[...]


def layer_call():
    vm = pl.BlockSpec(memory_space=pltpu.VMEM)
    return pl.pallas_call(
        layer_kernel,
        out_shape=(jax.ShapeDtypeStruct((T, D), BF), jax.ShapeDtypeStruct((T, D), BF),
                   jax.ShapeDtypeStruct((2, 4, 4, D // 16, COLS), BF), jax.ShapeDtypeStruct((8, D), F32)),
        in_specs=[vm] * 6, out_specs=(vm,) * 4,
        scratch_shapes=[pltpu.VMEM(*v) for v in SCRATCH.values()],
        compiler_params=pltpu.CompilerParams(vmem_limit_bytes=60 << 20),
    )


def split_cols(x):
    ins = jnp.concatenate([x[:, in_cols(u)] for u in range(2)], axis=1)
    downs = jnp.concatenate([x[:, down_cols(u)] for u in range(2)], axis=1)
    return x[:, QO:KO], x[:, KO:VO], x[:, VO:OO], x[:, OO:FO], ins, downs


def join_cols(q, k, v, o, i, d):
    parts = [q, k, v, o]
    for u in range(2):
        parts += [i[:, u * UNITS:(u + 1) * UNITS], d[:, u * UNITS:(u + 1) * UNITS]]
    return jnp.concatenate(parts, axis=1)


def by_collectives(tokens, gain_attn, gain_ffn, w_query, w_key, w_value, w_out, w_in, w_down, segment_ids, cotangent):
    tp = lax.axis_index("tp")
    tok = lax.all_to_all(tokens, "tp", 0, 0, tiled=True).reshape(T, D)
    cot = lax.all_to_all(cotangent, "tp", 0, 0, tiled=True).reshape(T, D)
    own = join_cols(w_query, w_key, w_value, w_out.T, w_in, w_down.T)
    half = lax.all_gather(own, "fsdp", axis=0, tiled=True)
    w = lax.all_gather(half, "tp", axis=0)
    seg = lax.dynamic_index_in_dim(segment_ids, tp, 0)
    res, gtok, g, gg = layer_call()(tok, cot, gain_attn[None], gain_ffn[None], w, seg)
    res = lax.all_to_all(res.reshape(tokens.shape), "tp", 0, 0, tiled=True)
    gtok = lax.all_to_all(gtok.reshape(tokens.shape), "tp", 0, 0, tiled=True)
    gsum = lax.psum_scatter(g.reshape(2, D, COLS).astype(F32), "tp", scatter_dimension=0)
    gsum = lax.psum_scatter(gsum, "fsdp", scatter_dimension=0, tiled=True)
    gains = lax.psum_scatter(gg[:2], ("fsdp", "tp"), scatter_dimension=1, tiled=True)
    q, k, v, o, i, d = split_cols(gsum)
    return res, gtok, gains[0], gains[1], q, k, v, o.T, i, d.T


PIECES = ((0, 512), (512, 1024), (1024, 2048), (2048, 3072))
GPIECES = ((1024, 2048), (2048, 3072), (768, 1024), (512, 768), (0, 512))
MESH = pl.DeviceIdType.MESH
ROWS = D // 16

EXCHANGE = dict(
    w=((2, D, COLS), BF), g=((2, 4, 4, ROWS, COLS), BF), other=((4, 4, ROWS, COLS), BF),
    rx=((3, 4, ROWS, COLS), BF), zs=((4, ROWS, COLS), BF), rz=((3, ROWS, COLS), BF),
    tok=((T, D), BF), cot=((T, D), BF), gr=((7, 8, D), F32), gs=((3, 8, D), F32),
)


def halves(lo, hi):
    mid = (lo + hi) // 2
    return slice(lo, mid), slice(mid, hi)


class Links:
    def __init__(self, e, sems):
        self.e = e
        self.sems = sems
        f, self.c = lax.axis_index("fsdp"), lax.axis_index("tp")
        self.zi, self.xy = f // 4, f % 4
        x, y = self.xy % 2, self.xy // 2
        self.f = f
        self.x_at, self.y_at, self.d_at = (1 - x) + 2 * y, x + 2 * (1 - y), (1 - x) + 2 * (1 - y)
        self.across = {"x": self.x_at, "y": self.y_at, "d": self.d_at}
        self.copies = {}
        self.agenda = []
        self.ran = set()

    def plan(self, *events):
        self.agenda += events

    def tick(self, n=1):
        for _ in range(n):
            if self.agenda:
                name = self.agenda.pop(0)
                getattr(self, name[0])(*name[1:])
                self.ran.add(name)

    def until(self, *name):
        while name not in self.ran:
            self.tick()

    def z_at(self, dz):
        return (self.zi + dz) % 4

    def z_from(self, dz):
        return (self.zi + 4 - dz) % 4

    def greet(self):
        self.bar = pltpu.get_barrier_semaphore()
        for dev in ([(self.z_at(d) * 4 + self.xy, self.c) for d in (1, 2, 3)]
                    + [(self.zi * 4 + k, self.c) for k in self.across.values()] + [(self.f, 1 - self.c)]):
            pl.semaphore_signal(self.bar, inc=1, device_id=dev, device_id_type=MESH)

    def meet(self):
        pl.semaphore_wait(self.bar, 7)

    def send(self, key, src, dst, to):
        sem = len(self.copies)
        if isinstance(to, int):
            dev = (self.z_at(to) * 4 + self.xy, self.c)
        elif to == "t":
            dev = (self.f, 1 - self.c)
        else:
            dev = (self.zi * 4 + self.across[to], self.c)
        copy = pltpu.make_async_remote_copy(
            src_ref=src, dst_ref=dst, send_sem=self.sems[0].at[sem], recv_sem=self.sems[1].at[sem],
            device_id=dev, device_id_type=MESH)
        copy.start()
        self.copies[key] = copy

    def arrived(self, *key):
        self.copies[key].wait_recv()

    def finish(self):
        for copy in self.copies.values():
            copy.wait_send()

    def w_rows(self, first, count, cols):
        return self.e.w.at[self.c, pl.ds(pl.multiple_of(first * ROWS, count * ROWS), count * ROWS), cols]

    def own(self, piece):
        at = self.w_rows(self.f, 1, slice(*PIECES[piece]))
        for d in (1, 2, 3):
            self.send(("z", piece, d), at, at, d)
        self.to_plane(piece, 0, at)

    def to_plane(self, piece, d, at):
        for k in ("x", "y") + (("d",) if piece == 0 else ()):
            self.send((k, piece, d), at, at, k)

    def plane(self, piece, d):
        self.arrived("z", piece, d)
        self.to_plane(piece, d, self.w_rows(self.z_from(d) * 4 + self.xy, 1, slice(*PIECES[piece])))

    def corner(self, piece, d):
        first, second = halves(*PIECES[piece])
        for k, to, cols in (("x", "y", first), ("y", "x", second)):
            self.arrived(k, piece, d)
            at = self.w_rows(self.z_from(d) * 4 + self.across[k], 1, cols)
            self.send((k + to, piece, d), at, at, to)

    def pair(self, piece, d):
        for k in ("x", "y", "d") if piece == 0 else ("xy", "yx"):
            self.arrived(k, piece, d)
        at = self.w_rows(self.z_from(d) * 4, 4, slice(*PIECES[piece]))
        self.send(("t", piece, d), at, at, "t")

    def gathered(self, piece):
        self.until("pair", piece, 3)
        for d in range(4):
            self.arrived("t", piece, d)

    def grads_pair(self, name, lo, hi):
        e = self.e
        self.send(("gt", name), e.g.at[1 - self.c, :, :, :, lo:hi], e.other.at[:, :, :, lo:hi], "t")

    def mine(self, k, cols):
        return self.e.g.at[self.c, :, self.across[k], :, cols]

    def grads_plane(self, piece):
        cols = slice(*GPIECES[piece])
        for n, k in enumerate("xyd"):
            self.send(("g" + k, piece), self.mine(k, cols), self.e.rx.at[n, :, :, cols], k)

    def grads_part(self, piece):
        first, second = halves(*GPIECES[piece])
        rx = self.e.rx
        self.send(("gd", piece, 0), self.mine("d", first), rx.at[2, :, :, first], "x")
        self.send(("gd", piece, 1), self.mine("d", second), rx.at[2, :, :, second], "y")
        self.send(("gx", piece, 0), self.mine("x", first), rx.at[0, :, :, first], "x")
        self.send(("gy", piece, 1), self.mine("y", second), rx.at[1, :, :, second], "y")

    def grads_join(self, piece):
        first, second = halves(*GPIECES[piece])
        rx = self.e.rx
        for n, k, cols in ((0, "y", first), (1, "x", second)):
            self.arrived("gd", piece, n)
            at = self.mine(k, cols)
            at[...] = (at[...].astype(F32) + rx[2, :, :, cols].astype(F32)).astype(BF)
            self.send(("g" + k, piece, n), at, rx.at["xy".index(k), :, :, cols], k)

    def grads_line(self, piece, direct):
        e = self.e
        lo, hi = GPIECES[piece]
        cols = slice(lo, hi)
        if direct:
            for k in "xyd":
                self.arrived("g" + k, piece)
        else:
            for k in "xy":
                for n in range(2):
                    self.arrived("g" + k, piece, n)
        for d in (1, 2, 3, 0):
            z = self.z_at(d)
            total = e.g[self.c, z, self.xy, :, cols].astype(F32)
            for n in range(3 if direct else 2):
                total = total + e.rx[n, z, :, cols].astype(F32)
            if d:
                e.zs[d, :, cols] = total.astype(BF)
                self.send(("gz", piece, d), e.zs.at[d, :, cols], e.rz.at[d - 1, :, cols], d)
            else:
                self.out.put(cols, total)

    def grads_in(self, piece):
        cols = slice(*GPIECES[piece])
        for d in (1, 2, 3):
            self.arrived("gz", piece, d)
        total = self.out.get(cols)
        for d in range(3):
            total = total + self.e.rz[d, :, cols].astype(F32)
        self.out.put(cols, total)

    def gains_sum(self, step):
        e = self.e
        if step == 0:
            self.send(("n", 0), e.gs.at[0], e.gr.at[0], "t")
        if step == 1:
            self.arrived("n", 0)
            e.gs[1] = e.gs[0] + e.gr[0]
            for n, k in enumerate("xyd"):
                self.send(("n", 1 + n), e.gs.at[1], e.gr.at[1 + n], k)
        if step == 2:
            for n in range(3):
                self.arrived("n", 1 + n)
            e.gs[2] = e.gs[1] + e.gr[1] + e.gr[2] + e.gr[3]
            for d in (1, 2, 3):
                self.send(("n", 3 + d), e.gs.at[2], e.gr.at[3 + d], d)
        if step == 3:
            for d in (1, 2, 3):
                self.arrived("n", 3 + d)
            return e.gs[2] + e.gr[4] + e.gr[5] + e.gr[6]


NSEM = 200


class GradOut:
    def __init__(self, gq, gk, gv, go, gi, gd):
        half = slice(0, HALF)
        self.places = [(QO, gq, half), (KO, gk, half), (VO, gv, half), (OO, go, half)]
        for u in range(2):
            at = slice(u * UNITS, (u + 1) * UNITS)
            self.places += [(in_cols(u).start, gi, at), (down_cols(u).start, gd, at)]

    def within(self, cols):
        for start, ref, at in self.places:
            if cols.start <= start < cols.stop:
                yield start - cols.start, ref, at

    def put(self, cols, val):
        for off, ref, at in self.within(cols):
            ref[:, at] = val[:, off:off + at.stop - at.start]

    def get(self, cols):
        return jnp.concatenate([ref[:, at] for _, ref, at in self.within(cols)], axis=1)


def step_kernel(tokens, cotangent, gain_attn, gain_ffn, wq, wk, wv, wo, wi, wd, seg, result, gtok, gain_a, gain_f,
                gq, gk, gv, go, gi, gd, *scr):
    ns, ne = len(SCRATCH), len(EXCHANGE)
    s = stage_names(scr[:ns])
    e = Names()
    for n, r in zip(EXCHANGE, scr[ns:ns + ne]):
        setattr(e, n, r)
    send_sem, recv_sem, local = scr[ns + ne:]
    link = Links(e, (send_sem, recv_sem))
    c, f, w, g = link.c, link.f, e.w, e.g
    half = T // 2
    mine = pl.ds(pl.multiple_of(c * half, half), half)
    theirs = pl.ds(pl.multiple_of((1 - c) * half, half), half)
    pair = (f, 1 - c)

    link.out = GradOut(gq, gk, gv, go, gi, gd)
    loads = [pltpu.make_async_copy(tokens.at[c], e.tok.at[mine, :], local.at[0]),
             pltpu.make_async_copy(cotangent.at[c], e.cot.at[mine, :], local.at[1])]
    for cp in loads:
        cp.start()
    link.greet()
    w[c, pl.ds(pl.multiple_of(f * ROWS, ROWS), ROWS), :] = join_cols(wq[...], wk[...], wv[...], wo[...], wi[...], wd[...])
    link.meet()
    link.own(0)
    link.send(("tok",), tokens.at[1 - c], e.tok.at[mine, :], "t")
    link.send(("cot",), cotangent.at[1 - c], e.cot.at[mine, :], "t")
    link.own(1)
    loads[0].wait()
    link.arrived("tok")
    st_tokens(s, e.tok, gain_attn)
    link.plan(*[("plane", 0, d) for d in (1, 2, 3)], *[("plane", 1, d) for d in (1, 2, 3)], ("own", 2))
    link.tick(3)
    loads[1].wait()
    link.arrived("cot")
    st_cot(s, e.cot)
    link.tick(4)
    transpose_into(s.cott, s.cotp)
    transpose_into(s.nmt, s.nm)
    st_bias(s)
    link.plan(*[("pair", 0, d) for d in range(4)], *[("corner", 1, d) for d in range(4)])
    link.plan(*[("plane", 2, d) for d in (1, 2, 3)], *[("pair", 1, d) for d in range(4)], ("own", 3))
    link.plan(*[("corner", 2, d) for d in range(4)], *[("plane", 3, d) for d in (1, 2, 3)])
    link.plan(*[("pair", 2, d) for d in range(4)], *[("corner", 3, d) for d in range(4)], *[("pair", 3, d) for d in range(4)])
    link.gathered(0)
    st_query_key(s, w, lambda i: link.tick())
    st_sinkhorn(s, seg.at[pl.ds(c, 1), :], lambda i: link.tick())
    link.gathered(1)
    st_values(s, w)
    st_sort(s)
    link.until("own", 3)
    st_attend(s, 0, lambda i: link.tick() if i % 4 == 3 else None)
    st_attend(s, 1, lambda i: link.tick() if i % 4 == 3 else None)
    st_out(s, w, gain_ffn)
    transpose_into(s.nft, s.nf)
    link.gathered(2)
    grads_at = {
        (0, "mid"): lambda i: link.tick() if i % 2 == 1 else None,
        (0, "own"): lambda i: link.tick() if i % 2 == 1 else None,
        (1, "mid"): lambda i: link.tick() if i == 3 else None,
        (1, "own"): lambda i: None,
    }
    for u in range(2):
        if u == 1:
            link.gathered(3)
            link.plan(("grads_join", 0))
        st_ffn(s, w, 1 - c, u, u == 0, grads_at[u, "mid"])
        st_ffn_grads(s, g, None, 1 - c, u, False)
        link.grads_pair(u, *GPIECES[u])
        st_ffn(s, w, c, u, False, grads_at[u, "own"])
        link.arrived("gt", u)
        st_ffn_grads(s, g, e.other, c, u, True)
        link.grads_part(u)
    st_result(s, e.tok, s.res)
    stores = [pltpu.make_async_copy(e.tok.at[mine, :], result.at[c], local.at[2])]
    stores[0].start()
    link.send(("res",), e.tok.at[theirs, :], result.at[c], "t")
    st_mid_back(s, w, gain_ffn)
    st_out_grads(s, g, None, 1 - c, False)
    link.grads_pair(2, *GPIECES[2])
    link.plan(("grads_line", 0, False), ("grads_join", 1))
    link.tick()
    link.arrived("gt", 2)
    st_out_grads(s, g, e.other, c, True)
    link.grads_plane(2)

    def first():
        link.grads_pair(3, 0, 768)
        link.plan(("grads_line", 1, False), ("grads_in", 0))
        link.tick()

    def values():
        link.arrived("gt", 3)

    def sort1():
        values()
        link.tick()

    def after_values():
        link.grads_plane(3)
        link.plan(("grads_line", 2, True))
        link.tick()

    def last():
        link.grads_plane(4)
        link.plan(("grads_line", 3, True), ("grads_in", 1), ("grads_in", 2))
        link.tick(1)

    attention_backward(s, w, g, e.other, c, gain_attn, {
        "attend0": lambda i: link.tick() if i == 12 else None, "sort0": lambda: None, "attend1": lambda i: None,
        "first": first, "sort1": sort1, "values": after_values, "last": last})
    e.gs[0] = s.gg[...]
    link.gains_sum(0)
    st_result(s, e.cot, s.mid)
    stores.append(pltpu.make_async_copy(e.cot.at[mine, :], gtok.at[c], local.at[3]))
    stores[1].start()
    link.send(("gtok",), e.cot.at[theirs, :], gtok.at[c], "t")
    link.gains_sum(1)
    link.grads_line(4, True)
    link.gains_sum(2)
    link.tick(2)
    link.grads_in(3)
    total = link.gains_sum(3)
    width = gain_a.shape[1]
    pick = (iota((D, width), 0) == iota((D, width), 1) + (2 * f + c) * width).astype(F32)
    picked = nn(total, pick, precision=HI)
    gain_a[...] = picked[0:1]
    gain_f[...] = picked[1:2]
    link.grads_in(4)
    link.arrived("res")
    link.arrived("gtok")
    for cp in stores:
        cp.wait()
    link.finish()


def by_kernel(tokens, gain_attn, gain_ffn, w_query, w_key, w_value, w_out, w_in, w_down, segment_ids, cotangent):
    vm, hbm = pl.BlockSpec(memory_space=pltpu.VMEM), pl.BlockSpec(memory_space=pl.ANY)
    width = D // 32
    shapes = list(SCRATCH.values()) + list(EXCHANGE.values())
    square, long, row = (ROWS, HALF), (ROWS, FF // 2), (1, width)
    outs = [row, row, square, square, square, square, long, long]
    res, gtok, gain_a, gain_f, q, k, v, o, i, d = pl.pallas_call(
        step_kernel,
        out_shape=(jax.ShapeDtypeStruct(tokens.shape, BF),) * 2 + tuple(jax.ShapeDtypeStruct(x, F32) for x in outs),
        in_specs=[hbm] * 2 + [vm] * 9, out_specs=(hbm, hbm) + (vm,) * 8,
        scratch_shapes=[pltpu.VMEM(*v) for v in shapes] + [
            pltpu.SemaphoreType.DMA((NSEM,)), pltpu.SemaphoreType.DMA((NSEM,)), pltpu.SemaphoreType.DMA((4,))],
        compiler_params=pltpu.CompilerParams(collective_id=0, has_side_effects=True, vmem_limit_bytes=63 << 20),
    )(tokens, cotangent, gain_attn[None], gain_ffn[None], w_query, w_key, w_value, w_out.T, w_in, w_down.T, segment_ids)
    return res, gtok, gain_a.reshape(width), gain_f.reshape(width), q, k, v, o.T, i, d.T


def solution(mesh):
    body = by_kernel if mesh.shape["fsdp"] == 16 else by_collectives
    return jax.shard_map(
        body,
        mesh=mesh,
        in_specs=(P(None, ("fsdp", "tp"), None), P(), P(), P("fsdp", "tp"), P("fsdp", "tp"), P("fsdp", "tp"),
                  P("tp", "fsdp"), P("fsdp", "tp"), P("tp", "fsdp"), P(None, "fsdp"), P(None, ("fsdp", "tp"), None)),
        out_specs=(P(None, ("fsdp", "tp"), None), P(None, ("fsdp", "tp"), None), P(("fsdp", "tp")), P(("fsdp", "tp")),
                   P("fsdp", "tp"), P("fsdp", "tp"), P("fsdp", "tp"), P("tp", "fsdp"), P("fsdp", "tp"), P("tp", "fsdp")),
        check_vma=False,
    )
```

```python
import collections
import functools
import math
import jax, jax.numpy as jnp
from jax import lax
from jax.experimental import pallas as pl
from jax.experimental.pallas import tpu as pltpu
from jax.sharding import PartitionSpec as P

F32, BF = jnp.float32, jnp.bfloat16
HI = lax.Precision.HIGHEST
HD, BLK, ITERS, NB, D, FF, T = 64, 32, 8, 32, 512, 2048, 1024
HALF = D // 2
COLS = 3 * HALF + HALF + FF
QO, KO, VO, OO, FO = 0, 256, 512, 768, 1024
UNITS = 512


def in_cols(u):
    return slice(FO + 2 * u * UNITS, FO + (2 * u + 1) * UNITS)


def down_cols(u):
    return slice(FO + (2 * u + 1) * UNITS, FO + (2 * u + 2) * UNITS)


def span(start, count):
    return pl.ds(pl.multiple_of(start, 128), count)


def nn(a, b, precision=None):
    return lax.dot_general(a, b, (((1,), (0,)), ((), ())), precision=precision, preferred_element_type=F32)


def nt(a, b, precision=None):
    return lax.dot_general(a, b, (((1,), (1,)), ((), ())), precision=precision, preferred_element_type=F32)


def tn(a, b, precision=None):
    return lax.dot_general(a, b, (((0,), (0,)), ((), ())), precision=precision, preferred_element_type=F32)


def iota(shape, dim):
    return lax.broadcasted_iota(jnp.int32, shape, dim)


def order_matrix(inverse):
    n, m = iota((128, 128), 0), iota((128, 128), 1)
    if inverse:
        n, m = m, n
    return (m == (n & 3) * 32 + (n >> 2)).astype(BF)


def norm_rows(x, gain):
    center = x - jnp.mean(x, axis=1, keepdims=True)
    inv = lax.rsqrt(jnp.mean(center * center, axis=1, keepdims=True) + 1e-05)
    xhat = center * inv
    return xhat, inv


def norm_back(xhat, inv, gain, grad):
    gx = grad * gain
    m1 = jnp.mean(gx, axis=1, keepdims=True)
    m2 = jnp.mean(gx * xhat, axis=1, keepdims=True)
    return inv * (gx - m1 - xhat * m2)


def even_lanes(shape):
    return (iota(shape, len(shape) - 1) & 127) < 64


def stack_heads(x):
    ev = even_lanes(x.shape)
    z = jnp.zeros_like(x)
    return jnp.concatenate([jnp.where(ev, x, z), jnp.where(ev, z, x)], axis=0)


def pick_heads(r):
    n = r.shape[0] // 2
    ev = even_lanes((n, r.shape[1]))
    return jnp.where(ev, r[:n], r[n:])


SCRATCH = dict(
    tokp=((T, D), BF), cotp=((T, D), BF), cott=((D, T), BF), nm=((T, D), BF), nmt=((D, T), BF),
    q=((T, D), BF), k=((T, D), BF), v=((T, D), BF), ks=((T, D), BF), vs=((T, D), BF),
    qm=((NB, D), F32), km=((NB, D), F32), sk=((2 * ITERS, 8 * NB, NB), F32), allow=((NB, NB), F32),
    kr=((8, 128, 128), BF), krt=((8, 128, 128), BF), hidq=((256, 128), BF), hidk=((256, 128), BF),
    pr=((4, 8, 256, 256), BF), mix=((T, D), BF), mid=((T, D), F32), nf=((T, D), BF), nft=((D, T), BF),
    hid=((T, UNITS), BF), gp=((T, UNITS), BF), res=((T, D), F32), gnf=((T, D), F32),
    ga=((T, D), BF), gat=((D, T), BF), gmix=((T, D), BF), dv=((T, D), F32), ds=((8 * NB, NB), F32),
    gg=((8, D), F32),
)
SHARED = dict(dq="res", dk="gnf", dks="hid", dvs="gp", dqb="ga", dkb="nm", dvb="nf")


def loop(n, body, unroll=1):
    lax.fori_loop(0, n, lambda i, c: (body(i), c)[1], 0, unroll=unroll)


def rows(i, n):
    return pl.ds(pl.multiple_of(i * n, n), n)


def pipeline(units, stages, lags, after=None):
    vals = [{} for _ in units]
    for step in range(len(units) + lags[-1]):
        for st, lag in reversed(list(zip(stages, lags))):
            if 0 <= step - lag < len(units):
                st(units[step - lag], vals[step - lag])
        if after is not None:
            after(step)


def st_tokens(s, tok, gain_attn):
    pm = order_matrix(False)

    def body(c):
        def order(i, v):
            v["x"] = nn(pm, tok[rows(4 * c + i, 128), :])

        def norm(i, v):
            at = rows(4 * c + i, 128)
            x = v.pop("x")
            s.tokp[at, :] = x.astype(BF)
            xhat, _ = norm_rows(x, None)
            s.nm[at, :] = (xhat * gain_attn[...]).astype(BF)
        pipeline(range(4), (order, norm), (0, 1))
    loop(2, body)


def st_cot(s, cot):
    pm = order_matrix(False)

    def body(c):
        for i in range(4):
            at = rows(4 * c + i, 128)
            s.cotp[at, :] = nn(pm, cot[at, :]).astype(BF)
    loop(2, body)


def transpose_into(dst, src):
    for c in range(4):
        dst[:, c * 256:(c + 1) * 256] = jnp.transpose(src[c * 256:(c + 1) * 256, :], (1, 0))


def block_sums(x):
    y = jnp.sum(x.reshape(16, 8, x.shape[1]), axis=0)
    return y[0:4] + y[4:8]


def st_values(s, w):
    for m in range(4):
        x = s.nm[rows(m, 256), :]
        for t in range(2):
            s.v[rows(m, 256), t * 256:(t + 1) * 256] = nn(x, w[t, :, VO:VO + HALF]).astype(BF)


def st_query_key(s, w):
    def product(m, v):
        x = s.nm[rows(m, 256), :]
        v["x"] = [nn(x, w[t, :, 0:512]).astype(BF) for t in range(2)]

    def store(m, v):
        at = rows(m, 256)
        for t, out in enumerate(v.pop("x")):
            cs = slice(t * 256, (t + 1) * 256)
            qv, kv = out[:, 0:256].astype(F32), out[:, 256:512].astype(F32)
            s.q[at, cs] = (qv * (1.0 / math.sqrt(HD))).astype(BF)
            s.k[at, cs] = out[:, 256:512]
            for ref, val in ((s.qm, qv), (s.km, kv)):
                sums = jnp.concatenate([block_sums(val[:128]), block_sums(val[128:])], axis=0)
                ref[rows(m, 8), cs] = sums * (1.0 / BLK)
    pipeline(range(4), (product, store), (0, 1))


def st_sinkhorn(s, seg, halfway=None):
    row = jnp.broadcast_to(seg[...], (NB, NB))
    ri, ci = iota((NB, NB), 0), iota((NB, NB), 1)
    col = jnp.sum(jnp.where(ri == ci, row, 0), axis=1, keepdims=True)
    allow = ((row == col) & (ci <= ri)) | ((row == 0) & (col > 0))
    s.allow[...] = allow.astype(F32)
    parts = []
    for p in range(4):
        cs = slice(p * 128, (p + 1) * 128)
        parts.append(nt(stack_heads(s.qm[:, cs]), s.km[:, cs], precision=HI))
    x = jnp.concatenate(parts, axis=0) * (BLK / math.sqrt(HD))
    mask = jnp.concatenate([allow.astype(F32)] * 8, axis=0) > 0
    x = jnp.where(mask, x, -1000000000.0)
    for it in range(ITERS):
        m = jnp.max(x, axis=1, keepdims=True)
        e = jnp.exp(x - m)
        z = jnp.sum(e, axis=1, keepdims=True)
        s.sk[2 * it] = e * (1.0 / z)
        x = x - (m + jnp.log(z))
        y = x.reshape(8, NB, NB)
        m = jnp.max(y, axis=1, keepdims=True)
        e = jnp.exp(y - m)
        z = jnp.sum(e, axis=1, keepdims=True)
        s.sk[2 * it + 1] = (e * (1.0 / z)).reshape(8 * NB, NB)
        x = (y - (m + jnp.log(z))).reshape(8 * NB, NB)
        if it == ITERS // 2 - 1 and halfway is not None:
            halfway()
    sorter = s.sk[2 * ITERS - 1].astype(BF)
    n = iota((128, NB), 0)
    e_mat = (((n >> 4) * 4 + (n & 3)) == iota((128, NB), 1)).astype(BF)
    wide = nt(sorter, e_mat).astype(BF)
    a, b = iota((128, 128), 0), iota((128, 128), 1)
    same = ((a >> 2) & 3) == ((b >> 2) & 3)
    for h in range(8):
        kr = jnp.where(same, nn(e_mat, wide[h * NB:(h + 1) * NB]), 0.0)
        s.kr[h] = kr.astype(BF)
        s.krt[h] = jnp.transpose(kr, (1, 0)).astype(BF)


def gather_chunk(ref, rq, cs):
    return jnp.concatenate([ref[pl.ds(pl.multiple_of(i * 128 + rq * 16, 16), 16), cs] for i in range(8)], axis=0)


def split_pair(x):
    return stack_heads(x)


def st_sort(s):
    def body(r):
        def mix(unit, v):
            rq, p = 2 * r + unit // 4, unit % 4
            cs = slice(p * 128, (p + 1) * 128)
            kv = jnp.concatenate([gather_chunk(s.k, rq, cs), gather_chunk(s.v, rq, cs)], axis=1)
            lhs = jnp.concatenate([s.kr[2 * p], s.kr[2 * p + 1]], axis=1)
            v["out"] = nn(lhs, split_pair(kv))

        def store(unit, v):
            rq, p = 2 * r + unit // 4, unit % 4
            cs = slice(p * 128, (p + 1) * 128)
            out = v.pop("out").astype(BF)
            for i in range(8):
                at = pl.ds(pl.multiple_of(i * 128 + rq * 16, 16), 16)
                s.ks[at, cs] = out[i * 16:(i + 1) * 16, 0:128]
                s.vs[at, cs] = out[i * 16:(i + 1) * 16, 128:256]
        pipeline(range(8), (mix, store), (0, 2))
    loop(4, body)


def st_bias(s):
    n, a = iota((256, 128), 0), iota((256, 128), 1)
    s.hidq[...] = ((a == (n & 3)) | (a == 4 + ((n & 127) >> 2))).astype(BF)
    other = (a < 4) & (a != (n & 3))
    later = (n < 128) & (a >= 4) & (a < 36) & ((n >> 2) > a - 4)
    s.hidk[...] = jnp.where(other | later, -1e30, 0.0).astype(BF)


def pick_rows(r):
    n = r.shape[1] // 2
    return jnp.concatenate([r[:64, :n], r[64:, n:]], axis=0)


def chunk_pair(c, i):
    p = i % 4
    c = c + i // 4
    return c, p, rows(c, 128), slice(p * 128, (p + 1) * 128)


def st_attend(s, b):
    def score(i, v):
        c, p, at, cs = chunk_pair(4 * b, i)
        qs = jnp.concatenate([stack_heads(s.q[at, cs]), s.hidq[...]], axis=1)
        kk = jnp.concatenate([jnp.concatenate([s.k[at, cs], s.ks[at, cs]], axis=0), s.hidk[...]], axis=1)
        v["x"] = nt(kk, qs)

    def soften(i, v):
        c, p, at, cs = chunk_pair(4 * b, i)
        x = v.pop("x")
        e = jnp.exp(x - jnp.max(x, axis=0, keepdims=True))
        v["p"] = (e * (1.0 / jnp.sum(e, axis=0, keepdims=True))).astype(BF)
        s.pr[p, c] = v["p"]

    def blend(i, v):
        c, p, at, cs = chunk_pair(4 * b, i)
        vv = jnp.concatenate([s.v[at, cs], s.vs[at, cs]], axis=0)
        v["o"] = pick_rows(nn(jnp.transpose(vv, (1, 0)), v.pop("p")))

    def store(i, v):
        c, p, at, cs = chunk_pair(4 * b, i)
        s.mix[at, cs] = jnp.transpose(v.pop("o"), (1, 0)).astype(BF)
    pipeline(range(16), (score, soften, blend, store), (0, 2, 4, 6))


def st_out(s, w, gain_ffn):
    def product(m, v):
        at = rows(m, 256)
        v["x"] = sum(nt(s.mix[at, t * 256:(t + 1) * 256], w[t, :, OO:OO + HALF]) for t in range(2))

    def norm(m, v):
        at = rows(m, 256)
        mid = s.tokp[at, :].astype(F32) + v.pop("x")
        s.mid[at, :] = mid
        s.res[at, :] = mid
        s.gnf[at, :] = jnp.zeros((256, D), F32)
        xhat, _ = norm_rows(mid, None)
        s.nf[at, :] = (xhat * gain_ffn[...]).astype(BF)
    pipeline(range(4), (product, norm), (0, 1))


def gelu_pair(x):
    k0, k1 = math.sqrt(2.0 / math.pi), 0.044715
    x2 = x * x
    half = 0.5 + 0.5 * jnp.tanh(x * (k0 + (k0 * k1) * x2))
    val = x * half
    der = half + (val - val * half) * (2 * k0 + (6 * k0 * k1) * x2)
    return val, der


def add_grads(g, other, t, own, cols, val):
    if own:
        val = val + other[:, :, :, cols].reshape(D, val.shape[1]).astype(F32)
    g[t, :, :, :, cols] = val.astype(BF).reshape(4, 4, D // 16, val.shape[1])


def st_ffn(s, w, t, u, out):
    ic, dc = span(FO + 2 * u * UNITS, UNITS), span(FO + (2 * u + 1) * UNITS, UNITS)

    def into(m, v):
        at = rows(m, 256)
        v["x"] = nn(s.nf[at, :], w[t, :, ic])
        v["g"] = nn(s.cotp[at, :], w[t, :, dc])

    def bend(m, v):
        at = rows(m, 256)
        val, der = gelu_pair(v.pop("x"))
        v["h"] = val.astype(BF)
        v["g"] = (v["g"] * der).astype(BF)
        s.hid[at, :] = v["h"]
        s.gp[at, :] = v["g"]

    def back(m, v):
        at = rows(m, 256)
        add = nt(v.pop("h"), w[t, :, dc])
        add = s.res[at, :] + add
        s.res[at, :] = add
        if out is not None:
            out[at, :] = add.astype(BF)
        add = nt(v.pop("g"), w[t, :, ic])
        s.gnf[at, :] = s.gnf[at, :] + add
    pipeline(range(4), (into, bend, back), (0, 2, 3))


def st_ffn_grads(s, g, other, t, u, own):
    add_grads(g, other, t, own, span(FO + 2 * u * UNITS, UNITS), nn(s.nft[...], s.gp[...]))
    add_grads(g, other, t, own, span(FO + (2 * u + 1) * UNITS, UNITS), nn(s.cott[...], s.hid[...]))


def st_mid_back(s, w, gain_ffn):
    parts = []

    def norm(m, v):
        at = rows(m, 256)
        xhat, inv = norm_rows(s.mid[at, :], None)
        gnf = s.gnf[at, :]
        parts.append(jnp.sum((gnf * xhat).reshape(32, 8, D), axis=0))
        gm = s.cotp[at, :].astype(F32) + norm_back(xhat, inv, gain_ffn[...], gnf)
        s.mid[at, :] = gm
        v["ga"] = gm.astype(BF)
        s.ga[at, :] = v["ga"]

    def product(m, v):
        at = rows(m, 256)
        ga = v.pop("ga")
        for t in range(2):
            s.gmix[at, t * 256:(t + 1) * 256] = nn(ga, w[t, :, OO:OO + HALF]).astype(BF)
        s.gat[:, m * 256:(m + 1) * 256] = jnp.transpose(ga, (1, 0))
    pipeline(range(4), (norm, product), (0, 1))
    s.gg[1:2, :] = jnp.sum(sum(parts), axis=0, keepdims=True)


def half_cols(t):
    return pl.ds(pl.multiple_of(t * HALF, HALF), HALF)


def st_out_grads(s, g, other, t, own):
    add_grads(g, other, t, own, slice(OO, OO + HALF), nn(s.gat[...], s.mix[:, half_cols(t)]))


def st_restore(src):
    pm = order_matrix(True)
    for c in range(8):
        at = slice(c * 128, (c + 1) * 128)
        src[at, :] = nn(pm, src[at, :]).astype(BF)


def pair_cols(t, j):
    return pl.ds(pl.multiple_of(t * HALF + j * 128, 128), 128)


def st_attend_back(s, t, after=None):
    scale = 1.0 / math.sqrt(HD)

    def place(i):
        c, j = i // 2, i % 2
        return c, 2 * t + j, slice(c * 128, (c + 1) * 128), pair_cols(t, j)

    def grad_probs(i, v):
        c, p, at, cs = place(i)
        g = s.gmix[at, cs]
        go = (g.astype(F32) * s.mix[at, cs].astype(F32)).astype(BF)
        vv = jnp.concatenate([s.v[at, cs], s.vs[at, cs]], axis=0)
        v["dp"] = nt(jnp.concatenate([vv, jnp.full_like(vv, -1.0)], axis=1),
                     jnp.concatenate([stack_heads(g), stack_heads(go)], axis=1))

    def grad_scores(i, v):
        c, p, at, cs = place(i)
        v["ds"] = (s.pr[p, c].astype(F32) * v.pop("dp")).astype(BF)

    def products(i, v):
        c, p, at, cs = place(i)
        ds = v.pop("ds")
        dkk = nn(ds, stack_heads(s.q[at, cs]))
        dvv = nn(s.pr[p, c], stack_heads(s.gmix[at, cs]))
        s.dk[at, cs] = dkk[:128]
        s.dks[at, cs] = dkk[128:].astype(BF)
        s.dv[at, cs] = dvv[:128]
        s.dvs[at, cs] = dvv[128:].astype(BF)
        kk = jnp.concatenate([s.k[at, cs], s.ks[at, cs]], axis=0)
        v["dq"] = pick_rows(nn(jnp.transpose(kk, (1, 0)), ds))

    def store(i, v):
        c, p, at, cs = place(i)
        s.dq[at, cs] = jnp.transpose(v.pop("dq"), (1, 0)) * scale
    pipeline(range(16), (grad_probs, grad_scores, products, store), (0, 2, 4, 6), after)


def st_sort_back(s, t):
    a, b = iota((128, 128), 0), iota((128, 128), 1)
    same = ((a >> 2) & 3) == ((b >> 2) & 3)
    accs = [[], []]

    def mix(i, v):
        j, rq = i // 8, i % 8
        cs = pair_cols(t, j)
        kv = jnp.concatenate([gather_chunk(s.k, rq, cs), gather_chunk(s.v, rq, cs)], axis=1)
        st = split_pair(jnp.concatenate([gather_chunk(s.dks, rq, cs), gather_chunk(s.dvs, rq, cs)], axis=1))
        accs[j].append(nt(st, kv))
        h = 4 * t + 2 * j
        v["out"] = nn(jnp.concatenate([s.krt[h], s.krt[h + 1]], axis=1), st)

    def store(i, v):
        j, rq = i // 8, i % 8
        cs = pair_cols(t, j)
        out = v.pop("out")
        for n in range(8):
            at = slice(n * 128 + rq * 16, n * 128 + rq * 16 + 16)
            s.dk[at, cs] = s.dk[at, cs] + out[n * 16:(n + 1) * 16, 0:128]
            s.dvb[at, cs] = (s.dv[at, cs] + out[n * 16:(n + 1) * 16, 128:256]).astype(BF)
    pipeline(range(16), (mix, store), (0, 2))
    x = jnp.concatenate([sum(accs[0]), sum(accs[1])], axis=0)
    x = jnp.where(jnp.concatenate([same] * 4, axis=0), x, 0.0)
    n = iota((128, NB), 0)
    cols_of = (((n >> 4) * 4 + (n & 3)) == iota((128, NB), 1)).astype(BF)
    m, n = iota((4 * NB, 512), 0), iota((4 * NB, 512), 1)
    rows_of = ((m >> 5) == (n >> 7)) & ((m & 31) == ((n >> 4) & 7) * 4 + (n & 3))
    high, low = two_terms(x)
    high, low = two_terms(nn(high, cols_of) + nn(low, cols_of))
    rows_of = rows_of.astype(BF)
    s.ds[pl.ds(pl.multiple_of(t * 4 * NB, 4 * NB), 4 * NB), :] = nn(rows_of, high) + nn(rows_of, low)


def two_terms(x):
    high = x.astype(BF)
    return high, (x - high.astype(F32)).astype(BF)


def sinkhorn_back(s, t):
    hs = pl.ds(pl.multiple_of(t * 4 * NB, 4 * NB), 4 * NB)
    v = {}

    def sweep(it):
        x = v["x"] if it < ITERS - 1 else s.ds[hs, :] * s.sk[2 * ITERS - 1, hs, :]
        y = x.reshape(4, NB, NB)
        pk = s.sk[2 * it + 1, hs, :].reshape(4, NB, NB)
        x = (y - pk * jnp.sum(y, axis=1, keepdims=True)).reshape(4 * NB, NB)
        v["x"] = x - s.sk[2 * it, hs, :] * jnp.sum(x, axis=1, keepdims=True)

    def means():
        mask = jnp.concatenate([s.allow[...]] * 4, axis=0) > 0
        x = jnp.where(mask, v.pop("x"), 0.0) * (1.0 / math.sqrt(HD))
        for j in range(2):
            cs = pair_cols(t, j)
            x0, x1 = x[2 * j * NB:(2 * j + 1) * NB], x[(2 * j + 1) * NB:(2 * j + 2) * NB]
            ev = even_lanes((NB, 128))
            km, qm = s.km[:, cs], s.qm[:, cs]
            v[j] = (jnp.where(ev, nn(x0, km, precision=HI), nn(x1, km, precision=HI)),
                    jnp.where(ev, tn(x0, qm, precision=HI), tn(x1, qm, precision=HI)))

    def spread(j):
        cs = pair_cols(t, j)
        dqm, dkm = v.pop(j)
        for c in range(8):
            at = slice(c * 128, (c + 1) * 128)
            for src, ref, dst in ((dqm, s.dq, s.dqb), (dkm, s.dk, s.dkb)):
                four = src[c * 4:(c + 1) * 4]
                eight = jnp.concatenate([four, four], axis=0)
                val = ref[at, cs].reshape(16, 8, 128) + eight[None]
                dst[at, cs] = val.reshape(128, 128).astype(BF)
    steps = [functools.partial(sweep, it) for it in reversed(range(ITERS))]
    return steps + [means, functools.partial(spread, 0), functools.partial(spread, 1)]


def st_value_grads(s, g, other, t, own):
    add_grads(g, other, t, own, slice(VO, VO + HALF), nn(s.nmt[...], s.dvb[:, half_cols(t)]))


def st_query_key_grads(s, g, other, t, own):
    for off, ref in ((QO, s.dqb), (KO, s.dkb)):
        add_grads(g, other, t, own, slice(off, off + HALF), nn(s.nmt[...], ref[:, half_cols(t)]))


def st_tokens_back(s, w, gain_attn, out):
    parts = []

    def product(m, v):
        at = rows(m, 256)
        v["g"] = 0.0
        for t in range(2):
            cs = slice(t * 256, (t + 1) * 256)
            v["g"] = v["g"] + nt(jnp.concatenate([s.dqb[at, cs], s.dkb[at, cs], s.dvb[at, cs]], axis=1), w[t, :, 0:768])

    def norm(m, v):
        at = rows(m, 256)
        gn = v.pop("g")
        xhat, inv = norm_rows(s.tokp[at, :].astype(F32), None)
        parts.append(jnp.sum((gn * xhat).reshape(32, 8, D), axis=0))
        out[at, :] = (s.mid[at, :] + norm_back(xhat, inv, gain_attn[...], gn)).astype(BF)
    pipeline(range(4), (product, norm), (0, 1))
    s.gg[0:1, :] = jnp.sum(sum(parts), axis=0, keepdims=True)


def attention_backward(s, w, g, other, c, gain_attn, out, hooks):
    st_attend_back(s, 1 - c)
    hooks["attend0"]()
    st_sort_back(s, 1 - c)
    steps = sinkhorn_back(s, 1 - c)

    st_attend_back(s, c, lambda n: steps[n]() if n < len(steps) else None)
    st_value_grads(s, g, None, 1 - c, False)
    st_query_key_grads(s, g, None, 1 - c, False)
    hooks["first"]()
    st_sort_back(s, c)
    hooks["sort1"]()
    st_value_grads(s, g, other, c, other is not None)
    hooks["values"]()
    for step in sinkhorn_back(s, c):
        step()
    st_query_key_grads(s, g, other, c, other is not None)
    hooks["last"]()
    st_tokens_back(s, w, gain_attn, out)


class Names:
    pass


def stage_names(refs):
    s = Names()
    for n, r in zip(SCRATCH, refs):
        setattr(s, n, r)
    for n, o in SHARED.items():
        setattr(s, n, getattr(s, o))
    return s


def layer_kernel(tok, cot, gain_attn, gain_ffn, w, seg, result, gtok, g, gg, *scr):
    s = stage_names(scr)
    st_tokens(s, tok, gain_attn)
    st_cot(s, cot)
    transpose_into(s.cott, s.cotp)
    transpose_into(s.nmt, s.nm)
    st_bias(s)
    st_query_key(s, w)
    st_sinkhorn(s, seg)
    st_values(s, w)
    st_sort(s)
    loop(2, functools.partial(st_attend, s))
    st_out(s, w, gain_ffn)
    transpose_into(s.nft, s.nf)
    def ffn(u):
        for t in range(2):
            st_ffn(s, w, t, u, result if t == 1 else None)
            st_ffn_grads(s, g, None, t, u, False)
    loop(2, ffn)
    st_mid_back(s, w, gain_ffn)
    for t in range(2):
        st_out_grads(s, g, None, t, False)
    attention_backward(s, w, g, None, 0, gain_attn, gtok, collections.defaultdict(lambda: lambda: None))
    st_restore(result)
    st_restore(gtok)
    gg[...] = s.gg[...]


def layer_call():
    vm = pl.BlockSpec(memory_space=pltpu.VMEM)
    return pl.pallas_call(
        layer_kernel,
        out_shape=(jax.ShapeDtypeStruct((T, D), BF), jax.ShapeDtypeStruct((T, D), BF),
                   jax.ShapeDtypeStruct((2, 4, 4, D // 16, COLS), BF), jax.ShapeDtypeStruct((8, D), F32)),
        in_specs=[vm] * 6, out_specs=(vm,) * 4,
        scratch_shapes=[pltpu.VMEM(*v) for v in SCRATCH.values()],
        compiler_params=pltpu.CompilerParams(vmem_limit_bytes=60 << 20),
    )


def last_kernel(res, gtok, grads, gains, result, grad_tokens, gain_a, gain_f, gq, gk, gv, go, gi, gd, hold, sems):
    parts = [(n, half) for half in range(res.shape[0]) for n in range(2)]
    ins = [pltpu.make_async_copy((res, gtok)[n].at[half], hold.at[n, half], sems.at[0, n, half]) for n, half in parts]
    outs = [pltpu.make_async_copy(hold.at[n, half], (result, grad_tokens)[n].at[half], sems.at[1, n, half]) for n, half in parts]
    for cp in ins:
        cp.start()
    width = gain_a.shape[1]
    gain_a[...] = gains[0:1, 0:width]
    gain_f[...] = gains[1:2, 0:width]
    for ref, val in zip((gq, gk, gv, go, gi, gd), split_cols(grads[...])):
        ref[...] = val
    for cp, out in zip(ins, outs):
        cp.wait()
        out.start()
    for out in outs:
        out.wait()


def last_call(res, gtok, grads, gains, width):
    vm, hbm = pl.BlockSpec(memory_space=pltpu.VMEM), pl.BlockSpec(memory_space=pl.ANY)
    square, long, row = (grads.shape[0], HALF), (grads.shape[0], FF // 2), (1, width)
    outs = [row, row, square, square, square, square, long, long]
    return pl.pallas_call(
        last_kernel,
        out_shape=(jax.ShapeDtypeStruct(res.shape, BF),) * 2 + tuple(jax.ShapeDtypeStruct(x, F32) for x in outs),
        in_specs=[hbm, hbm, vm, vm],
        out_specs=(hbm, hbm) + (vm,) * len(outs),
        scratch_shapes=[pltpu.VMEM((2,) + res.shape, BF), pltpu.SemaphoreType.DMA((2, 2, res.shape[0]))],
    )(res, gtok, grads, gains)


def split_cols(x):
    ins = jnp.concatenate([x[:, in_cols(u)] for u in range(2)], axis=1)
    downs = jnp.concatenate([x[:, down_cols(u)] for u in range(2)], axis=1)
    return x[:, QO:KO], x[:, KO:VO], x[:, VO:OO], x[:, OO:FO], ins, downs


def join_cols(q, k, v, o, i, d):
    parts = [q, k, v, o]
    for u in range(2):
        parts += [i[:, u * UNITS:(u + 1) * UNITS], d[:, u * UNITS:(u + 1) * UNITS]]
    return jnp.concatenate(parts, axis=1)


def by_collectives(tokens, gain_attn, gain_ffn, w_query, w_key, w_value, w_out, w_in, w_down, segment_ids, cotangent):
    tp = lax.axis_index("tp")
    tok = lax.all_to_all(tokens, "tp", 0, 0, tiled=True).reshape(T, D)
    cot = lax.all_to_all(cotangent, "tp", 0, 0, tiled=True).reshape(T, D)
    own = join_cols(w_query, w_key, w_value, w_out.T, w_in, w_down.T)
    half = lax.all_gather(own, "fsdp", axis=0, tiled=True)
    w = lax.all_gather(half, "tp", axis=0)
    seg = lax.dynamic_index_in_dim(segment_ids, tp, 0)
    res, gtok, g, gg = layer_call()(tok, cot, gain_attn[None], gain_ffn[None], w, seg)
    res = lax.all_to_all(res.reshape(tokens.shape), "tp", 0, 0, tiled=True)
    gtok = lax.all_to_all(gtok.reshape(tokens.shape), "tp", 0, 0, tiled=True)
    gsum = lax.psum_scatter(g.reshape(2, D, COLS).astype(F32), "tp", scatter_dimension=0)
    gsum = lax.psum_scatter(gsum, "fsdp", scatter_dimension=0, tiled=True)
    gains = lax.psum_scatter(gg, ("fsdp", "tp"), scatter_dimension=1, tiled=True)
    return finish(res, gtok, gsum, gains, gains.shape[1])


def finish(res, gtok, grads, gains, width):
    res, gtok, gain_a, gain_f, q, k, v, o, i, d = last_call(res, gtok, grads, gains, width)
    return res, gtok, gain_a.reshape(width), gain_f.reshape(width), q, k, v, o.T, i, d.T


PIECES = ((0, 512), (512, 1024), (1024, 2048), (2048, 3072))
GPIECES = ((1024, 2048), (2048, 3072), (768, 1024), (512, 768), (0, 512))
MESH = pl.DeviceIdType.MESH
ROWS = D // 16

EXCHANGE = dict(
    w=((2, D, COLS), BF), g=((2, 4, 4, ROWS, COLS), BF), other=((4, 4, ROWS, COLS), BF),
    rx=((3, 4, ROWS, COLS), BF), zs=((4, ROWS, COLS), BF), rz=((3, ROWS, COLS), BF),
    tok=((T, D), BF), cot=((T, D), BF), gr=((7, 8, D), F32), gs=((3, 8, D), F32),
)


def halves(lo, hi):
    mid = (lo + hi) // 2
    return slice(lo, mid), slice(mid, hi)


class Links:
    def __init__(self, e, sems):
        self.e = e
        self.sems = sems
        f, self.c = lax.axis_index("fsdp"), lax.axis_index("tp")
        self.zi, self.xy = f // 4, f % 4
        x, y = self.xy % 2, self.xy // 2
        self.f = f
        self.across = {"x": (1 - x) + 2 * y, "y": x + 2 * (1 - y), "d": (1 - x) + 2 * (1 - y)}
        self.arrival, self.sent = {}, []
        self.fixed = {}

    def z_at(self, dz):
        return (self.zi + dz) % 4

    def z_from(self, dz):
        return (self.zi + 4 - dz) % 4

    def greet(self):
        self.bar = pltpu.get_barrier_semaphore()
        for dev in ([(self.z_at(d) * 4 + self.xy, self.c) for d in (1, 2, 3)]
                    + [(self.zi * 4 + k, self.c) for k in self.across.values()] + [(self.f, 1 - self.c)]):
            pl.semaphore_signal(self.bar, inc=1, device_id=dev, device_id_type=MESH)

    def meet(self):
        pl.semaphore_wait(self.bar, 7)

    def w_rows(self, first, count, cols):
        return self.e.w.at[self.c, pl.ds(pl.multiple_of(first * ROWS, count * ROWS), count * ROWS), cols]

    def mine(self, k, cols):
        return self.e.g.at[self.c, :, self.across[k], :, cols]

    def route(self, kind, *key):
        e = self.e
        if kind in self.fixed:
            return self.fixed[kind][key[0]] + ("t",)
        if kind in ("z", "x", "y", "d", "xy", "yx", "t"):
            piece, d = key
            cols = slice(*PIECES[piece])
            first, second = halves(*PIECES[piece])
            if kind == "z":
                at, to = self.w_rows(self.f, 1, cols), d
            elif kind == "t":
                at, to = self.w_rows(self.z_from(d) * 4, 4, cols), "t"
            elif kind == "xy":
                at, to = self.w_rows(self.z_from(d) * 4 + self.across["x"], 1, first), "y"
            elif kind == "yx":
                at, to = self.w_rows(self.z_from(d) * 4 + self.across["y"], 1, second), "x"
            else:
                at, to = self.w_rows(self.z_from(d) * 4 + self.xy, 1, cols), kind
            return at, at, to
        if kind == "n":
            n = key[0]
            return e.gs.at[0 if n == 0 else 1 if n < 4 else 2], e.gr.at[n], "t" if n == 0 else "xyd"[n - 1] if n < 4 else n - 3
        piece = key[0]
        if kind == "gt":
            lo, hi = GPIECES[piece] if piece < 3 else (0, OO)
            return e.g.at[1 - self.c, :, :, :, lo:hi], e.other.at[:, :, :, lo:hi], "t"
        cols = slice(*GPIECES[piece])
        if kind == "gz":
            d = key[1]
            return e.zs.at[d, :, cols], e.rz.at[d - 1, :, cols], d
        to = kind[1]
        if len(key) > 1:
            cols = halves(*GPIECES[piece])[key[1]]
            if kind == "gd":
                to = "xy"[key[1]]
        return self.mine(kind[1], cols), e.rx.at["xyd".index(kind[1]), :, :, cols], to

    def copy(self, key):
        src, dst, to = self.route(*key)
        if isinstance(to, int):
            dev = (self.z_at(to) * 4 + self.xy, self.c)
        elif to == "t":
            dev = (self.f, 1 - self.c)
        else:
            dev = (self.zi * 4 + self.across[to], self.c)
        sent = self.sent.index(key) % NSEND if key in self.sent else 0
        return pltpu.make_async_remote_copy(
            src_ref=src, dst_ref=dst, send_sem=self.sems[0].at[sent],
            recv_sem=self.sems[1].at[self.arrival.setdefault(key, len(self.arrival))], device_id=dev, device_id_type=MESH)

    def send(self, *key):
        self.sent.append(key)
        if len(self.sent) > NSEND:
            self.copy(self.sent[-1 - NSEND]).wait_send()
        self.copy(key).start()

    def arrived(self, *key):
        self.copy(key).wait_recv()

    def finish(self):
        assert len(self.sent) == len(self.arrival) == NSEM, len(self.sent)
        for key in self.sent[-NSEND:]:
            self.copy(key).wait_send()

    def own_z(self, piece):
        for d in (1, 2, 3):
            self.send("z", piece, d)

    def own_plane(self, piece):
        self.to_plane(piece, 0)

    def to_plane(self, piece, d):
        for k in "xyd" if piece < 2 else "xy":
            self.send(k, piece, d)

    def plane(self, piece, d):
        self.arrived("z", piece, d)
        self.to_plane(piece, d)

    def corner(self, piece, d):
        self.arrived("x", piece, d)
        self.send("xy", piece, d)
        self.arrived("y", piece, d)
        self.send("yx", piece, d)

    def pair(self, piece, d):
        for k in ("x", "y", "d") if piece < 2 else ("xy", "yx"):
            self.arrived(k, piece, d)
        self.send("t", piece, d)

    def gathered(self, piece):
        for d in range(4):
            self.arrived("t", piece, d)

    def grads_pair(self, piece):
        self.send("gt", piece)

    def grads_plane(self, piece):
        for k in "xyd":
            self.send("g" + k, piece)

    def grads_part(self, piece):
        self.send("gd", piece, 0)
        self.send("gd", piece, 1)
        self.send("gx", piece, 0)
        self.send("gy", piece, 1)

    def grads_join(self, piece):
        first, second = halves(*GPIECES[piece])
        for n, k, cols in ((0, "y", first), (1, "x", second)):
            self.arrived("gd", piece, n)
            at = self.mine(k, cols)
            at[...] = (at[...].astype(F32) + self.e.rx[2, :, :, cols].astype(F32)).astype(BF)
            self.send("g" + k, piece, n)

    def grads_line(self, piece, direct):
        e = self.e
        cols = slice(*GPIECES[piece])
        if direct:
            for k in "xyd":
                self.arrived("g" + k, piece)
        else:
            for k in "xy":
                for n in range(2):
                    self.arrived("g" + k, piece, n)
        for d in (1, 2, 3, 0):
            z = self.z_at(d)
            total = e.g[self.c, z, self.xy, :, cols].astype(F32)
            for n in range(3 if direct else 2):
                total = total + e.rx[n, z, :, cols].astype(F32)
            if d:
                e.zs[d, :, cols] = total.astype(BF)
                self.send("gz", piece, d)
            else:
                self.out[:, cols] = total

    def grads_in(self, piece):
        cols = slice(*GPIECES[piece])
        for d in (1, 2, 3):
            self.arrived("gz", piece, d)
        total = self.out[:, cols]
        for d in range(3):
            total = total + self.e.rz[d, :, cols].astype(F32)
        self.out[:, cols] = total

    def gains_sum(self, step):
        e = self.e
        if step == 0:
            self.send("n", 0)
        if step == 1:
            self.arrived("n", 0)
            e.gs[1] = e.gs[0] + e.gr[0]
            for n in (1, 2, 3):
                self.send("n", n)
        if step == 2:
            for n in (1, 2, 3):
                self.arrived("n", n)
            e.gs[2] = e.gs[1] + e.gr[1] + e.gr[2] + e.gr[3]
            for n in (4, 5, 6):
                self.send("n", n)
        if step == 3:
            for n in (4, 5, 6):
                self.arrived("n", n)
            return e.gs[2] + e.gr[4] + e.gr[5] + e.gr[6]


NSEM = 135
NSEND = 24


def step_kernel(tokens, cotangent, gain_attn, gain_ffn, wq, wk, wv, wo, wi, wd, seg, result, gtok, gout, gains, *scr):
    ns, ne = len(SCRATCH), len(EXCHANGE)
    s = stage_names(scr[:ns])
    e = Names()
    for n, r in zip(EXCHANGE, scr[ns:ns + ne]):
        setattr(e, n, r)
    send_sem, recv_sem, local = scr[ns + ne:]
    link = Links(e, (send_sem, recv_sem))
    link.out = gout
    c, f, w, g = link.c, link.f, e.w, e.g
    half = T // 2
    mine = pl.ds(pl.multiple_of(c * half, half), half)
    theirs = pl.ds(pl.multiple_of((1 - c) * half, half), half)
    four, three = range(4), (1, 2, 3)

    link.fixed = {"in": [(tokens.at[1 - c], e.tok.at[mine, :]), (cotangent.at[1 - c], e.cot.at[mine, :])],
                  "out": [(e.cot.at[theirs, :], gtok.at[c]), (e.tok.at[theirs, :], result.at[c])]}
    loads = [pltpu.make_async_copy(tokens.at[c], e.tok.at[mine, :], local.at[0]),
             pltpu.make_async_copy(cotangent.at[c], e.cot.at[mine, :], local.at[1])]
    for cp in loads:
        cp.start()
    link.greet()
    w[c, pl.ds(pl.multiple_of(f * ROWS, ROWS), ROWS), :] = join_cols(wq[...], wk[...], wv[...], wo[...], wi[...], wd[...])
    link.meet()
    link.own_z(0)
    link.own_plane(0)
    link.send("in", 0)
    link.send("in", 1)
    link.own_z(1)
    link.own_plane(1)
    link.own_plane(2)
    loads[0].wait()
    link.arrived("in", 0)
    st_tokens(s, e.tok, gain_attn)
    loads[1].wait()
    link.arrived("in", 1)
    st_cot(s, e.cot)
    transpose_into(s.nmt, s.nm)
    for d in three:
        link.plane(0, d)
    link.own_z(2)
    transpose_into(s.cott, s.cotp)
    st_bias(s)
    for d in three:
        link.plane(1, d)
    for d in four:
        link.pair(0, d)
    link.own_z(3)
    link.gathered(0)
    st_query_key(s, w)
    link.plane(2, 1)
    link.plane(2, 2)

    def halfway():
        for d in four:
            link.pair(1, d)
        link.plane(2, 3)
        link.own_plane(3)
    st_sinkhorn(s, seg.at[pl.ds(c, 1), :], halfway)
    link.gathered(1)
    st_values(s, w)
    link.corner(2, 0)
    link.corner(2, 1)
    st_sort(s)
    link.plane(3, 1)
    link.corner(2, 2)
    link.corner(2, 3)
    st_attend(s, 0)
    link.plane(3, 2)
    link.plane(3, 3)
    link.pair(2, 0)
    link.pair(2, 1)
    st_attend(s, 1)
    link.pair(2, 2)
    link.pair(2, 3)
    link.corner(3, 0)
    link.corner(3, 1)
    st_out(s, w, gain_ffn)
    transpose_into(s.nft, s.nf)
    link.gathered(2)

    def ffn(u):
        early, late = u == 0, u == 1
        pl.when(late)(lambda: link.gathered(3))
        st_ffn(s, w, 1 - c, u, None)

        @pl.when(early)
        def _():
            link.corner(3, 2)
            link.corner(3, 3)
            link.pair(3, 0)
            link.pair(3, 1)
        st_ffn_grads(s, g, None, 1 - c, u, False)
        for n in range(2):
            pl.when(u == n)(functools.partial(link.grads_pair, n))
        st_ffn(s, w, c, u, e.tok)

        @pl.when(early)
        def _():
            link.pair(3, 2)
            link.pair(3, 3)
            link.arrived("gt", 0)

        @pl.when(late)
        def _():
            link.grads_join(0)
            link.arrived("gt", 1)
        st_ffn_grads(s, g, e.other, c, u, True)
        for n in range(2):
            pl.when(u == n)(functools.partial(link.grads_part, n))
    loop(2, ffn)
    st_mid_back(s, w, gain_ffn)
    st_out_grads(s, g, None, 1 - c, False)
    link.grads_pair(2)
    link.grads_line(0, False)
    link.arrived("gt", 2)
    st_out_grads(s, g, e.other, c, True)
    link.grads_plane(2)

    def attend0():
        link.grads_join(1)

    def first():
        link.grads_pair(3)
        link.grads_in(0)

    def sort1():
        link.arrived("gt", 3)
        link.grads_line(1, False)

    def values():
        link.grads_plane(3)
        link.grads_line(2, True)

    def last():
        link.grads_plane(4)

    attention_backward(s, w, g, e.other, c, gain_attn, e.cot, {
        "attend0": attend0, "first": first, "sort1": sort1, "values": values, "last": last})
    e.gs[0] = s.gg[...]
    link.gains_sum(0)
    stores = []
    for n, (buf, out) in enumerate(((e.cot, gtok), (e.tok, result))):
        st_restore(buf)
        stores.append(pltpu.make_async_copy(buf.at[mine, :], out.at[c], local.at[2 + n]))
        stores[n].start()
        link.send("out", n)
    link.grads_line(3, True)
    link.gains_sum(1)
    link.grads_in(1)
    link.grads_in(2)
    link.grads_line(4, True)
    link.gains_sum(2)
    link.grads_in(3)
    link.arrived("out", 0)
    link.arrived("out", 1)
    for cp in stores:
        cp.wait()
    total = link.gains_sum(3)
    width = D // 32
    pick = (iota((D, 128), 0) == iota((D, 128), 1) + (2 * f + c) * width).astype(F32)
    gains[...] = nn(total, pick, precision=HI)
    link.grads_in(4)
    link.finish()


def by_kernel(tokens, gain_attn, gain_ffn, w_query, w_key, w_value, w_out, w_in, w_down, segment_ids, cotangent):
    vm, hbm = pl.BlockSpec(memory_space=pltpu.VMEM), pl.BlockSpec(memory_space=pl.ANY)
    shapes = list(SCRATCH.values()) + list(EXCHANGE.values())
    res, gtok, grads, gains = pl.pallas_call(
        step_kernel,
        out_shape=(jax.ShapeDtypeStruct(tokens.shape, BF), jax.ShapeDtypeStruct(tokens.shape, BF),
                   jax.ShapeDtypeStruct((ROWS, COLS), F32), jax.ShapeDtypeStruct((8, 128), F32)),
        in_specs=[hbm] * 2 + [vm] * 9, out_specs=(hbm, hbm, vm, vm),
        scratch_shapes=[pltpu.VMEM(*v) for v in shapes] + [
            pltpu.SemaphoreType.DMA((NSEND,)), pltpu.SemaphoreType.DMA((NSEM,)), pltpu.SemaphoreType.DMA((4,))],
        compiler_params=pltpu.CompilerParams(collective_id=0, has_side_effects=True, vmem_limit_bytes=63 << 20),
    )(tokens, cotangent, gain_attn[None], gain_ffn[None], w_query, w_key, w_value, w_out.T, w_in, w_down.T, segment_ids)
    return finish(res, gtok, grads, gains, D // 32)


def solution(mesh):
    body = by_kernel if mesh.shape["fsdp"] == 16 else by_collectives
    return jax.shard_map(
        body,
        mesh=mesh,
        in_specs=(P(None, ("fsdp", "tp"), None), P(), P(), P("fsdp", "tp"), P("fsdp", "tp"), P("fsdp", "tp"),
                  P("tp", "fsdp"), P("fsdp", "tp"), P("tp", "fsdp"), P(None, "fsdp"), P(None, ("fsdp", "tp"), None)),
        out_specs=(P(None, ("fsdp", "tp"), None), P(None, ("fsdp", "tp"), None), P(("fsdp", "tp")), P(("fsdp", "tp")),
                   P("fsdp", "tp"), P("fsdp", "tp"), P("fsdp", "tp"), P("tp", "fsdp"), P("fsdp", "tp"), P("tp", "fsdp")),
        check_vma=False,
    )
```

```python
import collections
import functools
import math
import jax, jax.numpy as jnp
from jax import lax
from jax.experimental import pallas as pl
from jax.experimental.pallas import tpu as pltpu
from jax.sharding import PartitionSpec as P

F32, BF = jnp.float32, jnp.bfloat16
HI = lax.Precision.HIGHEST
HD, BLK, ITERS, NB, D, FF, T = 64, 32, 8, 32, 512, 2048, 1024
HALF = D // 2
COLS = 3 * HALF + HALF + FF
QO, VO, OO, FO = 0, 512, 768, 1024
UNITS = 512
STEPS = FF // 2 // UNITS


def in_cols(u):
    return slice(FO + 2 * u * UNITS, FO + (2 * u + 1) * UNITS)


def down_cols(u):
    return slice(FO + (2 * u + 1) * UNITS, FO + (2 * u + 2) * UNITS)


def span(start, count):
    return pl.ds(pl.multiple_of(start, 128), count)


def nn(a, b, precision=None):
    return lax.dot_general(a, b, (((1,), (0,)), ((), ())), precision=precision, preferred_element_type=F32)


def nt(a, b, precision=None):
    return lax.dot_general(a, b, (((1,), (1,)), ((), ())), precision=precision, preferred_element_type=F32)


def tn(a, b, precision=None):
    return lax.dot_general(a, b, (((0,), (0,)), ((), ())), precision=precision, preferred_element_type=F32)


def iota(shape, dim):
    return lax.broadcasted_iota(jnp.int32, shape, dim)


def order_matrix(inverse):
    n, m = iota((128, 128), 0), iota((128, 128), 1)
    if inverse:
        n, m = m, n
    return (m == (n & 3) * 32 + (n >> 2)).astype(BF)


def norm_rows(x, gain):
    center = x - jnp.mean(x, axis=1, keepdims=True)
    inv = lax.rsqrt(jnp.mean(center * center, axis=1, keepdims=True) + 1e-05)
    xhat = center * inv
    return xhat, inv


def norm_back(xhat, inv, gain, grad):
    gx = grad * gain
    m1 = jnp.mean(gx, axis=1, keepdims=True)
    m2 = jnp.mean(gx * xhat, axis=1, keepdims=True)
    return inv * (gx - m1 - xhat * m2)


def even_lanes(shape):
    return (iota(shape, len(shape) - 1) & 127) < 64


def stack_heads(x):
    ev = even_lanes(x.shape)
    z = jnp.zeros_like(x)
    return jnp.concatenate([jnp.where(ev, x, z), jnp.where(ev, z, x)], axis=0)


def pick_heads(r):
    n = r.shape[0] // 2
    ev = even_lanes((n, r.shape[1]))
    return jnp.where(ev, r[:n], r[n:])


SCRATCH = dict(
    tokp=((T, D), BF), cotp=((T, D), BF), cott=((D, T), BF), nm=((T, D), BF), nmt=((D, T), BF),
    q=((T, D), BF), k=((T, D), BF), v=((T, D), BF), ks=((T, D), BF), vs=((T, D), BF),
    qm=((NB, D), F32), km=((NB, D), F32), sk=((2 * ITERS, 8 * NB, NB), F32), allow=((NB, NB), F32),
    kr=((8, 128, 128), BF), krt=((8, 128, 128), BF), hidq=((256, 128), BF), hidk=((256, 128), BF),
    pr=((4, 8, 256, 256), BF), mix=((T, D), BF), mid=((T, D), F32), nf=((T, D), BF), nft=((D, T), BF),
    hid=((T, UNITS), BF), gp=((T, UNITS), BF), res=((T, D), F32), gnf=((T, D), F32),
    ga=((T, D), BF), gat=((D, T), BF), gmix=((T, D), BF), dv=((T, D), F32), ds=((8 * NB, NB), F32),
    gg=((8, D), F32),
)
SHARED = dict(dq="res", dk="gnf", dks="hid", dvs="gp", dqb="ga", dkb="nm", dvb="nf")


def loop(n, body, unroll=1):
    lax.fori_loop(0, n, lambda i, c: (body(i), c)[1], 0, unroll=unroll)


def rows(i, n):
    return pl.ds(pl.multiple_of(i * n, n), n)


def pipeline(units, stages, lags, after=None):
    vals = [{} for _ in units]
    for step in range(len(units) + lags[-1]):
        for st, lag in reversed(list(zip(stages, lags))):
            if 0 <= step - lag < len(units):
                st(units[step - lag], vals[step - lag])
        if after is not None:
            after(step)


def st_tokens(s, tok, gain_attn):
    pm = order_matrix(False)

    def body(c):
        def order(i, v):
            v["x"] = nn(pm, tok[rows(4 * c + i, 128), :])

        def norm(i, v):
            at = rows(4 * c + i, 128)
            x = v.pop("x")
            s.tokp[at, :] = x.astype(BF)
            xhat, _ = norm_rows(x, None)
            s.nm[at, :] = (xhat * gain_attn[...]).astype(BF)
        pipeline(range(4), (order, norm), (0, 1))
    loop(2, body)


def st_cot(s, cot):
    pm = order_matrix(False)

    def body(c):
        for i in range(4):
            at = rows(4 * c + i, 128)
            s.cotp[at, :] = nn(pm, cot[at, :]).astype(BF)
    loop(2, body)


def transpose_into(dst, src):
    for c in range(4):
        dst[:, c * 256:(c + 1) * 256] = jnp.transpose(src[c * 256:(c + 1) * 256, :], (1, 0))


def block_sums(x):
    y = jnp.sum(x.reshape(16, 8, x.shape[1]), axis=0)
    return y[0:4] + y[4:8]


def st_values(s, w):
    for m in range(4):
        x = s.nm[rows(m, 256), :]
        for t in range(2):
            s.v[rows(m, 256), t * 256:(t + 1) * 256] = nn(x, w[t, :, VO:VO + HALF]).astype(BF)


def st_query_key(s, w):
    def product(m, v):
        x = s.nm[rows(m, 256), :]
        v["x"] = [nn(x, w[t, :, 0:512]).astype(BF) for t in range(2)]

    def store(m, v):
        at = rows(m, 256)
        for t, out in enumerate(v.pop("x")):
            cs = slice(t * 256, (t + 1) * 256)
            queries = jnp.concatenate([out[:, 0:128], out[:, 256:384]], axis=1)
            keys = jnp.concatenate([out[:, 128:256], out[:, 384:512]], axis=1)
            qv, kv = queries.astype(F32), keys.astype(F32)
            s.q[at, cs] = (qv * (1.0 / math.sqrt(HD))).astype(BF)
            s.k[at, cs] = keys
            for ref, val in ((s.qm, qv), (s.km, kv)):
                sums = jnp.concatenate([block_sums(val[:128]), block_sums(val[128:])], axis=0)
                ref[rows(m, 8), cs] = sums * (1.0 / BLK)
    pipeline(range(4), (product, store), (0, 1))


def st_sinkhorn(s, seg, halfway=None):
    row = jnp.broadcast_to(seg[...], (NB, NB))
    ri, ci = iota((NB, NB), 0), iota((NB, NB), 1)
    col = jnp.sum(jnp.where(ri == ci, row, 0), axis=1, keepdims=True)
    allow = ((row == col) & (ci <= ri)) | ((row == 0) & (col > 0))
    s.allow[...] = allow.astype(F32)
    parts = []
    for p in range(4):
        cs = slice(p * 128, (p + 1) * 128)
        parts.append(nt(stack_heads(s.qm[:, cs]), s.km[:, cs], precision=HI))
    x = jnp.concatenate(parts, axis=0) * (BLK / math.sqrt(HD))
    mask = jnp.concatenate([allow.astype(F32)] * 8, axis=0) > 0
    x = jnp.where(mask, x, -1000000000.0)
    for it in range(ITERS):
        m = jnp.max(x, axis=1, keepdims=True)
        e = jnp.exp(x - m)
        z = jnp.sum(e, axis=1, keepdims=True)
        s.sk[2 * it] = e * (1.0 / z)
        x = x - (m + jnp.log(z))
        y = x.reshape(8, NB, NB)
        m = jnp.max(y, axis=1, keepdims=True)
        e = jnp.exp(y - m)
        z = jnp.sum(e, axis=1, keepdims=True)
        s.sk[2 * it + 1] = (e * (1.0 / z)).reshape(8 * NB, NB)
        x = (y - (m + jnp.log(z))).reshape(8 * NB, NB)
        if it == ITERS // 2 - 1 and halfway is not None:
            halfway()
    sorter = s.sk[2 * ITERS - 1].astype(BF)
    n = iota((128, NB), 0)
    e_mat = (((n >> 4) * 4 + (n & 3)) == iota((128, NB), 1)).astype(BF)
    wide = nt(sorter, e_mat).astype(BF)
    a, b = iota((128, 128), 0), iota((128, 128), 1)
    same = ((a >> 2) & 3) == ((b >> 2) & 3)
    for h in range(8):
        kr = jnp.where(same, nn(e_mat, wide[h * NB:(h + 1) * NB]), 0.0)
        s.kr[h] = kr.astype(BF)
        s.krt[h] = jnp.transpose(kr, (1, 0)).astype(BF)


def gather_chunk(ref, rq, cs):
    return jnp.concatenate([ref[pl.ds(pl.multiple_of(i * 128 + rq * 16, 16), 16), cs] for i in range(8)], axis=0)


def split_pair(x):
    return stack_heads(x)


def st_sort(s):
    def body(r):
        def mix(unit, v):
            rq, p = 2 * r + unit // 4, unit % 4
            cs = slice(p * 128, (p + 1) * 128)
            kv = jnp.concatenate([gather_chunk(s.k, rq, cs), gather_chunk(s.v, rq, cs)], axis=1)
            lhs = jnp.concatenate([s.kr[2 * p], s.kr[2 * p + 1]], axis=1)
            v["out"] = nn(lhs, split_pair(kv))

        def store(unit, v):
            rq, p = 2 * r + unit // 4, unit % 4
            cs = slice(p * 128, (p + 1) * 128)
            out = v.pop("out").astype(BF)
            for i in range(8):
                at = pl.ds(pl.multiple_of(i * 128 + rq * 16, 16), 16)
                s.ks[at, cs] = out[i * 16:(i + 1) * 16, 0:128]
                s.vs[at, cs] = out[i * 16:(i + 1) * 16, 128:256]
        pipeline(range(8), (mix, store), (0, 2))
    loop(4, body)


def st_bias(s):
    n, a = iota((256, 128), 0), iota((256, 128), 1)
    s.hidq[...] = ((a == (n & 3)) | (a == 4 + ((n & 127) >> 2))).astype(BF)
    other = (a < 4) & (a != (n & 3))
    later = (n < 128) & (a >= 4) & (a < 36) & ((n >> 2) > a - 4)
    s.hidk[...] = jnp.where(other | later, -1e30, 0.0).astype(BF)


def pick_rows(r):
    n = r.shape[1] // 2
    return jnp.concatenate([r[:64, :n], r[64:, n:]], axis=0)


def chunk_pair(c, i):
    p = i % 4
    c = c + i // 4
    return c, p, rows(c, 128), slice(p * 128, (p + 1) * 128)


def st_attend(s, b):
    def score(i, v):
        c, p, at, cs = chunk_pair(4 * b, i)
        qs = jnp.concatenate([stack_heads(s.q[at, cs]), s.hidq[...]], axis=1)
        kk = jnp.concatenate([jnp.concatenate([s.k[at, cs], s.ks[at, cs]], axis=0), s.hidk[...]], axis=1)
        v["x"] = nt(kk, qs)

    def soften(i, v):
        c, p, at, cs = chunk_pair(4 * b, i)
        x = v.pop("x")
        e = jnp.exp(x - jnp.max(x, axis=0, keepdims=True))
        v["p"] = (e * (1.0 / jnp.sum(e, axis=0, keepdims=True))).astype(BF)
        s.pr[p, c] = v["p"]

    def blend(i, v):
        c, p, at, cs = chunk_pair(4 * b, i)
        vv = jnp.concatenate([s.v[at, cs], s.vs[at, cs]], axis=0)
        v["o"] = pick_rows(nn(jnp.transpose(vv, (1, 0)), v.pop("p")))

    def store(i, v):
        c, p, at, cs = chunk_pair(4 * b, i)
        s.mix[at, cs] = jnp.transpose(v.pop("o"), (1, 0)).astype(BF)
    pipeline(range(16), (score, soften, blend, store), (0, 2, 4, 6))


def st_out(s, w, gain_ffn):
    def product(m, v):
        at = rows(m, 256)
        v["x"] = sum(nt(s.mix[at, t * 256:(t + 1) * 256], w[t, :, OO:OO + HALF]) for t in range(2))

    def norm(m, v):
        at = rows(m, 256)
        mid = s.tokp[at, :].astype(F32) + v.pop("x")
        s.mid[at, :] = mid
        s.res[at, :] = mid
        s.gnf[at, :] = jnp.zeros((256, D), F32)
        xhat, _ = norm_rows(mid, None)
        s.nf[at, :] = (xhat * gain_ffn[...]).astype(BF)
    pipeline(range(4), (product, norm), (0, 1))


def gelu_pair(x):
    k0, k1 = math.sqrt(2.0 / math.pi), 0.044715
    x2 = x * x
    half = 0.5 + 0.5 * jnp.tanh(x * (k0 + (k0 * k1) * x2))
    val = x * half
    der = half + (val - val * half) * (2 * k0 + (6 * k0 * k1) * x2)
    return val, der


def add_grads(g, other, t, own, cols, val):
    if own:
        val = val + other[:, :, :, cols].reshape(D, val.shape[1]).astype(F32)
    g[t, :, :, :, cols] = val.astype(BF).reshape(4, 4, D // 16, val.shape[1])


def st_ffn(s, w, t, u, out):
    ic, dc = span(FO + 2 * u * UNITS, UNITS), span(FO + (2 * u + 1) * UNITS, UNITS)

    def into(m, v):
        at = rows(m, 256)
        v["x"] = nn(s.nf[at, :], w[t, :, ic])
        v["g"] = nn(s.cotp[at, :], w[t, :, dc])

    def bend(m, v):
        at = rows(m, 256)
        val, der = gelu_pair(v.pop("x"))
        v["h"] = val.astype(BF)
        v["g"] = (v["g"] * der).astype(BF)
        s.hid[at, :] = v["h"]
        s.gp[at, :] = v["g"]

    def back(m, v):
        at = rows(m, 256)
        add = nt(v.pop("h"), w[t, :, dc])
        add = s.res[at, :] + add
        s.res[at, :] = add
        if out is not None:
            out[at, :] = add.astype(BF)
        add = nt(v.pop("g"), w[t, :, ic])
        s.gnf[at, :] = s.gnf[at, :] + add
    pipeline(range(4), (into, bend, back), (0, 2, 3))


def st_ffn_grads(s, g, other, t, u, own):
    add_grads(g, other, t, own, span(FO + 2 * u * UNITS, UNITS), nn(s.nft[...], s.gp[...]))
    add_grads(g, other, t, own, span(FO + (2 * u + 1) * UNITS, UNITS), nn(s.cott[...], s.hid[...]))


def st_mid_back(s, w, gain_ffn):
    parts = []

    def norm(m, v):
        at = rows(m, 256)
        xhat, inv = norm_rows(s.mid[at, :], None)
        gnf = s.gnf[at, :]
        parts.append(jnp.sum((gnf * xhat).reshape(32, 8, D), axis=0))
        gm = s.cotp[at, :].astype(F32) + norm_back(xhat, inv, gain_ffn[...], gnf)
        s.mid[at, :] = gm
        v["ga"] = gm.astype(BF)
        s.ga[at, :] = v["ga"]

    def product(m, v):
        at = rows(m, 256)
        ga = v.pop("ga")
        for t in range(2):
            s.gmix[at, t * 256:(t + 1) * 256] = nn(ga, w[t, :, OO:OO + HALF]).astype(BF)
        s.gat[:, m * 256:(m + 1) * 256] = jnp.transpose(ga, (1, 0))
    pipeline(range(4), (norm, product), (0, 1))
    s.gg[1:2, :] = jnp.sum(sum(parts), axis=0, keepdims=True)


def half_cols(t):
    return pl.ds(pl.multiple_of(t * HALF, HALF), HALF)


def st_out_grads(s, g, other, t, own):
    add_grads(g, other, t, own, slice(OO, OO + HALF), nn(s.gat[...], s.mix[:, half_cols(t)]))


def st_restore(src):
    pm = order_matrix(True)
    for c in range(8):
        at = slice(c * 128, (c + 1) * 128)
        src[at, :] = nn(pm, src[at, :]).astype(BF)


def pair_cols(t, j):
    return pl.ds(pl.multiple_of(t * HALF + j * 128, 128), 128)


def st_attend_back(s, t, pairs, after=None):
    scale = 1.0 / math.sqrt(HD)

    def place(i):
        c, j = i // len(pairs), pairs[i % len(pairs)]
        return c, 2 * t + j, slice(c * 128, (c + 1) * 128), pair_cols(t, j)

    def grad_probs(i, v):
        c, p, at, cs = place(i)
        g = s.gmix[at, cs]
        go = (g.astype(F32) * s.mix[at, cs].astype(F32)).astype(BF)
        vv = jnp.concatenate([s.v[at, cs], s.vs[at, cs]], axis=0)
        v["dp"] = nt(jnp.concatenate([vv, jnp.full_like(vv, -1.0)], axis=1),
                     jnp.concatenate([stack_heads(g), stack_heads(go)], axis=1))

    def grad_scores(i, v):
        c, p, at, cs = place(i)
        v["ds"] = (s.pr[p, c].astype(F32) * v.pop("dp")).astype(BF)

    def products(i, v):
        c, p, at, cs = place(i)
        ds = v.pop("ds")
        dkk = nn(ds, stack_heads(s.q[at, cs]))
        dvv = nn(s.pr[p, c], stack_heads(s.gmix[at, cs]))
        s.dk[at, cs] = dkk[:128]
        s.dks[at, cs] = dkk[128:].astype(BF)
        s.dv[at, cs] = dvv[:128]
        s.dvs[at, cs] = dvv[128:].astype(BF)
        kk = jnp.concatenate([s.k[at, cs], s.ks[at, cs]], axis=0)
        v["dq"] = pick_rows(nn(jnp.transpose(kk, (1, 0)), ds))

    def store(i, v):
        c, p, at, cs = place(i)
        s.dq[at, cs] = jnp.transpose(v.pop("dq"), (1, 0)) * scale
    pipeline(range(8 * len(pairs)), (grad_probs, grad_scores, products, store), (0, 2, 4, 6), after)


def heads_at(t, pairs):
    n = 2 * NB
    return pl.ds(pl.multiple_of(t * 2 * n + pairs[0] * n, n), n * len(pairs))


def st_sort_back(s, t, pairs):
    a, b = iota((128, 128), 0), iota((128, 128), 1)
    same = ((a >> 2) & 3) == ((b >> 2) & 3)
    accs = {j: [] for j in pairs}

    def mix(i, v):
        j, rq = pairs[i // 8], i % 8
        cs = pair_cols(t, j)
        kv = jnp.concatenate([gather_chunk(s.k, rq, cs), gather_chunk(s.v, rq, cs)], axis=1)
        st = split_pair(jnp.concatenate([gather_chunk(s.dks, rq, cs), gather_chunk(s.dvs, rq, cs)], axis=1))
        accs[j].append(nt(st, kv))
        h = 4 * t + 2 * j
        v["out"] = nn(jnp.concatenate([s.krt[h], s.krt[h + 1]], axis=1), st)

    def store(i, v):
        j, rq = pairs[i // 8], i % 8
        cs = pair_cols(t, j)
        out = v.pop("out")
        for n in range(8):
            at = slice(n * 128 + rq * 16, n * 128 + rq * 16 + 16)
            s.dk[at, cs] = s.dk[at, cs] + out[n * 16:(n + 1) * 16, 0:128]
            s.dvb[at, cs] = (s.dv[at, cs] + out[n * 16:(n + 1) * 16, 128:256]).astype(BF)
    pipeline(range(8 * len(pairs)), (mix, store), (0, 2))

    def fold():
        heads = 2 * len(pairs)
        x = jnp.concatenate([sum(accs[j]) for j in pairs], axis=0)
        x = jnp.where(jnp.concatenate([same] * heads, axis=0), x, 0.0)
        n = iota((128, NB), 0)
        cols_of = (((n >> 4) * 4 + (n & 3)) == iota((128, NB), 1)).astype(BF)
        m, n = iota((heads * NB, heads * 128), 0), iota((heads * NB, heads * 128), 1)
        rows_of = ((m >> 5) == (n >> 7)) & ((m & 31) == ((n >> 4) & 7) * 4 + (n & 3))
        high, low = two_terms(x)
        high, low = two_terms(nn(high, cols_of) + nn(low, cols_of))
        rows_of = rows_of.astype(BF)
        s.ds[heads_at(t, pairs), :] = nn(rows_of, high) + nn(rows_of, low)
    return fold


def two_terms(x):
    high = x.astype(BF)
    return high, (x - high.astype(F32)).astype(BF)


def sinkhorn_back(s, t, pairs):
    hs, n = heads_at(t, pairs), 2 * len(pairs)
    v = {}

    def sweep(it):
        x = v["x"] if it < ITERS - 1 else s.ds[hs, :] * s.sk[2 * ITERS - 1, hs, :]
        y = x.reshape(n, NB, NB)
        pk = s.sk[2 * it + 1, hs, :].reshape(n, NB, NB)
        x = (y - pk * jnp.sum(y, axis=1, keepdims=True)).reshape(n * NB, NB)
        v["x"] = x - s.sk[2 * it, hs, :] * jnp.sum(x, axis=1, keepdims=True)

    def means():
        mask = jnp.concatenate([s.allow[...]] * n, axis=0) > 0
        x = jnp.where(mask, v.pop("x"), 0.0) * (1.0 / math.sqrt(HD))
        for h, j in enumerate(pairs):
            cs = pair_cols(t, j)
            x0, x1 = x[2 * h * NB:(2 * h + 1) * NB], x[(2 * h + 1) * NB:(2 * h + 2) * NB]
            ev = even_lanes((NB, 128))
            km, qm = s.km[:, cs], s.qm[:, cs]
            v[j] = (jnp.where(ev, nn(x0, km, precision=HI), nn(x1, km, precision=HI)),
                    jnp.where(ev, tn(x0, qm, precision=HI), tn(x1, qm, precision=HI)))

    def spread(j):
        cs = pair_cols(t, j)
        dqm, dkm = v.pop(j)
        for c in range(8):
            at = slice(c * 128, (c + 1) * 128)
            for src, ref, dst in ((dqm, s.dq, s.dqb), (dkm, s.dk, s.dkb)):
                four = src[c * 4:(c + 1) * 4]
                eight = jnp.concatenate([four, four], axis=0)
                val = ref[at, cs].reshape(16, 8, 128) + eight[None]
                dst[at, cs] = val.reshape(128, 128).astype(BF)
    steps = [functools.partial(sweep, it) for it in reversed(range(ITERS))]
    return steps + [means] + [functools.partial(spread, j) for j in pairs]


def st_value_grads(s, g, other, t, own, part):
    val = nn(s.nmt[part * 256:(part + 1) * 256, :], s.dvb[:, half_cols(t)])
    if own:
        val = val + other[2 * part:2 * part + 2, :, :, VO:OO].reshape(256, HALF).astype(F32)
    g[t, 2 * part:2 * part + 2, :, :, VO:OO] = val.astype(BF).reshape(2, 4, D // 16, HALF)


def st_query_key_grads(s, g, other, t, own, pairs):
    for j in pairs:
        cs = pair_cols(t, j)
        add_grads(g, other, t, own, slice(j * 256, (j + 1) * 256),
                  nn(s.nmt[...], jnp.concatenate([s.dqb[:, cs], s.dkb[:, cs]], axis=1)))


def st_tokens_back(s, w, gain_attn, out):
    parts = []

    def product(m, v):
        at = rows(m, 256)
        v["g"] = 0.0
        for t in range(2):
            cs = slice(t * 256, (t + 1) * 256)
            dq, dk = s.dqb[at, cs], s.dkb[at, cs]
            lhs = jnp.concatenate([dq[:, :128], dk[:, :128], dq[:, 128:], dk[:, 128:], s.dvb[at, cs]], axis=1)
            v["g"] = v["g"] + nt(lhs, w[t, :, 0:OO])

    def norm(m, v):
        at = rows(m, 256)
        gn = v.pop("g")
        xhat, inv = norm_rows(s.tokp[at, :].astype(F32), None)
        parts.append(jnp.sum((gn * xhat).reshape(32, 8, D), axis=0))
        out[at, :] = (s.mid[at, :] + norm_back(xhat, inv, gain_attn[...], gn)).astype(BF)
    pipeline(range(4), (product, norm), (0, 1))
    s.gg[0:1, :] = jnp.sum(sum(parts), axis=0, keepdims=True)


def attention_backward(s, w, g, other, c, gain_attn, out, hooks):
    own, both = other is not None, (0, 1)

    def with_steps(steps):
        return lambda n: steps[n]() if n < len(steps) else None
    st_attend_back(s, 1 - c, both)
    hooks["attend0"]()
    fold = st_sort_back(s, 1 - c, both)
    hooks["sort0"]()
    st_attend_back(s, c, (0,), with_steps([fold] + sinkhorn_back(s, 1 - c, both)))
    for part in range(2):
        st_value_grads(s, g, None, 1 - c, False, part)
    st_query_key_grads(s, g, None, 1 - c, False, both)
    hooks["first"]()
    fold = st_sort_back(s, c, (0,))
    st_attend_back(s, c, (1,), with_steps([fold] + sinkhorn_back(s, c, (0,))))
    hooks["pair"]()
    st_query_key_grads(s, g, other, c, own, (0,))
    hooks["queries"]()
    steps = [st_sort_back(s, c, (1,))] + sinkhorn_back(s, c, (1,))
    for n, step in enumerate(steps):
        step()
        if n in (0, 2):
            st_value_grads(s, g, other, c, own, n // 2)
        if n == 3:
            hooks["values"]()
    st_query_key_grads(s, g, other, c, own, (1,))
    hooks["last"]()
    st_tokens_back(s, w, gain_attn, out)


class Names:
    pass


def stage_names(refs):
    s = Names()
    for n, r in zip(SCRATCH, refs):
        setattr(s, n, r)
    for n, o in SHARED.items():
        setattr(s, n, getattr(s, o))
    return s


def layer_kernel(tok, cot, gain_attn, gain_ffn, w, seg, result, gtok, g, gg, *scr):
    s = stage_names(scr)
    st_tokens(s, tok, gain_attn)
    st_cot(s, cot)
    transpose_into(s.cott, s.cotp)
    transpose_into(s.nmt, s.nm)
    st_bias(s)
    st_query_key(s, w)
    st_sinkhorn(s, seg)
    st_values(s, w)
    st_sort(s)
    loop(2, functools.partial(st_attend, s))
    st_out(s, w, gain_ffn)
    transpose_into(s.nft, s.nf)
    def ffn(u):
        for t in range(2):
            st_ffn(s, w, t, u, result if t == 1 else None)
            st_ffn_grads(s, g, None, t, u, False)
    loop(2, ffn)
    st_mid_back(s, w, gain_ffn)
    for t in range(2):
        st_out_grads(s, g, None, t, False)
    attention_backward(s, w, g, None, 0, gain_attn, gtok, collections.defaultdict(lambda: lambda: None))
    st_restore(result)
    st_restore(gtok)
    gg[...] = s.gg[...]


def layer_call():
    vm = pl.BlockSpec(memory_space=pltpu.VMEM)
    return pl.pallas_call(
        layer_kernel,
        out_shape=(jax.ShapeDtypeStruct((T, D), BF), jax.ShapeDtypeStruct((T, D), BF),
                   jax.ShapeDtypeStruct((2, 4, 4, D // 16, COLS), BF), jax.ShapeDtypeStruct((8, D), F32)),
        in_specs=[vm] * 6, out_specs=(vm,) * 4,
        scratch_shapes=[pltpu.VMEM(*v) for v in SCRATCH.values()],
        compiler_params=pltpu.CompilerParams(vmem_limit_bytes=60 << 20),
    )


def last_kernel(res, gtok, grads, gains, result, grad_tokens, gain_a, gain_f, gq, gk, gv, go, gi, gd, hold, held, sems):
    sem = iter(range(sems.shape[0]))

    def copy(src, dst):
        return pltpu.make_async_copy(src, dst, sems.at[next(sem)])
    moves = [(copy(grads, held), [copy(held.at[:, cols], ref.at[:, at]) for cols, ref, at in places(gq, gk, gv, go, gi, gd)])]
    for half in range(res.shape[0]):
        for n, (src, dst) in enumerate(((res, result), (gtok, grad_tokens))):
            moves.append((copy(src.at[half], hold.at[n, half]), [copy(hold.at[n, half], dst.at[half])]))
    for cp, _ in moves:
        cp.start()
    width = gain_a.shape[1]
    gain_a[...] = gains[0:1, 0:width]
    gain_f[...] = gains[1:2, 0:width]
    for cp, outs in moves:
        cp.wait()
        for out in outs:
            out.start()
    for _, outs in moves:
        for out in outs:
            out.wait()


def places(gq, gk, gv, go, gi, gd):
    runs = [(slice(VO, OO), gv, slice(0, HALF)), (slice(OO, FO), go, slice(0, HALF))]
    for j in range(2):
        at = slice(j * 128, (j + 1) * 128)
        runs += [(slice(j * 256, j * 256 + 128), gq, at), (slice(j * 256 + 128, (j + 1) * 256), gk, at)]
    for u in range(STEPS):
        at = slice(u * UNITS, (u + 1) * UNITS)
        runs += [(in_cols(u), gi, at), (down_cols(u), gd, at)]
    return runs


def last_call(res, gtok, grads, gains, width):
    vm, hbm = pl.BlockSpec(memory_space=pltpu.VMEM), pl.BlockSpec(memory_space=pl.ANY)
    square, long, row = (grads.shape[0], HALF), (grads.shape[0], FF // 2), (1, width)
    outs = [row, row, square, square, square, square, long, long]
    return pl.pallas_call(
        last_kernel,
        out_shape=(jax.ShapeDtypeStruct(res.shape, BF),) * 2 + tuple(jax.ShapeDtypeStruct(x, F32) for x in outs),
        in_specs=[hbm, hbm, hbm, vm],
        out_specs=(hbm, hbm, vm, vm) + (hbm,) * 6,
        scratch_shapes=[pltpu.VMEM((2,) + res.shape, BF), pltpu.VMEM(grads.shape, F32),
                        pltpu.SemaphoreType.DMA((7 + 4 * res.shape[0] + 2 * STEPS,))],
    )(res, gtok, grads, gains)


def join_cols(q, k, v, o, i, d):
    parts = []
    for j in range(2):
        parts += [q[:, j * 128:(j + 1) * 128], k[:, j * 128:(j + 1) * 128]]
    parts += [v, o]
    for u in range(STEPS):
        parts += [i[:, u * UNITS:(u + 1) * UNITS], d[:, u * UNITS:(u + 1) * UNITS]]
    return jnp.concatenate(parts, axis=1)


def by_collectives(tokens, gain_attn, gain_ffn, w_query, w_key, w_value, w_out, w_in, w_down, segment_ids, cotangent):
    tp = lax.axis_index("tp")
    tok = lax.all_to_all(tokens, "tp", 0, 0, tiled=True).reshape(T, D)
    cot = lax.all_to_all(cotangent, "tp", 0, 0, tiled=True).reshape(T, D)
    own = join_cols(w_query, w_key, w_value, w_out.T, w_in, w_down.T)
    half = lax.all_gather(own, "fsdp", axis=0, tiled=True)
    w = lax.all_gather(half, "tp", axis=0)
    seg = lax.dynamic_index_in_dim(segment_ids, tp, 0)
    res, gtok, g, gg = layer_call()(tok, cot, gain_attn[None], gain_ffn[None], w, seg)
    res = lax.all_to_all(res.reshape(tokens.shape), "tp", 0, 0, tiled=True)
    gtok = lax.all_to_all(gtok.reshape(tokens.shape), "tp", 0, 0, tiled=True)
    gsum = lax.psum_scatter(g.reshape(2, D, COLS).astype(F32), "tp", scatter_dimension=0)
    gsum = lax.psum_scatter(gsum, "fsdp", scatter_dimension=0, tiled=True)
    gains = lax.psum_scatter(gg, ("fsdp", "tp"), scatter_dimension=1, tiled=True)
    return finish(res, gtok, gsum, gains, gains.shape[1])


def finish(res, gtok, grads, gains, width):
    res, gtok, gain_a, gain_f, q, k, v, o, i, d = last_call(res, gtok, grads, gains, width)
    return res, gtok, gain_a.reshape(width), gain_f.reshape(width), q, k, v, o.T, i, d.T


PIECES = ((0, 512), (512, 768), (768, 1024), (1024, 2048), (2048, 3072))
GPIECES = ((1024, 2048), (2048, 3072), (768, 1024), (512, 768), (0, 256), (256, 512))
MESH = pl.DeviceIdType.MESH
ROWS = D // 16

EXCHANGE = dict(
    w=((2, D, COLS), BF), g=((2, 4, 4, ROWS, COLS), BF), other=((4, 4, ROWS, COLS), BF),
    rx=((3, 4, ROWS, COLS), BF), zs=((4, ROWS, COLS), BF), rz=((3, ROWS, COLS), BF),
    tok=((T, D), BF), cot=((T, D), BF), gr=((7, 8, D), F32), gs=((3, 8, D), F32),
)


def halves(lo, hi):
    mid = (lo + hi) // 2
    return slice(lo, mid), slice(mid, hi)


class Links:
    def __init__(self, e, sems):
        self.e = e
        self.sems = sems
        f, self.c = lax.axis_index("fsdp"), lax.axis_index("tp")
        self.zi, self.xy = f // 4, f % 4
        x, y = self.xy % 2, self.xy // 2
        self.f = f
        self.across = {"x": (1 - x) + 2 * y, "y": x + 2 * (1 - y), "d": (1 - x) + 2 * (1 - y)}
        self.arrival, self.sent = {}, []
        self.fixed = {}

    def z_at(self, dz):
        return (self.zi + dz) % 4

    def z_from(self, dz):
        return (self.zi + 4 - dz) % 4

    def greet(self):
        self.bar = pltpu.get_barrier_semaphore()
        for dev in ([(self.z_at(d) * 4 + self.xy, self.c) for d in (1, 2, 3)]
                    + [(self.zi * 4 + k, self.c) for k in self.across.values()] + [(self.f, 1 - self.c)]):
            pl.semaphore_signal(self.bar, inc=1, device_id=dev, device_id_type=MESH)

    def meet(self):
        pl.semaphore_wait(self.bar, 7)

    def w_rows(self, first, count, cols):
        return self.e.w.at[self.c, pl.ds(pl.multiple_of(first * ROWS, count * ROWS), count * ROWS), cols]

    def mine(self, k, cols):
        return self.e.g.at[self.c, :, self.across[k], :, cols]

    def route(self, kind, *key):
        e = self.e
        if kind in self.fixed:
            return self.fixed[kind][key[0]] + ("t",)
        if kind in ("z", "zz", "x", "y", "d", "xy", "yx", "t"):
            piece, d = key
            cols = slice(*PIECES[piece])
            first, second = halves(*PIECES[piece])
            if kind == "z":
                at, to = self.w_rows(self.f, 1, cols), d
            elif kind == "zz":
                at, to = self.w_rows(self.zi * 4, 4, cols), d
            elif kind == "t":
                at, to = self.w_rows(self.z_from(d) * 4, 4, cols), "t"
            elif kind == "xy":
                at, to = self.w_rows(self.z_from(d) * 4 + self.across["x"], 1, first), "y"
            elif kind == "yx":
                at, to = self.w_rows(self.z_from(d) * 4 + self.across["y"], 1, second), "x"
            else:
                at, to = self.w_rows(self.z_from(d) * 4 + self.xy, 1, cols), kind
            return at, at, to
        if kind == "n":
            n = key[0]
            return e.gs.at[0 if n == 0 else 1 if n < 4 else 2], e.gr.at[n], "t" if n == 0 else "xyd"[n - 1] if n < 4 else n - 3
        piece = key[0]
        if kind == "gt":
            lo, hi = GPIECES[piece] if piece < 3 else (0, OO)
            return e.g.at[1 - self.c, :, :, :, lo:hi], e.other.at[:, :, :, lo:hi], "t"
        cols = slice(*GPIECES[piece])
        if kind == "gz":
            d = key[1]
            return e.zs.at[d, :, cols], e.rz.at[d - 1, :, cols], d
        to = kind[1]
        if len(key) > 1:
            cols = halves(*GPIECES[piece])[key[1]]
            if kind == "gd":
                to = "xy"[key[1]]
        return self.mine(kind[1], cols), e.rx.at["xyd".index(kind[1]), :, :, cols], to

    def copy(self, key):
        src, dst, to = self.route(*key)
        if isinstance(to, int):
            dev = (self.z_at(to) * 4 + self.xy, self.c)
        elif to == "t":
            dev = (self.f, 1 - self.c)
        else:
            dev = (self.zi * 4 + self.across[to], self.c)
        sent = self.sent.index(key) % NSEND if key in self.sent else 0
        return pltpu.make_async_remote_copy(
            src_ref=src, dst_ref=dst, send_sem=self.sems[0].at[sent],
            recv_sem=self.sems[1].at[self.arrival.setdefault(key, len(self.arrival))], device_id=dev, device_id_type=MESH)

    def send(self, *key):
        self.sent.append(key)
        if len(self.sent) > NSEND:
            self.copy(self.sent[-1 - NSEND]).wait_send()
        self.copy(key).start()

    def arrived(self, *key):
        self.copy(key).wait_recv()

    def finish(self):
        assert len(self.sent) == len(self.arrival) == NSEM, len(self.sent)
        for key in self.sent[-NSEND:]:
            self.copy(key).wait_send()

    def own_z(self, piece):
        for d in (1, 2, 3):
            self.send("z", piece, d)

    def own_plane(self, piece):
        self.to_plane(piece, 0)

    def to_plane(self, piece, d):
        for k in "xyd" if piece < 3 else "xy":
            self.send(k, piece, d)

    def plane(self, piece, d):
        self.arrived("z", piece, d)
        self.to_plane(piece, d)

    def corner(self, piece, d):
        self.arrived("x", piece, d)
        self.send("xy", piece, d)
        self.arrived("y", piece, d)
        self.send("yx", piece, d)

    def pair(self, piece, d):
        for k in ("x", "y", "d") if piece < 2 else ("xy", "yx"):
            self.arrived(k, piece, d)
        self.send("t", piece, d)

    def turn(self, piece):
        for k in "xyd":
            self.arrived(k, piece, 0)
        for d in (1, 2, 3):
            self.send("zz", piece, d)
        self.send("t", piece, 0)

    def turned(self, piece):
        for d in (1, 2, 3):
            self.arrived("zz", piece, d)
            self.send("t", piece, d)

    def gathered(self, piece):
        for d in range(4):
            self.arrived("t", piece, d)

    def grads_pair(self, piece):
        self.send("gt", piece)

    def grads_plane(self, piece):
        for k in "xyd":
            self.send("g" + k, piece)

    def grads_part(self, piece):
        self.send("gd", piece, 0)
        self.send("gd", piece, 1)
        self.send("gx", piece, 0)
        self.send("gy", piece, 1)

    def grads_join(self, piece):
        first, second = halves(*GPIECES[piece])
        for n, k, cols in ((0, "y", first), (1, "x", second)):
            self.arrived("gd", piece, n)
            at = self.mine(k, cols)
            at[...] = (at[...].astype(F32) + self.e.rx[2, :, :, cols].astype(F32)).astype(BF)
            self.send("g" + k, piece, n)

    def grads_line(self, piece, direct):
        e = self.e
        cols = slice(*GPIECES[piece])
        if direct:
            for k in "xyd":
                self.arrived("g" + k, piece)
        else:
            for k in "xy":
                for n in range(2):
                    self.arrived("g" + k, piece, n)
        for d in (1, 2, 3, 0):
            z = self.z_at(d)
            total = e.g[self.c, z, self.xy, :, cols].astype(F32)
            for n in range(3 if direct else 2):
                total = total + e.rx[n, z, :, cols].astype(F32)
            if d:
                e.zs[d, :, cols] = total.astype(BF)
                self.send("gz", piece, d)
            else:
                self.out[:, cols] = total

    def grads_in(self, piece):
        cols = slice(*GPIECES[piece])
        for n in range(3):
            self.arrived("gz", piece, n + 1)
        total = self.out[:, cols]
        for n in range(3):
            total = total + self.e.rz[n, :, cols].astype(F32)
        self.out[:, cols] = total

    def gains_sum(self, step):
        e = self.e
        if step == 0:
            self.send("n", 0)
        if step == 1:
            self.arrived("n", 0)
            e.gs[1] = e.gs[0] + e.gr[0]
            for n in (1, 2, 3):
                self.send("n", n)
        if step == 2:
            for n in (1, 2, 3):
                self.arrived("n", n)
            e.gs[2] = e.gs[1] + e.gr[1] + e.gr[2] + e.gr[3]
            for n in (4, 5, 6):
                self.send("n", n)
        if step == 3:
            for n in (4, 5, 6):
                self.arrived("n", n)
            return e.gs[2] + e.gr[4] + e.gr[5] + e.gr[6]


NSEM = 151
NSEND = 24


def step_kernel(tokens, cotangent, gain_attn, gain_ffn, wq, wk, wv, wo, wi, wd, seg, result, gtok, gout, gains, *scr):
    ns, ne = len(SCRATCH), len(EXCHANGE)
    s = stage_names(scr[:ns])
    e = Names()
    for n, r in zip(EXCHANGE, scr[ns:ns + ne]):
        setattr(e, n, r)
    send_sem, recv_sem, local = scr[ns + ne:]
    link = Links(e, (send_sem, recv_sem))
    link.out = gout
    c, f, w, g = link.c, link.f, e.w, e.g
    half = T // 2
    mine = pl.ds(pl.multiple_of(c * half, half), half)
    theirs = pl.ds(pl.multiple_of((1 - c) * half, half), half)
    four, three = range(4), (1, 2, 3)

    link.fixed = {"in": [(tokens.at[1 - c], e.tok.at[mine, :]), (cotangent.at[1 - c], e.cot.at[mine, :])],
                  "out": [(e.cot.at[theirs, :], gtok.at[c]), (e.tok.at[theirs, :], result.at[c])]}
    loads = [pltpu.make_async_copy(tokens.at[c], e.tok.at[mine, :], local.at[0]),
             pltpu.make_async_copy(cotangent.at[c], e.cot.at[mine, :], local.at[1])]
    for cp in loads:
        cp.start()
    link.greet()
    w[c, pl.ds(pl.multiple_of(f * ROWS, ROWS), ROWS), :] = join_cols(wq[...], wk[...], wv[...], wo[...], wi[...], wd[...])
    link.meet()
    link.own_z(0)
    link.own_plane(0)
    link.send("in", 0)
    link.send("in", 1)
    link.own_z(1)
    link.own_plane(1)
    link.own_plane(2)
    loads[0].wait()
    link.arrived("in", 0)
    st_tokens(s, e.tok, gain_attn)
    loads[1].wait()
    link.arrived("in", 1)
    st_cot(s, e.cot)
    transpose_into(s.nmt, s.nm)
    for d in three:
        link.plane(0, d)
    link.own_z(3)
    transpose_into(s.cott, s.cotp)
    st_bias(s)
    for d in three:
        link.plane(1, d)
    link.own_plane(3)
    link.turn(2)
    for d in four:
        link.pair(0, d)
    link.own_z(4)
    link.gathered(0)
    st_query_key(s, w)
    link.plane(3, 1)
    link.plane(3, 2)

    def halfway():
        for d in four:
            link.pair(1, d)
        link.plane(3, 3)
        link.own_plane(4)
    st_sinkhorn(s, seg.at[pl.ds(c, 1), :], halfway)
    link.gathered(1)
    st_values(s, w)
    link.corner(3, 0)
    link.corner(3, 1)
    st_sort(s)
    link.corner(3, 2)
    link.corner(3, 3)
    st_attend(s, 0)
    link.pair(3, 0)
    link.pair(3, 1)
    link.turned(2)
    link.plane(4, 1)
    link.plane(4, 2)
    link.plane(4, 3)
    st_attend(s, 1)
    link.pair(3, 2)
    link.pair(3, 3)
    link.gathered(2)
    st_out(s, w, gain_ffn)
    transpose_into(s.nft, s.nf)
    link.gathered(3)

    def ffn(u):
        early, late = u == 0, u == 1
        @pl.when(late)
        def _():
            link.gathered(4)

        st_ffn(s, w, 1 - c, u, None)

        @pl.when(early)
        def _():
            for d in four:
                link.corner(4, d)
        st_ffn_grads(s, g, None, 1 - c, u, False)
        for n in range(2):
            pl.when(u == n)(functools.partial(link.grads_pair, n))
        st_ffn(s, w, c, u, e.tok)

        @pl.when(early)
        def _():
            for d in four:
                link.pair(4, d)
            link.arrived("gt", 0)

        @pl.when(late)
        def _():
            link.grads_join(0)
            link.arrived("gt", 1)
        st_ffn_grads(s, g, e.other, c, u, True)
        for n in range(2):
            pl.when(u == n)(functools.partial(link.grads_part, n))
    loop(2, ffn)
    st_mid_back(s, w, gain_ffn)
    st_out_grads(s, g, None, 1 - c, False)
    link.grads_pair(2)

    def attend0():
        link.arrived("gt", 2)
        st_out_grads(s, g, e.other, c, True)
        link.grads_plane(2)
        link.grads_line(0, False)

    def sort0():
        link.grads_join(1)

    def first():
        link.grads_pair(3)

    def pair():
        link.arrived("gt", 3)

    def queries():
        link.grads_plane(4)
        link.grads_line(1, False)

    def values():
        link.grads_plane(3)
        link.grads_line(2, True)

    def last():
        link.grads_plane(5)

    attention_backward(s, w, g, e.other, c, gain_attn, e.cot, {
        "attend0": attend0, "sort0": sort0, "first": first, "pair": pair, "queries": queries, "values": values, "last": last})
    e.gs[0] = s.gg[...]
    link.gains_sum(0)
    stores = []
    for n, (buf, out) in enumerate(((e.cot, gtok), (e.tok, result))):
        st_restore(buf)
        stores.append(pltpu.make_async_copy(buf.at[mine, :], out.at[c], local.at[2 + n]))
        stores[n].start()
        link.send("out", n)
    link.grads_line(4, True)
    link.gains_sum(1)
    link.grads_in(0)
    link.grads_in(2)
    link.grads_line(3, True)
    link.grads_line(5, True)
    link.gains_sum(2)
    link.grads_in(1)
    link.grads_in(4)
    link.grads_in(3)
    link.arrived("out", 0)
    link.arrived("out", 1)
    for cp in stores:
        cp.wait()
    total = link.gains_sum(3)
    width = D // 32
    pick = (iota((D, 128), 0) == iota((D, 128), 1) + (2 * f + c) * width).astype(F32)
    gains[...] = nn(total, pick, precision=HI)
    link.grads_in(5)
    link.finish()


def by_kernel(tokens, gain_attn, gain_ffn, w_query, w_key, w_value, w_out, w_in, w_down, segment_ids, cotangent):
    vm, hbm = pl.BlockSpec(memory_space=pltpu.VMEM), pl.BlockSpec(memory_space=pl.ANY)
    shapes = list(SCRATCH.values()) + list(EXCHANGE.values())
    res, gtok, grads, gains = pl.pallas_call(
        step_kernel,
        out_shape=(jax.ShapeDtypeStruct(tokens.shape, BF), jax.ShapeDtypeStruct(tokens.shape, BF),
                   jax.ShapeDtypeStruct((ROWS, COLS), F32), jax.ShapeDtypeStruct((8, 128), F32)),
        in_specs=[hbm] * 2 + [vm] * 9, out_specs=(hbm, hbm, vm, vm),
        scratch_shapes=[pltpu.VMEM(*v) for v in shapes] + [
            pltpu.SemaphoreType.DMA((NSEND,)), pltpu.SemaphoreType.DMA((NSEM,)), pltpu.SemaphoreType.DMA((4,))],
        compiler_params=pltpu.CompilerParams(collective_id=0, has_side_effects=True, vmem_limit_bytes=63 << 20),
    )(tokens, cotangent, gain_attn[None], gain_ffn[None], w_query, w_key, w_value, w_out.T, w_in, w_down.T, segment_ids)
    return finish(res, gtok, grads, gains, D // 32)


def solution(mesh):
    body = by_kernel if mesh.shape["fsdp"] == 16 else by_collectives
    return jax.shard_map(
        body,
        mesh=mesh,
        in_specs=(P(None, ("fsdp", "tp"), None), P(), P(), P("fsdp", "tp"), P("fsdp", "tp"), P("fsdp", "tp"),
                  P("tp", "fsdp"), P("fsdp", "tp"), P("tp", "fsdp"), P(None, "fsdp"), P(None, ("fsdp", "tp"), None)),
        out_specs=(P(None, ("fsdp", "tp"), None), P(None, ("fsdp", "tp"), None), P(("fsdp", "tp")), P(("fsdp", "tp")),
                   P("fsdp", "tp"), P("fsdp", "tp"), P("fsdp", "tp"), P("tp", "fsdp"), P("fsdp", "tp"), P("tp", "fsdp")),
        check_vma=False,
    )
```

```python
import collections
import functools
import math
import jax, jax.numpy as jnp
from jax import lax
from jax.experimental import pallas as pl
from jax.experimental.pallas import tpu as pltpu
from jax.sharding import PartitionSpec as P

F32, BF = jnp.float32, jnp.bfloat16
HI = lax.Precision.HIGHEST
HD, BLK, ITERS, NB, D, FF, T = 64, 32, 8, 32, 512, 2048, 1024
HALF = D // 2
COLS = 3 * HALF + HALF + FF
QO, VO, OO, FO = 0, 512, 768, 1024
UNITS = 512
STEPS = FF // 2 // UNITS


def in_cols(u):
    return slice(FO + 2 * u * UNITS, FO + (2 * u + 1) * UNITS)


def down_cols(u):
    return slice(FO + (2 * u + 1) * UNITS, FO + (2 * u + 2) * UNITS)


def span(start, count):
    return pl.ds(pl.multiple_of(start, 128), count)


def nn(a, b, precision=None):
    return lax.dot_general(a, b, (((1,), (0,)), ((), ())), precision=precision, preferred_element_type=F32)


def nt(a, b, precision=None):
    return lax.dot_general(a, b, (((1,), (1,)), ((), ())), precision=precision, preferred_element_type=F32)


def tn(a, b, precision=None):
    return lax.dot_general(a, b, (((0,), (0,)), ((), ())), precision=precision, preferred_element_type=F32)


def iota(shape, dim):
    return lax.broadcasted_iota(jnp.int32, shape, dim)


def order_matrix(inverse):
    n, m = iota((128, 128), 0), iota((128, 128), 1)
    if inverse:
        n, m = m, n
    return (m == (n & 3) * 32 + (n >> 2)).astype(BF)


def norm_rows(x, gain):
    center = x - jnp.mean(x, axis=1, keepdims=True)
    inv = lax.rsqrt(jnp.mean(center * center, axis=1, keepdims=True) + 1e-05)
    xhat = center * inv
    return xhat, inv


def norm_back(xhat, inv, gain, grad):
    gx = grad * gain
    m1 = jnp.mean(gx, axis=1, keepdims=True)
    m2 = jnp.mean(gx * xhat, axis=1, keepdims=True)
    return inv * (gx - m1 - xhat * m2)


def even_lanes(shape):
    return (iota(shape, len(shape) - 1) & 127) < 64


def stack_heads(x):
    ev = even_lanes(x.shape)
    z = jnp.zeros_like(x)
    return jnp.concatenate([jnp.where(ev, x, z), jnp.where(ev, z, x)], axis=0)


def pick_heads(r):
    n = r.shape[0] // 2
    ev = even_lanes((n, r.shape[1]))
    return jnp.where(ev, r[:n], r[n:])


SCRATCH = dict(
    tokp=((T, D), BF), cotp=((T, D), BF), cott=((D, T), BF), nm=((T, D), BF), nmt=((D, T), BF),
    q=((T, D), BF), k=((T, D), BF), v=((T, D), BF), ks=((T, D), BF), vs=((T, D), BF),
    qm=((NB, D), F32), km=((NB, D), F32), sk=((2 * ITERS, 8 * NB, NB), F32), allow=((NB, NB), F32),
    kr=((8, 128, 128), BF), krt=((8, 128, 128), BF), hidq=((256, 128), BF), hidk=((256, 128), BF),
    pr=((4, 8, 256, 256), BF), mix=((T, D), BF), mid=((T, D), F32), nf=((T, D), BF), nft=((D, T), BF),
    hid=((T, UNITS), BF), gp=((T, UNITS), BF), res=((T, D), F32), gnf=((T, D), F32),
    ga=((T, D), BF), gat=((D, T), BF), gmix=((T, D), BF), dv=((T, D), F32), ds=((8 * NB, NB), F32),
    gg=((8, D), F32),
)
SHARED = dict(dq="res", dk="gnf", dks="hid", dvs="gp", dqb="ga", dkb="nm", dvb="nf")


def loop(n, body, unroll=1):
    lax.fori_loop(0, n, lambda i, c: (body(i), c)[1], 0, unroll=unroll)


def rows(i, n):
    return pl.ds(pl.multiple_of(i * n, n), n)


def pipeline(units, stages, lags, after=None):
    vals = [{} for _ in units]
    for step in range(len(units) + lags[-1]):
        for st, lag in reversed(list(zip(stages, lags))):
            if 0 <= step - lag < len(units):
                st(units[step - lag], vals[step - lag])
        if after is not None:
            after(step)


def st_tokens(s, tok, gain_attn):
    pm = order_matrix(False)

    def body(c):
        def order(i, v):
            v["x"] = nn(pm, tok[rows(4 * c + i, 128), :])

        def norm(i, v):
            at = rows(4 * c + i, 128)
            x = v.pop("x")
            s.tokp[at, :] = x.astype(BF)
            xhat, _ = norm_rows(x, None)
            s.nm[at, :] = (xhat * gain_attn[...]).astype(BF)
        pipeline(range(4), (order, norm), (0, 1))
    loop(2, body)


def st_cot(s, cot):
    pm = order_matrix(False)

    def body(c):
        for i in range(4):
            at = rows(4 * c + i, 128)
            s.cotp[at, :] = nn(pm, cot[at, :]).astype(BF)
    loop(2, body)


def transpose_into(dst, src):
    for c in range(4):
        dst[:, c * 256:(c + 1) * 256] = jnp.transpose(src[c * 256:(c + 1) * 256, :], (1, 0))


def block_sums(x):
    y = jnp.sum(x.reshape(16, 8, x.shape[1]), axis=0)
    return y[0:4] + y[4:8]


def st_values(s, w):
    for m in range(4):
        x = s.nm[rows(m, 256), :]
        for t in range(2):
            s.v[rows(m, 256), t * 256:(t + 1) * 256] = nn(x, w[t, :, VO:VO + HALF]).astype(BF)


def st_query_key(s, w, t):
    cs = half_cols(t)

    def product(m, v):
        v["x"] = nn(s.nm[rows(m, 256), :], w[t, :, 0:512]).astype(BF)

    def store(m, v):
        at, out = rows(m, 256), v.pop("x")
        queries = jnp.concatenate([out[:, 0:128], out[:, 256:384]], axis=1)
        keys = jnp.concatenate([out[:, 128:256], out[:, 384:512]], axis=1)
        qv, kv = queries.astype(F32), keys.astype(F32)
        s.q[at, cs] = (qv * (1.0 / math.sqrt(HD))).astype(BF)
        s.k[at, cs] = keys
        for ref, val in ((s.qm, qv), (s.km, kv)):
            sums = jnp.concatenate([block_sums(val[:128]), block_sums(val[128:])], axis=0)
            ref[rows(m, 8), cs] = sums * (1.0 / BLK)
    pipeline(range(4), (product, store), (0, 1))


def st_sinkhorn(s, seg, halfway=None):
    row = jnp.broadcast_to(seg[...], (NB, NB))
    ri, ci = iota((NB, NB), 0), iota((NB, NB), 1)
    col = jnp.sum(jnp.where(ri == ci, row, 0), axis=1, keepdims=True)
    allow = ((row == col) & (ci <= ri)) | ((row == 0) & (col > 0))
    s.allow[...] = allow.astype(F32)
    parts = []
    for p in range(4):
        cs = slice(p * 128, (p + 1) * 128)
        parts.append(nt(stack_heads(s.qm[:, cs]), s.km[:, cs], precision=HI))
    x = jnp.concatenate(parts, axis=0) * (BLK / math.sqrt(HD))
    mask = jnp.concatenate([allow.astype(F32)] * 8, axis=0) > 0
    x = jnp.where(mask, x, -1000000000.0)
    for it in range(ITERS):
        m = jnp.max(x, axis=1, keepdims=True)
        e = jnp.exp(x - m)
        z = jnp.sum(e, axis=1, keepdims=True)
        s.sk[2 * it] = e * (1.0 / z)
        x = x - (m + jnp.log(z))
        y = x.reshape(8, NB, NB)
        m = jnp.max(y, axis=1, keepdims=True)
        e = jnp.exp(y - m)
        z = jnp.sum(e, axis=1, keepdims=True)
        s.sk[2 * it + 1] = (e * (1.0 / z)).reshape(8 * NB, NB)
        x = (y - (m + jnp.log(z))).reshape(8 * NB, NB)
        if it == ITERS // 2 - 1 and halfway is not None:
            halfway()
    sorter = s.sk[2 * ITERS - 1].astype(BF)
    n = iota((128, NB), 0)
    e_mat = (((n >> 4) * 4 + (n & 3)) == iota((128, NB), 1)).astype(BF)
    wide = nt(sorter, e_mat).astype(BF)
    a, b = iota((128, 128), 0), iota((128, 128), 1)
    same = ((a >> 2) & 3) == ((b >> 2) & 3)
    for h in range(8):
        kr = jnp.where(same, nn(e_mat, wide[h * NB:(h + 1) * NB]), 0.0)
        s.kr[h] = kr.astype(BF)
        s.krt[h] = jnp.transpose(kr, (1, 0)).astype(BF)


def gather_chunk(ref, rq, cs):
    return jnp.concatenate([ref[pl.ds(pl.multiple_of(i * 128 + rq * 16, 16), 16), cs] for i in range(8)], axis=0)


def split_pair(x):
    return stack_heads(x)


def st_sort(s):
    def body(r):
        def mix(unit, v):
            rq, p = 2 * r + unit // 4, unit % 4
            cs = slice(p * 128, (p + 1) * 128)
            kv = jnp.concatenate([gather_chunk(s.k, rq, cs), gather_chunk(s.v, rq, cs)], axis=1)
            lhs = jnp.concatenate([s.kr[2 * p], s.kr[2 * p + 1]], axis=1)
            v["out"] = nn(lhs, split_pair(kv))

        def store(unit, v):
            rq, p = 2 * r + unit // 4, unit % 4
            cs = slice(p * 128, (p + 1) * 128)
            out = v.pop("out").astype(BF)
            for i in range(8):
                at = pl.ds(pl.multiple_of(i * 128 + rq * 16, 16), 16)
                s.ks[at, cs] = out[i * 16:(i + 1) * 16, 0:128]
                s.vs[at, cs] = out[i * 16:(i + 1) * 16, 128:256]
        pipeline(range(8), (mix, store), (0, 2))
    loop(4, body)


def st_bias(s):
    n, a = iota((256, 128), 0), iota((256, 128), 1)
    s.hidq[...] = ((a == (n & 3)) | (a == 4 + ((n & 127) >> 2))).astype(BF)
    other = (a < 4) & (a != (n & 3))
    later = (n < 128) & (a >= 4) & (a < 36) & ((n >> 2) > a - 4)
    s.hidk[...] = jnp.where(other | later, -1e30, 0.0).astype(BF)


def pick_rows(r):
    n = r.shape[1] // 2
    return jnp.concatenate([r[:64, :n], r[64:, n:]], axis=0)


def chunk_pair(c, i):
    p = i % 4
    c = c + i // 4
    return c, p, rows(c, 128), slice(p * 128, (p + 1) * 128)


def st_attend(s, b):
    def score(i, v):
        c, p, at, cs = chunk_pair(4 * b, i)
        qs = jnp.concatenate([stack_heads(s.q[at, cs]), s.hidq[...]], axis=1)
        kk = jnp.concatenate([jnp.concatenate([s.k[at, cs], s.ks[at, cs]], axis=0), s.hidk[...]], axis=1)
        v["x"] = nt(kk, qs)

    def soften(i, v):
        c, p, at, cs = chunk_pair(4 * b, i)
        x = v.pop("x")
        e = jnp.exp(x - jnp.max(x, axis=0, keepdims=True))
        v["p"] = (e * (1.0 / jnp.sum(e, axis=0, keepdims=True))).astype(BF)
        s.pr[p, c] = v["p"]

    def blend(i, v):
        c, p, at, cs = chunk_pair(4 * b, i)
        vv = jnp.concatenate([s.v[at, cs], s.vs[at, cs]], axis=0)
        v["o"] = pick_rows(nn(jnp.transpose(vv, (1, 0)), v.pop("p")))

    def store(i, v):
        c, p, at, cs = chunk_pair(4 * b, i)
        s.mix[at, cs] = jnp.transpose(v.pop("o"), (1, 0)).astype(BF)
    pipeline(range(16), (score, soften, blend, store), (0, 2, 4, 6))


def st_out(s, w, gain_ffn):
    def product(m, v):
        at = rows(m, 256)
        v["x"] = sum(nt(s.mix[at, t * 256:(t + 1) * 256], w[t, :, OO:OO + HALF]) for t in range(2))

    def norm(m, v):
        at = rows(m, 256)
        mid = s.tokp[at, :].astype(F32) + v.pop("x")
        s.mid[at, :] = mid
        s.res[at, :] = mid
        s.gnf[at, :] = jnp.zeros((256, D), F32)
        xhat, _ = norm_rows(mid, None)
        s.nf[at, :] = (xhat * gain_ffn[...]).astype(BF)
    pipeline(range(4), (product, norm), (0, 1))


def gelu_pair(x):
    k0, k1 = math.sqrt(2.0 / math.pi), 0.044715
    x2 = x * x
    half = 0.5 + 0.5 * jnp.tanh(x * (k0 + (k0 * k1) * x2))
    val = x * half
    der = half + (val - val * half) * (2 * k0 + (6 * k0 * k1) * x2)
    return val, der


def add_grads(g, other, t, own, cols, val):
    if own:
        val = val + other[:, :, :, cols].reshape(D, val.shape[1]).astype(F32)
    g[t, :, :, :, cols] = val.astype(BF).reshape(4, 4, D // 16, val.shape[1])


def st_ffn(s, w, t, u, out):
    ic, dc = span(FO + 2 * u * UNITS, UNITS), span(FO + (2 * u + 1) * UNITS, UNITS)

    def into(m, v):
        at = rows(m, 256)
        v["x"] = nn(s.nf[at, :], w[t, :, ic])
        v["g"] = nn(s.cotp[at, :], w[t, :, dc])

    def bend(m, v):
        at = rows(m, 256)
        val, der = gelu_pair(v.pop("x"))
        v["h"] = val.astype(BF)
        v["g"] = (v["g"] * der).astype(BF)
        s.hid[at, :] = v["h"]
        s.gp[at, :] = v["g"]

    def back(m, v):
        at = rows(m, 256)
        add = nt(v.pop("h"), w[t, :, dc])
        add = s.res[at, :] + add
        s.res[at, :] = add
        if out is not None:
            out[at, :] = add.astype(BF)
        add = nt(v.pop("g"), w[t, :, ic])
        s.gnf[at, :] = s.gnf[at, :] + add
    pipeline(range(4), (into, bend, back), (0, 2, 3))


def st_ffn_grads(s, g, other, t, u, own):
    add_grads(g, other, t, own, span(FO + 2 * u * UNITS, UNITS), nn(s.nft[...], s.gp[...]))
    add_grads(g, other, t, own, span(FO + (2 * u + 1) * UNITS, UNITS), nn(s.cott[...], s.hid[...]))


def st_mid_back(s, w, gain_ffn):
    parts = []

    def norm(m, v):
        at = rows(m, 256)
        xhat, inv = norm_rows(s.mid[at, :], None)
        gnf = s.gnf[at, :]
        parts.append(jnp.sum((gnf * xhat).reshape(32, 8, D), axis=0))
        gm = s.cotp[at, :].astype(F32) + norm_back(xhat, inv, gain_ffn[...], gnf)
        s.mid[at, :] = gm
        v["ga"] = gm.astype(BF)
        s.ga[at, :] = v["ga"]

    def product(m, v):
        at = rows(m, 256)
        ga = v.pop("ga")
        for t in range(2):
            s.gmix[at, t * 256:(t + 1) * 256] = nn(ga, w[t, :, OO:OO + HALF]).astype(BF)
        s.gat[:, m * 256:(m + 1) * 256] = jnp.transpose(ga, (1, 0))
    pipeline(range(4), (norm, product), (0, 1))
    s.gg[1:2, :] = jnp.sum(sum(parts), axis=0, keepdims=True)


def half_cols(t):
    return pl.ds(pl.multiple_of(t * HALF, HALF), HALF)


def st_out_grads(s, g, other, t, own):
    add_grads(g, other, t, own, slice(OO, OO + HALF), nn(s.gat[...], s.mix[:, half_cols(t)]))


def st_restore(src):
    pm = order_matrix(True)
    for c in range(8):
        at = slice(c * 128, (c + 1) * 128)
        src[at, :] = nn(pm, src[at, :]).astype(BF)


def pair_cols(t, j):
    return pl.ds(pl.multiple_of(t * HALF + j * 128, 128), 128)


def st_attend_back(s, t, pairs, after=None):
    scale = 1.0 / math.sqrt(HD)

    def place(i):
        c, j = i // len(pairs), pairs[i % len(pairs)]
        return c, 2 * t + j, slice(c * 128, (c + 1) * 128), pair_cols(t, j)

    def grad_probs(i, v):
        c, p, at, cs = place(i)
        g = s.gmix[at, cs]
        go = (g.astype(F32) * s.mix[at, cs].astype(F32)).astype(BF)
        vv = jnp.concatenate([s.v[at, cs], s.vs[at, cs]], axis=0)
        v["dp"] = nt(jnp.concatenate([vv, jnp.full_like(vv, -1.0)], axis=1),
                     jnp.concatenate([stack_heads(g), stack_heads(go)], axis=1))

    def grad_scores(i, v):
        c, p, at, cs = place(i)
        v["ds"] = (s.pr[p, c].astype(F32) * v.pop("dp")).astype(BF)

    def products(i, v):
        c, p, at, cs = place(i)
        ds = v.pop("ds")
        dkk = nn(ds, stack_heads(s.q[at, cs]))
        dvv = nn(s.pr[p, c], stack_heads(s.gmix[at, cs]))
        s.dk[at, cs] = dkk[:128]
        s.dks[at, cs] = dkk[128:].astype(BF)
        s.dv[at, cs] = dvv[:128]
        s.dvs[at, cs] = dvv[128:].astype(BF)
        kk = jnp.concatenate([s.k[at, cs], s.ks[at, cs]], axis=0)
        v["dq"] = pick_rows(nn(jnp.transpose(kk, (1, 0)), ds))

    def store(i, v):
        c, p, at, cs = place(i)
        s.dq[at, cs] = jnp.transpose(v.pop("dq"), (1, 0)) * scale
    pipeline(range(8 * len(pairs)), (grad_probs, grad_scores, products, store), (0, 2, 4, 6), after)


def heads_at(t, pairs):
    n = 2 * NB
    return pl.ds(pl.multiple_of(t * 2 * n + pairs[0] * n, n), n * len(pairs))


def st_sort_back(s, t, pairs):
    a, b = iota((128, 128), 0), iota((128, 128), 1)
    same = ((a >> 2) & 3) == ((b >> 2) & 3)
    accs = {j: [] for j in pairs}

    def mix(i, v):
        j, rq = pairs[i // 8], i % 8
        cs = pair_cols(t, j)
        kv = jnp.concatenate([gather_chunk(s.k, rq, cs), gather_chunk(s.v, rq, cs)], axis=1)
        st = split_pair(jnp.concatenate([gather_chunk(s.dks, rq, cs), gather_chunk(s.dvs, rq, cs)], axis=1))
        accs[j].append(nt(st, kv))
        h = 4 * t + 2 * j
        v["out"] = nn(jnp.concatenate([s.krt[h], s.krt[h + 1]], axis=1), st)

    def store(i, v):
        j, rq = pairs[i // 8], i % 8
        cs = pair_cols(t, j)
        out = v.pop("out")
        for n in range(8):
            at = slice(n * 128 + rq * 16, n * 128 + rq * 16 + 16)
            s.dk[at, cs] = s.dk[at, cs] + out[n * 16:(n + 1) * 16, 0:128]
            s.dvb[at, cs] = (s.dv[at, cs] + out[n * 16:(n + 1) * 16, 128:256]).astype(BF)
    pipeline(range(8 * len(pairs)), (mix, store), (0, 2))

    def fold():
        heads = 2 * len(pairs)
        x = jnp.concatenate([sum(accs[j]) for j in pairs], axis=0)
        x = jnp.where(jnp.concatenate([same] * heads, axis=0), x, 0.0)
        n = iota((128, NB), 0)
        cols_of = (((n >> 4) * 4 + (n & 3)) == iota((128, NB), 1)).astype(BF)
        m, n = iota((heads * NB, heads * 128), 0), iota((heads * NB, heads * 128), 1)
        rows_of = ((m >> 5) == (n >> 7)) & ((m & 31) == ((n >> 4) & 7) * 4 + (n & 3))
        high, low = two_terms(x)
        high, low = two_terms(nn(high, cols_of) + nn(low, cols_of))
        rows_of = rows_of.astype(BF)
        s.ds[heads_at(t, pairs), :] = nn(rows_of, high) + nn(rows_of, low)
    return fold


def two_terms(x):
    high = x.astype(BF)
    return high, (x - high.astype(F32)).astype(BF)


def sinkhorn_back(s, t, pairs):
    hs, n = heads_at(t, pairs), 2 * len(pairs)
    v = {}

    def sweep(it):
        x = v["x"] if it < ITERS - 1 else s.ds[hs, :] * s.sk[2 * ITERS - 1, hs, :]
        y = x.reshape(n, NB, NB)
        pk = s.sk[2 * it + 1, hs, :].reshape(n, NB, NB)
        x = (y - pk * jnp.sum(y, axis=1, keepdims=True)).reshape(n * NB, NB)
        v["x"] = x - s.sk[2 * it, hs, :] * jnp.sum(x, axis=1, keepdims=True)

    def means():
        mask = jnp.concatenate([s.allow[...]] * n, axis=0) > 0
        x = jnp.where(mask, v.pop("x"), 0.0) * (1.0 / math.sqrt(HD))
        for h, j in enumerate(pairs):
            cs = pair_cols(t, j)
            x0, x1 = x[2 * h * NB:(2 * h + 1) * NB], x[(2 * h + 1) * NB:(2 * h + 2) * NB]
            ev = even_lanes((NB, 128))
            km, qm = s.km[:, cs], s.qm[:, cs]
            v[j] = (jnp.where(ev, nn(x0, km, precision=HI), nn(x1, km, precision=HI)),
                    jnp.where(ev, tn(x0, qm, precision=HI), tn(x1, qm, precision=HI)))

    def spread(j):
        cs = pair_cols(t, j)
        dqm, dkm = v.pop(j)
        for c in range(8):
            at = slice(c * 128, (c + 1) * 128)
            for src, ref, dst in ((dqm, s.dq, s.dqb), (dkm, s.dk, s.dkb)):
                four = src[c * 4:(c + 1) * 4]
                eight = jnp.concatenate([four, four], axis=0)
                val = ref[at, cs].reshape(16, 8, 128) + eight[None]
                dst[at, cs] = val.reshape(128, 128).astype(BF)
    steps = [functools.partial(sweep, it) for it in reversed(range(ITERS))]
    return steps + [means] + [functools.partial(spread, j) for j in pairs]


def st_value_grads(s, g, other, t, own, part):
    val = nn(s.nmt[part * 256:(part + 1) * 256, :], s.dvb[:, half_cols(t)])
    if own:
        val = val + other[2 * part:2 * part + 2, :, :, VO:OO].reshape(256, HALF).astype(F32)
    g[t, 2 * part:2 * part + 2, :, :, VO:OO] = val.astype(BF).reshape(2, 4, D // 16, HALF)


def st_query_key_grads(s, g, other, t, own, pairs):
    for j in pairs:
        cs = pair_cols(t, j)
        add_grads(g, other, t, own, slice(j * 256, (j + 1) * 256),
                  nn(s.nmt[...], jnp.concatenate([s.dqb[:, cs], s.dkb[:, cs]], axis=1)))


def st_tokens_back(s, w, gain_attn, out):
    parts = []

    def product(m, v):
        at = rows(m, 256)
        v["g"] = 0.0
        for t in range(2):
            cs = slice(t * 256, (t + 1) * 256)
            dq, dk = s.dqb[at, cs], s.dkb[at, cs]
            lhs = jnp.concatenate([dq[:, :128], dk[:, :128], dq[:, 128:], dk[:, 128:], s.dvb[at, cs]], axis=1)
            v["g"] = v["g"] + nt(lhs, w[t, :, 0:OO])

    def norm(m, v):
        at = rows(m, 256)
        gn = v.pop("g")
        xhat, inv = norm_rows(s.tokp[at, :].astype(F32), None)
        parts.append(jnp.sum((gn * xhat).reshape(32, 8, D), axis=0))
        out[at, :] = (s.mid[at, :] + norm_back(xhat, inv, gain_attn[...], gn)).astype(BF)
    pipeline(range(4), (product, norm), (0, 1))
    s.gg[0:1, :] = jnp.sum(sum(parts), axis=0, keepdims=True)


def attention_backward(s, w, g, other, c, gain_attn, out, hooks):
    own, both = other is not None, (0, 1)

    def with_steps(steps):
        return lambda n: steps[n]() if n < len(steps) else None
    st_attend_back(s, 1 - c, both)
    hooks["attend0"]()
    fold = st_sort_back(s, 1 - c, both)
    hooks["sort0"]()
    st_attend_back(s, c, (0,), with_steps([fold] + sinkhorn_back(s, 1 - c, both)))
    for part in range(2):
        st_value_grads(s, g, None, 1 - c, False, part)
    st_query_key_grads(s, g, None, 1 - c, False, both)
    hooks["first"]()
    fold = st_sort_back(s, c, (0,))
    st_attend_back(s, c, (1,), with_steps([fold] + sinkhorn_back(s, c, (0,))))
    hooks["pair"]()
    st_query_key_grads(s, g, other, c, own, (0,))
    hooks["queries"]()
    steps = [st_sort_back(s, c, (1,))] + sinkhorn_back(s, c, (1,))
    for n, step in enumerate(steps):
        step()
        if n in (0, 2):
            st_value_grads(s, g, other, c, own, n // 2)
        if n == 3:
            hooks["values"]()
    st_query_key_grads(s, g, other, c, own, (1,))
    hooks["last"]()
    st_tokens_back(s, w, gain_attn, out)


class Names:
    pass


def stage_names(refs):
    s = Names()
    for n, r in zip(SCRATCH, refs):
        setattr(s, n, r)
    for n, o in SHARED.items():
        setattr(s, n, getattr(s, o))
    return s


def layer_kernel(tok, cot, gain_attn, gain_ffn, w, seg, result, gtok, g, gg, *scr):
    s = stage_names(scr)
    st_tokens(s, tok, gain_attn)
    st_cot(s, cot)
    transpose_into(s.cott, s.cotp)
    transpose_into(s.nmt, s.nm)
    st_bias(s)
    for t in range(2):
        st_query_key(s, w, t)
    st_sinkhorn(s, seg)
    st_values(s, w)
    st_sort(s)
    loop(2, functools.partial(st_attend, s))
    st_out(s, w, gain_ffn)
    transpose_into(s.nft, s.nf)
    def ffn(u):
        for t in range(2):
            st_ffn(s, w, t, u, result if t == 1 else None)
            st_ffn_grads(s, g, None, t, u, False)
    loop(2, ffn)
    st_mid_back(s, w, gain_ffn)
    for t in range(2):
        st_out_grads(s, g, None, t, False)
    attention_backward(s, w, g, None, 0, gain_attn, gtok, collections.defaultdict(lambda: lambda: None))
    st_restore(result)
    st_restore(gtok)
    gg[...] = s.gg[...]


def layer_call():
    vm = pl.BlockSpec(memory_space=pltpu.VMEM)
    return pl.pallas_call(
        layer_kernel,
        out_shape=(jax.ShapeDtypeStruct((T, D), BF), jax.ShapeDtypeStruct((T, D), BF),
                   jax.ShapeDtypeStruct((2, 4, 4, D // 16, COLS), BF), jax.ShapeDtypeStruct((8, D), F32)),
        in_specs=[vm] * 6, out_specs=(vm,) * 4,
        scratch_shapes=[pltpu.VMEM(*v) for v in SCRATCH.values()],
        compiler_params=pltpu.CompilerParams(vmem_limit_bytes=60 << 20),
    )


def last_kernel(res, gtok, grads, gains, result, grad_tokens, gain_a, gain_f, gq, gk, gv, go, gi, gd, hold, held, sems):
    sem = iter(range(sems.shape[0]))

    def copy(src, dst):
        return pltpu.make_async_copy(src, dst, sems.at[next(sem)])
    moves = [(copy(grads, held), [copy(held.at[:, cols], ref.at[:, at]) for cols, ref, at in places(gq, gk, gv, go, gi, gd)])]
    for half in range(res.shape[0]):
        for n, (src, dst) in enumerate(((res, result), (gtok, grad_tokens))):
            moves.append((copy(src.at[half], hold.at[n, half]), [copy(hold.at[n, half], dst.at[half])]))
    for cp, _ in moves:
        cp.start()
    width = gain_a.shape[1]
    gain_a[...] = gains[0:1, 0:width]
    gain_f[...] = gains[1:2, 0:width]
    for cp, outs in moves:
        cp.wait()
        for out in outs:
            out.start()
    for _, outs in moves:
        for out in outs:
            out.wait()


def places(gq, gk, gv, go, gi, gd):
    runs = [(slice(VO, OO), gv, slice(0, HALF)), (slice(OO, FO), go, slice(0, HALF))]
    for j in range(2):
        at = slice(j * 128, (j + 1) * 128)
        runs += [(slice(j * 256, j * 256 + 128), gq, at), (slice(j * 256 + 128, (j + 1) * 256), gk, at)]
    for u in range(STEPS):
        at = slice(u * UNITS, (u + 1) * UNITS)
        runs += [(in_cols(u), gi, at), (down_cols(u), gd, at)]
    return runs


def last_call(res, gtok, grads, gains, width):
    vm, hbm = pl.BlockSpec(memory_space=pltpu.VMEM), pl.BlockSpec(memory_space=pl.ANY)
    square, long, row = (grads.shape[0], HALF), (grads.shape[0], FF // 2), (1, width)
    outs = [row, row, square, square, square, square, long, long]
    return pl.pallas_call(
        last_kernel,
        out_shape=(jax.ShapeDtypeStruct(res.shape, BF),) * 2 + tuple(jax.ShapeDtypeStruct(x, F32) for x in outs),
        in_specs=[hbm, hbm, hbm, vm],
        out_specs=(hbm, hbm, vm, vm) + (hbm,) * 6,
        scratch_shapes=[pltpu.VMEM((2,) + res.shape, BF), pltpu.VMEM(grads.shape, F32),
                        pltpu.SemaphoreType.DMA((7 + 4 * res.shape[0] + 2 * STEPS,))],
    )(res, gtok, grads, gains)


def join_cols(q, k, v, o, i, d):
    parts = []
    for j in range(2):
        parts += [q[:, j * 128:(j + 1) * 128], k[:, j * 128:(j + 1) * 128]]
    parts += [v, o]
    for u in range(STEPS):
        parts += [i[:, u * UNITS:(u + 1) * UNITS], d[:, u * UNITS:(u + 1) * UNITS]]
    return jnp.concatenate(parts, axis=1)


def by_collectives(tokens, gain_attn, gain_ffn, w_query, w_key, w_value, w_out, w_in, w_down, segment_ids, cotangent):
    tp = lax.axis_index("tp")
    tok = lax.all_to_all(tokens, "tp", 0, 0, tiled=True).reshape(T, D)
    cot = lax.all_to_all(cotangent, "tp", 0, 0, tiled=True).reshape(T, D)
    own = join_cols(w_query, w_key, w_value, w_out.T, w_in, w_down.T)
    half = lax.all_gather(own, "fsdp", axis=0, tiled=True)
    w = lax.all_gather(half, "tp", axis=0)
    seg = lax.dynamic_index_in_dim(segment_ids, tp, 0)
    res, gtok, g, gg = layer_call()(tok, cot, gain_attn[None], gain_ffn[None], w, seg)
    res = lax.all_to_all(res.reshape(tokens.shape), "tp", 0, 0, tiled=True)
    gtok = lax.all_to_all(gtok.reshape(tokens.shape), "tp", 0, 0, tiled=True)
    gsum = lax.psum_scatter(g.reshape(2, D, COLS).astype(F32), "tp", scatter_dimension=0)
    gsum = lax.psum_scatter(gsum, "fsdp", scatter_dimension=0, tiled=True)
    gains = lax.psum_scatter(gg, ("fsdp", "tp"), scatter_dimension=1, tiled=True)
    return finish(res, gtok, gsum, gains, gains.shape[1])


def finish(res, gtok, grads, gains, width):
    res, gtok, gain_a, gain_f, q, k, v, o, i, d = last_call(res, gtok, grads, gains, width)
    return res, gtok, gain_a.reshape(width), gain_f.reshape(width), q, k, v, o.T, i, d.T


PIECES = ((0, 512), (512, 768), (768, 1024), (1024, 2048), (2048, 3072))
GPIECES = ((1024, 2048), (2048, 3072), (768, 1024), (512, 768), (0, 256), (256, 512))
MESH = pl.DeviceIdType.MESH
ROWS = D // 16

EXCHANGE = dict(
    w=((2, D, COLS), BF), g=((2, 4, 4, ROWS, COLS), BF), other=((4, 4, ROWS, COLS), BF),
    rx=((3, 4, ROWS, COLS), BF), zs=((4, ROWS, COLS), BF), rz=((3, ROWS, COLS), BF),
    tok=((T, D), BF), cot=((T, D), BF), gr=((7, 8, D), F32), gs=((3, 8, D), F32),
)


def halves(lo, hi):
    mid = (lo + hi) // 2
    return slice(lo, mid), slice(mid, hi)


class Links:
    def __init__(self, e, sems):
        self.e = e
        self.sems = sems
        f, self.c = lax.axis_index("fsdp"), lax.axis_index("tp")
        self.zi, self.xy = f // 4, f % 4
        x, y = self.xy % 2, self.xy // 2
        self.f = f
        self.across = {"x": (1 - x) + 2 * y, "y": x + 2 * (1 - y), "d": (1 - x) + 2 * (1 - y)}
        self.arrival, self.sent = {}, []
        self.fixed = {}

    def z_at(self, dz):
        return (self.zi + dz) % 4

    def z_from(self, dz):
        return (self.zi + 4 - dz) % 4

    def greet(self):
        self.bar = pltpu.get_barrier_semaphore()
        for dev in ([(self.z_at(d) * 4 + self.xy, self.c) for d in (1, 2, 3)]
                    + [(self.zi * 4 + k, self.c) for k in self.across.values()] + [(self.f, 1 - self.c)]):
            pl.semaphore_signal(self.bar, inc=1, device_id=dev, device_id_type=MESH)

    def meet(self):
        pl.semaphore_wait(self.bar, 7)

    def w_rows(self, first, count, cols):
        return self.e.w.at[self.c, pl.ds(pl.multiple_of(first * ROWS, count * ROWS), count * ROWS), cols]

    def mine(self, k, cols):
        return self.e.g.at[self.c, :, self.across[k], :, cols]

    def route(self, kind, *key):
        e = self.e
        if kind in self.fixed:
            return self.fixed[kind][key[0]] + ("t",)
        if kind in ("z", "zz", "x", "y", "d", "xy", "yx", "t"):
            piece, d = key
            cols = slice(*PIECES[piece])
            first, second = halves(*PIECES[piece])
            if kind == "z":
                at, to = self.w_rows(self.f, 1, cols), d
            elif kind == "zz":
                at, to = self.w_rows(self.zi * 4, 4, cols), d
            elif kind == "t":
                at, to = self.w_rows(self.z_from(d) * 4, 4, cols), "t"
            elif kind == "xy":
                at, to = self.w_rows(self.z_from(d) * 4 + self.across["x"], 1, first), "y"
            elif kind == "yx":
                at, to = self.w_rows(self.z_from(d) * 4 + self.across["y"], 1, second), "x"
            else:
                at, to = self.w_rows(self.z_from(d) * 4 + self.xy, 1, cols), kind
            return at, at, to
        if kind == "n":
            n = key[0]
            return e.gs.at[0 if n == 0 else 1 if n < 4 else 2], e.gr.at[n], "t" if n == 0 else "xyd"[n - 1] if n < 4 else n - 3
        piece = key[0]
        if kind == "gt":
            lo, hi = GPIECES[piece] if piece < 3 else (0, OO)
            return e.g.at[1 - self.c, :, :, :, lo:hi], e.other.at[:, :, :, lo:hi], "t"
        cols = slice(*GPIECES[piece])
        if kind == "gz":
            d = key[1]
            return e.zs.at[d, :, cols], e.rz.at[d - 1, :, cols], d
        to = kind[1]
        if len(key) > 1:
            cols = halves(*GPIECES[piece])[key[1]]
            if kind == "gd":
                to = "xy"[key[1]]
        return self.mine(kind[1], cols), e.rx.at["xyd".index(kind[1]), :, :, cols], to

    def copy(self, key):
        src, dst, to = self.route(*key)
        if isinstance(to, int):
            dev = (self.z_at(to) * 4 + self.xy, self.c)
        elif to == "t":
            dev = (self.f, 1 - self.c)
        else:
            dev = (self.zi * 4 + self.across[to], self.c)
        sent = self.sent.index(key) % NSEND if key in self.sent else 0
        return pltpu.make_async_remote_copy(
            src_ref=src, dst_ref=dst, send_sem=self.sems[0].at[sent],
            recv_sem=self.sems[1].at[self.arrival.setdefault(key, len(self.arrival))], device_id=dev, device_id_type=MESH)

    def send(self, *key):
        self.sent.append(key)
        if len(self.sent) > NSEND:
            self.copy(self.sent[-1 - NSEND]).wait_send()
        self.copy(key).start()

    def arrived(self, *key):
        self.copy(key).wait_recv()

    def finish(self):
        assert len(self.sent) == len(self.arrival) == NSEM, len(self.sent)
        for key in self.sent[-NSEND:]:
            self.copy(key).wait_send()

    def own_z(self, piece):
        for d in (1, 2, 3):
            self.send("z", piece, d)

    def own_plane(self, piece):
        self.to_plane(piece, 0)

    def to_plane(self, piece, d):
        for k in "xyd" if piece < 3 else "xy":
            self.send(k, piece, d)

    def plane(self, piece, d):
        self.arrived("z", piece, d)
        self.to_plane(piece, d)

    def corner(self, piece, d):
        self.arrived("x", piece, d)
        self.send("xy", piece, d)
        self.arrived("y", piece, d)
        self.send("yx", piece, d)

    def pair(self, piece, d):
        for k in ("x", "y", "d") if piece < 2 else ("xy", "yx"):
            self.arrived(k, piece, d)
        self.send("t", piece, d)

    def turn(self, piece):
        for k in "xyd":
            self.arrived(k, piece, 0)
        for d in (1, 2, 3):
            self.send("zz", piece, d)
        self.send("t", piece, 0)

    def turned(self, piece):
        for d in (1, 2, 3):
            self.arrived("zz", piece, d)
            self.send("t", piece, d)

    def gathered(self, piece):
        for d in range(4):
            self.arrived("t", piece, d)

    def grads_pair(self, piece):
        self.send("gt", piece)

    def grads_plane(self, piece):
        for k in "xyd":
            self.send("g" + k, piece)

    def grads_part(self, piece):
        self.send("gd", piece, 0)
        self.send("gd", piece, 1)
        self.send("gx", piece, 0)
        self.send("gy", piece, 1)

    def grads_join(self, piece):
        first, second = halves(*GPIECES[piece])
        for n, k, cols in ((0, "y", first), (1, "x", second)):
            self.arrived("gd", piece, n)
            at = self.mine(k, cols)
            at[...] = (at[...].astype(F32) + self.e.rx[2, :, :, cols].astype(F32)).astype(BF)
            self.send("g" + k, piece, n)

    def grads_line(self, piece, direct):
        e = self.e
        cols = slice(*GPIECES[piece])
        if direct:
            for k in "xyd":
                self.arrived("g" + k, piece)
        else:
            for k in "xy":
                for n in range(2):
                    self.arrived("g" + k, piece, n)
        for d in (1, 2, 3, 0):
            z = self.z_at(d)
            total = e.g[self.c, z, self.xy, :, cols].astype(F32)
            for n in range(3 if direct else 2):
                total = total + e.rx[n, z, :, cols].astype(F32)
            if d:
                e.zs[d, :, cols] = total.astype(BF)
                self.send("gz", piece, d)
            else:
                self.out[:, cols] = total

    def grads_in(self, piece):
        cols = slice(*GPIECES[piece])
        for n in range(3):
            self.arrived("gz", piece, n + 1)
        total = self.out[:, cols]
        for n in range(3):
            total = total + self.e.rz[n, :, cols].astype(F32)
        self.out[:, cols] = total

    def gains_sum(self, step):
        e = self.e
        if step == 0:
            self.send("n", 0)
        if step == 1:
            self.arrived("n", 0)
            e.gs[1] = e.gs[0] + e.gr[0]
            for n in (1, 2, 3):
                self.send("n", n)
        if step == 2:
            for n in (1, 2, 3):
                self.arrived("n", n)
            e.gs[2] = e.gs[1] + e.gr[1] + e.gr[2] + e.gr[3]
            for n in (4, 5, 6):
                self.send("n", n)
        if step == 3:
            for n in (4, 5, 6):
                self.arrived("n", n)
            return e.gs[2] + e.gr[4] + e.gr[5] + e.gr[6]


NSEM = 154
NSEND = 24


def step_kernel(tokens, cotangent, gain_attn, gain_ffn, wq, wk, wv, wo, wi, wd, seg, result, gtok, gout, gains, *scr):
    ns, ne = len(SCRATCH), len(EXCHANGE)
    s = stage_names(scr[:ns])
    e = Names()
    for n, r in zip(EXCHANGE, scr[ns:ns + ne]):
        setattr(e, n, r)
    send_sem, recv_sem, local = scr[ns + ne:]
    link = Links(e, (send_sem, recv_sem))
    link.out = gout
    c, f, w, g = link.c, link.f, e.w, e.g
    half = T // 2
    mine = pl.ds(pl.multiple_of(c * half, half), half)
    theirs = pl.ds(pl.multiple_of((1 - c) * half, half), half)
    four, three = range(4), (1, 2, 3)

    link.fixed = {"in": [(tokens.at[1 - c], e.tok.at[mine, :]), (cotangent.at[1 - c], e.cot.at[mine, :])],
                  "out": [(e.cot.at[theirs, :], gtok.at[c]), (e.tok.at[theirs, :], result.at[c])]}
    loads = [pltpu.make_async_copy(tokens.at[c], e.tok.at[mine, :], local.at[0]),
             pltpu.make_async_copy(cotangent.at[c], e.cot.at[mine, :], local.at[1])]
    for cp in loads:
        cp.start()
    link.greet()
    w[c, pl.ds(pl.multiple_of(f * ROWS, ROWS), ROWS), :] = join_cols(wq[...], wk[...], wv[...], wo[...], wi[...], wd[...])
    link.meet()
    link.own_z(0)
    link.own_plane(0)
    link.send("in", 0)
    link.send("in", 1)
    link.own_z(1)
    link.own_plane(1)
    link.own_plane(2)
    loads[0].wait()
    link.arrived("in", 0)
    st_tokens(s, e.tok, gain_attn)
    loads[1].wait()
    link.arrived("in", 1)
    st_cot(s, e.cot)
    transpose_into(s.nmt, s.nm)
    for d in three:
        link.plane(0, d)
    link.own_z(3)
    transpose_into(s.cott, s.cotp)
    st_bias(s)
    for d in three:
        link.plane(1, d)
    link.own_plane(3)
    link.turn(2)
    for d in four:
        link.pair(0, d)
    link.own_z(4)
    st_query_key(s, w, c)
    link.gathered(0)
    st_query_key(s, w, 1 - c)
    link.plane(3, 1)
    link.plane(3, 2)

    def halfway():
        for d in four:
            link.pair(1, d)
        link.plane(3, 3)
        link.own_plane(4)
    st_sinkhorn(s, seg.at[pl.ds(c, 1), :], halfway)
    link.gathered(1)
    st_values(s, w)
    link.corner(3, 0)
    link.corner(3, 1)
    st_sort(s)
    link.corner(3, 2)
    link.corner(3, 3)
    st_attend(s, 0)
    link.pair(3, 0)
    link.pair(3, 1)
    link.turned(2)
    link.plane(4, 1)
    link.plane(4, 2)
    link.plane(4, 3)
    st_attend(s, 1)
    link.pair(3, 2)
    link.pair(3, 3)
    link.corner(4, 0)
    link.gathered(2)
    st_out(s, w, gain_ffn)
    transpose_into(s.nft, s.nf)
    link.gathered(3)

    def ffn(u):
        early, late = u == 0, u == 1
        @pl.when(late)
        def _():
            link.gathered(4)

        st_ffn(s, w, 1 - c, u, None)

        @pl.when(early)
        def _():
            for d in three:
                link.corner(4, d)
        st_ffn_grads(s, g, None, 1 - c, u, False)
        for n in range(2):
            pl.when(u == n)(functools.partial(link.grads_pair, n))
        st_ffn(s, w, c, u, e.tok)

        @pl.when(early)
        def _():
            for d in four:
                link.pair(4, d)
            link.arrived("gt", 0)

        @pl.when(late)
        def _():
            link.grads_join(0)
            link.arrived("gt", 1)
        st_ffn_grads(s, g, e.other, c, u, True)
        for n in range(2):
            pl.when(u == n)(functools.partial(link.grads_part, n))
    loop(2, ffn)
    st_mid_back(s, w, gain_ffn)
    st_out_grads(s, g, None, 1 - c, False)
    link.grads_pair(2)

    def attend0():
        link.arrived("gt", 2)
        st_out_grads(s, g, e.other, c, True)
        link.grads_plane(2)
        link.grads_line(0, False)

    def sort0():
        link.grads_join(1)

    def first():
        link.grads_pair(3)

    def pair():
        link.arrived("gt", 3)

    def queries():
        link.grads_plane(4)
        link.grads_line(1, False)

    def values():
        link.grads_part(3)
        link.grads_line(2, True)

    def last():
        link.grads_plane(5)

    attention_backward(s, w, g, e.other, c, gain_attn, e.cot, {
        "attend0": attend0, "sort0": sort0, "first": first, "pair": pair, "queries": queries, "values": values, "last": last})
    link.grads_join(3)
    e.gs[0] = s.gg[...]
    link.gains_sum(0)
    stores = []
    for n, (buf, out) in enumerate(((e.cot, gtok), (e.tok, result))):
        st_restore(buf)
        stores.append(pltpu.make_async_copy(buf.at[mine, :], out.at[c], local.at[2 + n]))
        stores[n].start()
        link.send("out", n)
    link.grads_line(4, True)
    link.gains_sum(1)
    link.grads_in(0)
    link.grads_in(2)
    link.grads_line(5, True)
    link.gains_sum(2)
    link.grads_line(3, False)
    link.grads_in(1)
    link.grads_in(4)
    link.grads_in(3)
    link.arrived("out", 0)
    link.arrived("out", 1)
    for cp in stores:
        cp.wait()
    total = link.gains_sum(3)
    width = D // 32
    pick = (iota((D, 128), 0) == iota((D, 128), 1) + (2 * f + c) * width).astype(F32)
    gains[...] = nn(total, pick, precision=HI)
    link.grads_in(5)
    link.finish()


def by_kernel(tokens, gain_attn, gain_ffn, w_query, w_key, w_value, w_out, w_in, w_down, segment_ids, cotangent):
    vm, hbm = pl.BlockSpec(memory_space=pltpu.VMEM), pl.BlockSpec(memory_space=pl.ANY)
    shapes = list(SCRATCH.values()) + list(EXCHANGE.values())
    res, gtok, grads, gains = pl.pallas_call(
        step_kernel,
        out_shape=(jax.ShapeDtypeStruct(tokens.shape, BF), jax.ShapeDtypeStruct(tokens.shape, BF),
                   jax.ShapeDtypeStruct((ROWS, COLS), F32), jax.ShapeDtypeStruct((8, 128), F32)),
        in_specs=[hbm] * 2 + [vm] * 9, out_specs=(hbm, hbm, vm, vm),
        scratch_shapes=[pltpu.VMEM(*v) for v in shapes] + [
            pltpu.SemaphoreType.DMA((NSEND,)), pltpu.SemaphoreType.DMA((NSEM,)), pltpu.SemaphoreType.DMA((4,))],
        compiler_params=pltpu.CompilerParams(collective_id=0, has_side_effects=True, vmem_limit_bytes=63 << 20),
    )(tokens, cotangent, gain_attn[None], gain_ffn[None], w_query, w_key, w_value, w_out.T, w_in, w_down.T, segment_ids)
    return finish(res, gtok, grads, gains, D // 32)


def solution(mesh):
    body = by_kernel if mesh.shape["fsdp"] == 16 else by_collectives
    return jax.shard_map(
        body,
        mesh=mesh,
        in_specs=(P(None, ("fsdp", "tp"), None), P(), P(), P("fsdp", "tp"), P("fsdp", "tp"), P("fsdp", "tp"),
                  P("tp", "fsdp"), P("fsdp", "tp"), P("tp", "fsdp"), P(None, "fsdp"), P(None, ("fsdp", "tp"), None)),
        out_specs=(P(None, ("fsdp", "tp"), None), P(None, ("fsdp", "tp"), None), P(("fsdp", "tp")), P(("fsdp", "tp")),
                   P("fsdp", "tp"), P("fsdp", "tp"), P("fsdp", "tp"), P("tp", "fsdp"), P("fsdp", "tp"), P("tp", "fsdp")),
        check_vma=False,
    )
```

```python
import collections
import functools
import math
import jax, jax.numpy as jnp
from jax import lax
from jax.experimental import pallas as pl
from jax.experimental.pallas import tpu as pltpu
from jax.sharding import PartitionSpec as P

F32, BF = jnp.float32, jnp.bfloat16
HI = lax.Precision.HIGHEST
HD, BLK, ITERS, NB, D, FF, T = 64, 32, 8, 32, 512, 2048, 1024
HALF = D // 2
COLS = 3 * HALF + HALF + FF
QO, VO, OO, FO = 0, 512, 768, 1024
UNITS = 512
STEPS = FF // 2 // UNITS


def in_cols(u):
    return slice(FO + 2 * u * UNITS, FO + (2 * u + 1) * UNITS)


def down_cols(u):
    return slice(FO + (2 * u + 1) * UNITS, FO + (2 * u + 2) * UNITS)


def span(start, count):
    return pl.ds(pl.multiple_of(start, 128), count)


def nn(a, b, precision=None):
    return lax.dot_general(a, b, (((1,), (0,)), ((), ())), precision=precision, preferred_element_type=F32)


def nt(a, b, precision=None):
    return lax.dot_general(a, b, (((1,), (1,)), ((), ())), precision=precision, preferred_element_type=F32)


def tn(a, b, precision=None):
    return lax.dot_general(a, b, (((0,), (0,)), ((), ())), precision=precision, preferred_element_type=F32)


def iota(shape, dim):
    return lax.broadcasted_iota(jnp.int32, shape, dim)


def order_matrix(inverse):
    n, m = iota((128, 128), 0), iota((128, 128), 1)
    if inverse:
        n, m = m, n
    return (m == (n & 3) * 32 + (n >> 2)).astype(BF)


def norm_rows(x, gain):
    center = x - jnp.mean(x, axis=1, keepdims=True)
    inv = lax.rsqrt(jnp.mean(center * center, axis=1, keepdims=True) + 1e-05)
    xhat = center * inv
    return xhat, inv


def norm_back(xhat, inv, gain, grad):
    gx = grad * gain
    m1 = jnp.mean(gx, axis=1, keepdims=True)
    m2 = jnp.mean(gx * xhat, axis=1, keepdims=True)
    return inv * (gx - m1 - xhat * m2)


def even_lanes(shape):
    return (iota(shape, len(shape) - 1) & 127) < 64


def stack_heads(x):
    ev = even_lanes(x.shape)
    z = jnp.zeros_like(x)
    return jnp.concatenate([jnp.where(ev, x, z), jnp.where(ev, z, x)], axis=0)


def pick_heads(r):
    n = r.shape[0] // 2
    ev = even_lanes((n, r.shape[1]))
    return jnp.where(ev, r[:n], r[n:])


SCRATCH = dict(
    tokp=((T, D), BF), cotp=((T, D), BF), cott=((D, T), BF), nm=((T, D), BF), nmt=((D, T), BF),
    q=((T, D), BF), k=((T, D), BF), v=((T, D), BF), ks=((T, D), BF), vs=((T, D), BF),
    qm=((NB, D), F32), km=((NB, D), F32), sk=((2 * ITERS, 8 * NB, NB), F32), allow=((NB, NB), F32),
    kr=((8, 128, 128), BF), krt=((8, 128, 128), BF), hidq=((256, 128), BF), hidk=((256, 128), BF),
    pr=((4, 8, 256, 256), BF), mix=((T, D), BF), mid=((T, D), F32), nf=((T, D), BF), nft=((D, T), BF),
    hid=((T, UNITS), BF), gp=((T, UNITS), BF), res=((T, D), F32), gnf=((T, D), F32),
    ga=((T, D), BF), gat=((D, T), BF), gmix=((T, D), BF), dv=((T, D), F32), ds=((8 * NB, NB), F32),
    gg=((8, D), F32),
)
SHARED = dict(dq="res", dk="gnf", dks="hid", dvs="gp", dqb="ga", dkb="nm", dvb="nf")


def loop(n, body, unroll=1):
    lax.fori_loop(0, n, lambda i, c: (body(i), c)[1], 0, unroll=unroll)


def rows(i, n):
    return pl.ds(pl.multiple_of(i * n, n), n)


def pipeline(units, stages, lags, after=None):
    vals = [{} for _ in units]
    for step in range(len(units) + lags[-1]):
        for st, lag in reversed(list(zip(stages, lags))):
            if 0 <= step - lag < len(units):
                st(units[step - lag], vals[step - lag])
        if after is not None:
            after(step)


def st_tokens(s, tok, gain_attn):
    pm = order_matrix(False)

    def body(c):
        def order(i, v):
            v["x"] = nn(pm, tok[rows(4 * c + i, 128), :])

        def norm(i, v):
            at = rows(4 * c + i, 128)
            x = v.pop("x")
            s.tokp[at, :] = x.astype(BF)
            xhat, _ = norm_rows(x, None)
            s.nm[at, :] = (xhat * gain_attn[...]).astype(BF)
        pipeline(range(4), (order, norm), (0, 1))
    loop(2, body)


def st_cot(s, cot):
    pm = order_matrix(False)

    def body(c):
        for i in range(4):
            at = rows(4 * c + i, 128)
            s.cotp[at, :] = nn(pm, cot[at, :]).astype(BF)
    loop(2, body)


def transpose_into(dst, src):
    for c in range(4):
        dst[:, c * 256:(c + 1) * 256] = jnp.transpose(src[c * 256:(c + 1) * 256, :], (1, 0))


def block_sums(x):
    y = jnp.sum(x.reshape(16, 8, x.shape[1]), axis=0)
    return y[0:4] + y[4:8]


def st_values(s, w):
    for m in range(4):
        x = s.nm[rows(m, 256), :]
        for t in range(2):
            s.v[rows(m, 256), t * 256:(t + 1) * 256] = nn(x, w[t, :, VO:VO + HALF]).astype(BF)


def st_query_key(s, w, t):
    cs = half_cols(t)

    def product(m, v):
        v["x"] = nn(s.nm[rows(m, 256), :], w[t, :, 0:512]).astype(BF)

    def store(m, v):
        at, out = rows(m, 256), v.pop("x")
        queries = jnp.concatenate([out[:, 0:128], out[:, 256:384]], axis=1)
        keys = jnp.concatenate([out[:, 128:256], out[:, 384:512]], axis=1)
        qv, kv = queries.astype(F32), keys.astype(F32)
        s.q[at, cs] = (qv * (1.0 / math.sqrt(HD))).astype(BF)
        s.k[at, cs] = keys
        for ref, val in ((s.qm, qv), (s.km, kv)):
            sums = jnp.concatenate([block_sums(val[:128]), block_sums(val[128:])], axis=0)
            ref[rows(m, 8), cs] = sums * (1.0 / BLK)
    pipeline(range(4), (product, store), (0, 1))


def st_sinkhorn(s, seg, halfway=None):
    row = jnp.broadcast_to(seg[...], (NB, NB))
    ri, ci = iota((NB, NB), 0), iota((NB, NB), 1)
    col = jnp.sum(jnp.where(ri == ci, row, 0), axis=1, keepdims=True)
    allow = ((row == col) & (ci <= ri)) | ((row == 0) & (col > 0))
    s.allow[...] = allow.astype(F32)
    parts = []
    for p in range(4):
        cs = slice(p * 128, (p + 1) * 128)
        parts.append(nt(stack_heads(s.qm[:, cs]), s.km[:, cs], precision=HI))
    x = jnp.concatenate(parts, axis=0) * (BLK / math.sqrt(HD))
    mask = jnp.concatenate([allow.astype(F32)] * 8, axis=0) > 0
    x = jnp.where(mask, x, -1000000000.0)
    for it in range(ITERS):
        m = jnp.max(x, axis=1, keepdims=True)
        e = jnp.exp(x - m)
        z = jnp.sum(e, axis=1, keepdims=True)
        s.sk[2 * it] = e * (1.0 / z)
        x = x - (m + jnp.log(z))
        y = x.reshape(8, NB, NB)
        m = jnp.max(y, axis=1, keepdims=True)
        e = jnp.exp(y - m)
        z = jnp.sum(e, axis=1, keepdims=True)
        s.sk[2 * it + 1] = (e * (1.0 / z)).reshape(8 * NB, NB)
        x = (y - (m + jnp.log(z))).reshape(8 * NB, NB)
        if it == ITERS // 2 - 1 and halfway is not None:
            halfway()
    sorter = s.sk[2 * ITERS - 1].astype(BF)
    n = iota((128, NB), 0)
    e_mat = (((n >> 4) * 4 + (n & 3)) == iota((128, NB), 1)).astype(BF)
    wide = nt(sorter, e_mat).astype(BF)
    a, b = iota((128, 128), 0), iota((128, 128), 1)
    same = ((a >> 2) & 3) == ((b >> 2) & 3)
    for h in range(8):
        kr = jnp.where(same, nn(e_mat, wide[h * NB:(h + 1) * NB]), 0.0)
        s.kr[h] = kr.astype(BF)
        s.krt[h] = jnp.transpose(kr, (1, 0)).astype(BF)


def gather_chunk(ref, rq, cs):
    return jnp.concatenate([ref[pl.ds(pl.multiple_of(i * 128 + rq * 16, 16), 16), cs] for i in range(8)], axis=0)


def split_pair(x):
    return stack_heads(x)


def st_sort(s):
    def body(r):
        def mix(unit, v):
            rq, p = 2 * r + unit // 4, unit % 4
            cs = slice(p * 128, (p + 1) * 128)
            kv = jnp.concatenate([gather_chunk(s.k, rq, cs), gather_chunk(s.v, rq, cs)], axis=1)
            lhs = jnp.concatenate([s.kr[2 * p], s.kr[2 * p + 1]], axis=1)
            v["out"] = nn(lhs, split_pair(kv))

        def store(unit, v):
            rq, p = 2 * r + unit // 4, unit % 4
            cs = slice(p * 128, (p + 1) * 128)
            out = v.pop("out").astype(BF)
            for i in range(8):
                at = pl.ds(pl.multiple_of(i * 128 + rq * 16, 16), 16)
                s.ks[at, cs] = out[i * 16:(i + 1) * 16, 0:128]
                s.vs[at, cs] = out[i * 16:(i + 1) * 16, 128:256]
        pipeline(range(8), (mix, store), (0, 2))
    loop(4, body)


def st_bias(s):
    n, a = iota((256, 128), 0), iota((256, 128), 1)
    s.hidq[...] = ((a == (n & 3)) | (a == 4 + ((n & 127) >> 2))).astype(BF)
    other = (a < 4) & (a != (n & 3))
    later = (n < 128) & (a >= 4) & (a < 36) & ((n >> 2) > a - 4)
    s.hidk[...] = jnp.where(other | later, -1e30, 0.0).astype(BF)


def pick_rows(r):
    n = r.shape[1] // 2
    return jnp.concatenate([r[:64, :n], r[64:, n:]], axis=0)


def chunk_pair(c, i):
    p = i % 4
    c = c + i // 4
    return c, p, rows(c, 128), slice(p * 128, (p + 1) * 128)


def st_attend(s, b):
    def score(i, v):
        c, p, at, cs = chunk_pair(4 * b, i)
        qs = jnp.concatenate([stack_heads(s.q[at, cs]), s.hidq[...]], axis=1)
        kk = jnp.concatenate([jnp.concatenate([s.k[at, cs], s.ks[at, cs]], axis=0), s.hidk[...]], axis=1)
        v["x"] = nt(kk, qs)

    def soften(i, v):
        c, p, at, cs = chunk_pair(4 * b, i)
        x = v.pop("x")
        e = jnp.exp(x - jnp.max(x, axis=0, keepdims=True))
        v["p"] = (e * (1.0 / jnp.sum(e, axis=0, keepdims=True))).astype(BF)
        s.pr[p, c] = v["p"]

    def blend(i, v):
        c, p, at, cs = chunk_pair(4 * b, i)
        vv = jnp.concatenate([s.v[at, cs], s.vs[at, cs]], axis=0)
        v["o"] = pick_rows(nn(jnp.transpose(vv, (1, 0)), v.pop("p")))

    def store(i, v):
        c, p, at, cs = chunk_pair(4 * b, i)
        s.mix[at, cs] = jnp.transpose(v.pop("o"), (1, 0)).astype(BF)
    pipeline(range(16), (score, soften, blend, store), (0, 2, 4, 6))


def st_out(s, w, gain_ffn):
    def product(m, v):
        at = rows(m, 256)
        v["x"] = sum(nt(s.mix[at, t * 256:(t + 1) * 256], w[t, :, OO:OO + HALF]) for t in range(2))

    def norm(m, v):
        at = rows(m, 256)
        mid = s.tokp[at, :].astype(F32) + v.pop("x")
        s.mid[at, :] = mid
        s.res[at, :] = mid
        s.gnf[at, :] = jnp.zeros((256, D), F32)
        xhat, _ = norm_rows(mid, None)
        s.nf[at, :] = (xhat * gain_ffn[...]).astype(BF)
    pipeline(range(4), (product, norm), (0, 1))


def gelu_pair(x):
    k0, k1 = math.sqrt(2.0 / math.pi), 0.044715
    x2 = x * x
    half = 0.5 + 0.5 * jnp.tanh(x * (k0 + (k0 * k1) * x2))
    val = x * half
    der = half + (val - val * half) * (2 * k0 + (6 * k0 * k1) * x2)
    return val, der


def add_grads(g, other, t, own, cols, val):
    if own:
        val = val + other[:, :, :, cols].reshape(D, val.shape[1]).astype(F32)
    g[t, :, :, :, cols] = val.astype(BF).reshape(4, 4, D // 16, val.shape[1])


def st_ffn(s, w, t, u, out):
    ic, dc = span(FO + 2 * u * UNITS, UNITS), span(FO + (2 * u + 1) * UNITS, UNITS)

    def into(m, v):
        at = rows(m, 256)
        v["x"] = nn(s.nf[at, :], w[t, :, ic])
        v["g"] = nn(s.cotp[at, :], w[t, :, dc])

    def bend(m, v):
        at = rows(m, 256)
        val, der = gelu_pair(v.pop("x"))
        v["h"] = val.astype(BF)
        v["g"] = (v["g"] * der).astype(BF)
        s.hid[at, :] = v["h"]
        s.gp[at, :] = v["g"]

    def back(m, v):
        at = rows(m, 256)
        add = nt(v.pop("h"), w[t, :, dc])
        add = s.res[at, :] + add
        s.res[at, :] = add
        if out is not None:
            out[at, :] = add.astype(BF)
        add = nt(v.pop("g"), w[t, :, ic])
        s.gnf[at, :] = s.gnf[at, :] + add
    pipeline(range(4), (into, bend, back), (0, 2, 3))


def st_ffn_grads(s, g, other, t, u, own):
    add_grads(g, other, t, own, span(FO + 2 * u * UNITS, UNITS), nn(s.nft[...], s.gp[...]))
    add_grads(g, other, t, own, span(FO + (2 * u + 1) * UNITS, UNITS), nn(s.cott[...], s.hid[...]))


def st_mid_back(s, w, gain_ffn):
    parts = []

    def norm(m, v):
        at = rows(m, 256)
        xhat, inv = norm_rows(s.mid[at, :], None)
        gnf = s.gnf[at, :]
        parts.append(jnp.sum((gnf * xhat).reshape(32, 8, D), axis=0))
        gm = s.cotp[at, :].astype(F32) + norm_back(xhat, inv, gain_ffn[...], gnf)
        s.mid[at, :] = gm
        v["ga"] = gm.astype(BF)
        s.ga[at, :] = v["ga"]

    def product(m, v):
        at = rows(m, 256)
        ga = v.pop("ga")
        for t in range(2):
            s.gmix[at, t * 256:(t + 1) * 256] = nn(ga, w[t, :, OO:OO + HALF]).astype(BF)
        s.gat[:, m * 256:(m + 1) * 256] = jnp.transpose(ga, (1, 0))
    pipeline(range(4), (norm, product), (0, 1))
    s.gg[1:2, :] = jnp.sum(sum(parts), axis=0, keepdims=True)


def half_cols(t):
    return pl.ds(pl.multiple_of(t * HALF, HALF), HALF)


def st_out_grads(s, g, other, t, own):
    add_grads(g, other, t, own, slice(OO, OO + HALF), nn(s.gat[...], s.mix[:, half_cols(t)]))


def st_restore(src):
    pm = order_matrix(True)
    for c in range(8):
        at = slice(c * 128, (c + 1) * 128)
        src[at, :] = nn(pm, src[at, :]).astype(BF)


def pair_cols(t, j):
    return pl.ds(pl.multiple_of(t * HALF + j * 128, 128), 128)


def st_attend_back(s, t, pairs, after=None):
    scale = 1.0 / math.sqrt(HD)

    def place(i):
        c, j = i // len(pairs), pairs[i % len(pairs)]
        return c, 2 * t + j, slice(c * 128, (c + 1) * 128), pair_cols(t, j)

    def grad_probs(i, v):
        c, p, at, cs = place(i)
        g = s.gmix[at, cs]
        go = (g.astype(F32) * s.mix[at, cs].astype(F32)).astype(BF)
        vv = jnp.concatenate([s.v[at, cs], s.vs[at, cs]], axis=0)
        v["dp"] = nt(jnp.concatenate([vv, jnp.full_like(vv, -1.0)], axis=1),
                     jnp.concatenate([stack_heads(g), stack_heads(go)], axis=1))

    def grad_scores(i, v):
        c, p, at, cs = place(i)
        v["ds"] = (s.pr[p, c].astype(F32) * v.pop("dp")).astype(BF)

    def products(i, v):
        c, p, at, cs = place(i)
        ds = v.pop("ds")
        dkk = nn(ds, stack_heads(s.q[at, cs]))
        dvv = nn(s.pr[p, c], stack_heads(s.gmix[at, cs]))
        s.dk[at, cs] = dkk[:128]
        s.dks[at, cs] = dkk[128:].astype(BF)
        s.dv[at, cs] = dvv[:128]
        s.dvs[at, cs] = dvv[128:].astype(BF)
        kk = jnp.concatenate([s.k[at, cs], s.ks[at, cs]], axis=0)
        v["dq"] = pick_rows(nn(jnp.transpose(kk, (1, 0)), ds))

    def store(i, v):
        c, p, at, cs = place(i)
        s.dq[at, cs] = jnp.transpose(v.pop("dq"), (1, 0)) * scale
    pipeline(range(8 * len(pairs)), (grad_probs, grad_scores, products, store), (0, 2, 4, 6), after)


def heads_at(t, pairs):
    n = 2 * NB
    return pl.ds(pl.multiple_of(t * 2 * n + pairs[0] * n, n), n * len(pairs))


def st_sort_back(s, t, pairs):
    a, b = iota((128, 128), 0), iota((128, 128), 1)
    same = ((a >> 2) & 3) == ((b >> 2) & 3)
    accs = {j: [] for j in pairs}

    def mix(i, v):
        j, rq = pairs[i // 8], i % 8
        cs = pair_cols(t, j)
        kv = jnp.concatenate([gather_chunk(s.k, rq, cs), gather_chunk(s.v, rq, cs)], axis=1)
        st = split_pair(jnp.concatenate([gather_chunk(s.dks, rq, cs), gather_chunk(s.dvs, rq, cs)], axis=1))
        accs[j].append(nt(st, kv))
        h = 4 * t + 2 * j
        v["out"] = nn(jnp.concatenate([s.krt[h], s.krt[h + 1]], axis=1), st)

    def store(i, v):
        j, rq = pairs[i // 8], i % 8
        cs = pair_cols(t, j)
        out = v.pop("out")
        for n in range(8):
            at = slice(n * 128 + rq * 16, n * 128 + rq * 16 + 16)
            s.dk[at, cs] = s.dk[at, cs] + out[n * 16:(n + 1) * 16, 0:128]
            s.dvb[at, cs] = (s.dv[at, cs] + out[n * 16:(n + 1) * 16, 128:256]).astype(BF)
    pipeline(range(8 * len(pairs)), (mix, store), (0, 2))

    def fold():
        heads = 2 * len(pairs)
        x = jnp.concatenate([sum(accs[j]) for j in pairs], axis=0)
        x = jnp.where(jnp.concatenate([same] * heads, axis=0), x, 0.0)
        n = iota((128, NB), 0)
        cols_of = (((n >> 4) * 4 + (n & 3)) == iota((128, NB), 1)).astype(BF)
        m, n = iota((heads * NB, heads * 128), 0), iota((heads * NB, heads * 128), 1)
        rows_of = ((m >> 5) == (n >> 7)) & ((m & 31) == ((n >> 4) & 7) * 4 + (n & 3))
        high, low = two_terms(x)
        high, low = two_terms(nn(high, cols_of) + nn(low, cols_of))
        rows_of = rows_of.astype(BF)
        s.ds[heads_at(t, pairs), :] = nn(rows_of, high) + nn(rows_of, low)
    return fold


def two_terms(x):
    high = x.astype(BF)
    return high, (x - high.astype(F32)).astype(BF)


def sinkhorn_back(s, t, pairs):
    hs, n = heads_at(t, pairs), 2 * len(pairs)
    v = {}

    def sweep(it):
        x = v["x"] if it < ITERS - 1 else s.ds[hs, :] * s.sk[2 * ITERS - 1, hs, :]
        y = x.reshape(n, NB, NB)
        pk = s.sk[2 * it + 1, hs, :].reshape(n, NB, NB)
        x = (y - pk * jnp.sum(y, axis=1, keepdims=True)).reshape(n * NB, NB)
        v["x"] = x - s.sk[2 * it, hs, :] * jnp.sum(x, axis=1, keepdims=True)

    def means():
        mask = jnp.concatenate([s.allow[...]] * n, axis=0) > 0
        x = jnp.where(mask, v.pop("x"), 0.0) * (1.0 / math.sqrt(HD))
        for h, j in enumerate(pairs):
            cs = pair_cols(t, j)
            x0, x1 = x[2 * h * NB:(2 * h + 1) * NB], x[(2 * h + 1) * NB:(2 * h + 2) * NB]
            ev = even_lanes((NB, 128))
            km, qm = s.km[:, cs], s.qm[:, cs]
            v[j] = (jnp.where(ev, nn(x0, km, precision=HI), nn(x1, km, precision=HI)),
                    jnp.where(ev, tn(x0, qm, precision=HI), tn(x1, qm, precision=HI)))

    def spread(j):
        cs = pair_cols(t, j)
        dqm, dkm = v.pop(j)
        for c in range(8):
            at = slice(c * 128, (c + 1) * 128)
            for src, ref, dst in ((dqm, s.dq, s.dqb), (dkm, s.dk, s.dkb)):
                four = src[c * 4:(c + 1) * 4]
                eight = jnp.concatenate([four, four], axis=0)
                val = ref[at, cs].reshape(16, 8, 128) + eight[None]
                dst[at, cs] = val.reshape(128, 128).astype(BF)
    steps = [functools.partial(sweep, it) for it in reversed(range(ITERS))]
    return steps + [means] + [functools.partial(spread, j) for j in pairs]


def st_value_grads(s, g, other, t, own, part):
    val = nn(s.nmt[part * 256:(part + 1) * 256, :], s.dvb[:, half_cols(t)])
    if own:
        val = val + other[2 * part:2 * part + 2, :, :, VO:OO].reshape(256, HALF).astype(F32)
    g[t, 2 * part:2 * part + 2, :, :, VO:OO] = val.astype(BF).reshape(2, 4, D // 16, HALF)


def st_query_key_grads(s, g, other, t, own, pairs):
    for j in pairs:
        cs = pair_cols(t, j)
        add_grads(g, other, t, own, slice(j * 256, (j + 1) * 256),
                  nn(s.nmt[...], jnp.concatenate([s.dqb[:, cs], s.dkb[:, cs]], axis=1)))


def st_tokens_back(s, w, gain_attn, out):
    parts = []

    def product(m, v):
        at = rows(m, 256)
        v["g"] = 0.0
        for t in range(2):
            cs = slice(t * 256, (t + 1) * 256)
            dq, dk = s.dqb[at, cs], s.dkb[at, cs]
            lhs = jnp.concatenate([dq[:, :128], dk[:, :128], dq[:, 128:], dk[:, 128:], s.dvb[at, cs]], axis=1)
            v["g"] = v["g"] + nt(lhs, w[t, :, 0:OO])

    def norm(m, v):
        at = rows(m, 256)
        gn = v.pop("g")
        xhat, inv = norm_rows(s.tokp[at, :].astype(F32), None)
        parts.append(jnp.sum((gn * xhat).reshape(32, 8, D), axis=0))
        out[at, :] = (s.mid[at, :] + norm_back(xhat, inv, gain_attn[...], gn)).astype(BF)
    pipeline(range(4), (product, norm), (0, 1))
    s.gg[0:1, :] = jnp.sum(sum(parts), axis=0, keepdims=True)


def attention_backward(s, w, g, other, c, gain_attn, out, hooks):
    own, both = other is not None, (0, 1)

    def with_steps(steps):
        return lambda n: steps[n]() if n < len(steps) else None
    st_attend_back(s, 1 - c, both)
    hooks["attend0"]()
    fold = st_sort_back(s, 1 - c, both)
    hooks["sort0"]()
    st_attend_back(s, c, (0,), with_steps([fold] + sinkhorn_back(s, 1 - c, both)))
    for part in range(2):
        st_value_grads(s, g, None, 1 - c, False, part)
    st_query_key_grads(s, g, None, 1 - c, False, both)
    hooks["first"]()
    fold = st_sort_back(s, c, (0,))
    st_attend_back(s, c, (1,), with_steps([fold] + sinkhorn_back(s, c, (0,))))
    hooks["pair"]()
    st_query_key_grads(s, g, other, c, own, (0,))
    hooks["queries"]()
    steps = [st_sort_back(s, c, (1,))] + sinkhorn_back(s, c, (1,))
    for n, step in enumerate(steps):
        step()
        if n in (0, 2):
            st_value_grads(s, g, other, c, own, n // 2)
        if n == 3:
            hooks["values"]()
    st_query_key_grads(s, g, other, c, own, (1,))
    hooks["last"]()
    st_tokens_back(s, w, gain_attn, out)


class Names:
    pass


def stage_names(refs):
    s = Names()
    for n, r in zip(SCRATCH, refs):
        setattr(s, n, r)
    for n, o in SHARED.items():
        setattr(s, n, getattr(s, o))
    return s


def layer_kernel(tok, cot, gain_attn, gain_ffn, w, seg, result, gtok, g, gg, *scr):
    s = stage_names(scr)
    st_tokens(s, tok, gain_attn)
    st_cot(s, cot)
    transpose_into(s.cott, s.cotp)
    transpose_into(s.nmt, s.nm)
    st_bias(s)
    for t in range(2):
        st_query_key(s, w, t)
    st_sinkhorn(s, seg)
    st_values(s, w)
    st_sort(s)
    loop(2, functools.partial(st_attend, s))
    st_out(s, w, gain_ffn)
    transpose_into(s.nft, s.nf)
    def ffn(u):
        for t in range(2):
            st_ffn(s, w, t, u, result if t == 1 else None)
            st_ffn_grads(s, g, None, t, u, False)
    loop(2, ffn)
    st_mid_back(s, w, gain_ffn)
    for t in range(2):
        st_out_grads(s, g, None, t, False)
    attention_backward(s, w, g, None, 0, gain_attn, gtok, collections.defaultdict(lambda: lambda: None))
    st_restore(result)
    st_restore(gtok)
    gg[...] = s.gg[...]


def layer_call():
    vm = pl.BlockSpec(memory_space=pltpu.VMEM)
    return pl.pallas_call(
        layer_kernel,
        out_shape=(jax.ShapeDtypeStruct((T, D), BF), jax.ShapeDtypeStruct((T, D), BF),
                   jax.ShapeDtypeStruct((2, 4, 4, D // 16, COLS), BF), jax.ShapeDtypeStruct((8, D), F32)),
        in_specs=[vm] * 6, out_specs=(vm,) * 4,
        scratch_shapes=[pltpu.VMEM(*v) for v in SCRATCH.values()],
        compiler_params=pltpu.CompilerParams(vmem_limit_bytes=60 << 20),
    )


def last_kernel(res, gtok, grads, gains, result, grad_tokens, gain_a, gain_f, gq, gk, gv, go, gi, gd, hold, held, sems):
    sem = iter(range(sems.shape[0]))

    def copy(src, dst):
        return pltpu.make_async_copy(src, dst, sems.at[next(sem)])
    moves = [(copy(grads, held), [copy(held.at[:, cols], ref.at[:, at]) for cols, ref, at in places(gq, gk, gv, go, gi, gd)])]
    for half in range(res.shape[0]):
        for n, (src, dst) in enumerate(((res, result), (gtok, grad_tokens))):
            moves.append((copy(src.at[half], hold.at[n, half]), [copy(hold.at[n, half], dst.at[half])]))
    for cp, _ in moves:
        cp.start()
    width = gain_a.shape[1]
    gain_a[...] = gains[0:1, 0:width]
    gain_f[...] = gains[1:2, 0:width]
    for cp, outs in moves:
        cp.wait()
        for out in outs:
            out.start()
    for _, outs in moves:
        for out in outs:
            out.wait()


def places(gq, gk, gv, go, gi, gd):
    runs = [(slice(VO, OO), gv, slice(0, HALF)), (slice(OO, FO), go, slice(0, HALF))]
    for j in range(2):
        at = slice(j * 128, (j + 1) * 128)
        runs += [(slice(j * 256, j * 256 + 128), gq, at), (slice(j * 256 + 128, (j + 1) * 256), gk, at)]
    for u in range(STEPS):
        at = slice(u * UNITS, (u + 1) * UNITS)
        runs += [(in_cols(u), gi, at), (down_cols(u), gd, at)]
    return runs


def last_call(res, gtok, grads, gains, width):
    vm, hbm = pl.BlockSpec(memory_space=pltpu.VMEM), pl.BlockSpec(memory_space=pl.ANY)
    square, long, row = (grads.shape[0], HALF), (grads.shape[0], FF // 2), (1, width)
    outs = [row, row, square, square, square, square, long, long]
    return pl.pallas_call(
        last_kernel,
        out_shape=(jax.ShapeDtypeStruct(res.shape, BF),) * 2 + tuple(jax.ShapeDtypeStruct(x, F32) for x in outs),
        in_specs=[hbm, hbm, hbm, vm],
        out_specs=(hbm, hbm, vm, vm) + (hbm,) * 6,
        scratch_shapes=[pltpu.VMEM((2,) + res.shape, BF), pltpu.VMEM(grads.shape, F32),
                        pltpu.SemaphoreType.DMA((7 + 4 * res.shape[0] + 2 * STEPS,))],
    )(res, gtok, grads, gains)


def join_cols(q, k, v, o, i, d):
    parts = []
    for j in range(2):
        parts += [q[:, j * 128:(j + 1) * 128], k[:, j * 128:(j + 1) * 128]]
    parts += [v, o]
    for u in range(STEPS):
        parts += [i[:, u * UNITS:(u + 1) * UNITS], d[:, u * UNITS:(u + 1) * UNITS]]
    return jnp.concatenate(parts, axis=1)


def by_collectives(tokens, gain_attn, gain_ffn, w_query, w_key, w_value, w_out, w_in, w_down, segment_ids, cotangent):
    tp = lax.axis_index("tp")
    tok = lax.all_to_all(tokens, "tp", 0, 0, tiled=True).reshape(T, D)
    cot = lax.all_to_all(cotangent, "tp", 0, 0, tiled=True).reshape(T, D)
    own = join_cols(w_query, w_key, w_value, w_out.T, w_in, w_down.T)
    half = lax.all_gather(own, "fsdp", axis=0, tiled=True)
    w = lax.all_gather(half, "tp", axis=0)
    seg = lax.dynamic_index_in_dim(segment_ids, tp, 0)
    res, gtok, g, gg = layer_call()(tok, cot, gain_attn[None], gain_ffn[None], w, seg)
    res = lax.all_to_all(res.reshape(tokens.shape), "tp", 0, 0, tiled=True)
    gtok = lax.all_to_all(gtok.reshape(tokens.shape), "tp", 0, 0, tiled=True)
    gsum = lax.psum_scatter(g.reshape(2, D, COLS).astype(F32), "tp", scatter_dimension=0)
    gsum = lax.psum_scatter(gsum, "fsdp", scatter_dimension=0, tiled=True)
    gains = lax.psum_scatter(gg, ("fsdp", "tp"), scatter_dimension=1, tiled=True)
    return finish(res, gtok, gsum, gains, gains.shape[1])


def finish(res, gtok, grads, gains, width):
    res, gtok, gain_a, gain_f, q, k, v, o, i, d = last_call(res, gtok, grads, gains, width)
    return res, gtok, gain_a.reshape(width), gain_f.reshape(width), q, k, v, o.T, i, d.T


PIECES = ((0, 512), (512, 768), (768, 1024), (1024, 2048), (2048, 3072))
GPIECES = ((1024, 2048), (2048, 3072), (768, 1024), (512, 768), (0, 256), (256, 512))
MESH = pl.DeviceIdType.MESH
ROWS = D // 16

EXCHANGE = dict(
    w=((2, D, COLS), BF), g=((2, 4, 4, ROWS, COLS), BF), other=((4, 4, ROWS, COLS), BF),
    rx=((3, 4, ROWS, COLS), BF), zs=((4, ROWS, COLS), BF), rz=((3, ROWS, COLS), BF),
    tok=((T, D), BF), cot=((T, D), BF), gr=((7, 8, D), F32), gs=((3, 8, D), F32),
)


def halves(lo, hi):
    mid = (lo + hi) // 2
    return slice(lo, mid), slice(mid, hi)


class Links:
    def __init__(self, e, sems):
        self.e = e
        self.sems = sems
        f, self.c = lax.axis_index("fsdp"), lax.axis_index("tp")
        self.zi, self.xy = f // 4, f % 4
        x, y = self.xy % 2, self.xy // 2
        self.f = f
        self.across = {"x": (1 - x) + 2 * y, "y": x + 2 * (1 - y), "d": (1 - x) + 2 * (1 - y)}
        self.arrival, self.sent = {}, []
        self.fixed = {}

    def z_at(self, dz):
        return (self.zi + dz) % 4

    def z_from(self, dz):
        return (self.zi + 4 - dz) % 4

    def greet(self):
        self.bar = pltpu.get_barrier_semaphore()
        for dev in ([(self.z_at(d) * 4 + self.xy, self.c) for d in (1, 2, 3)]
                    + [(self.zi * 4 + k, self.c) for k in self.across.values()] + [(self.f, 1 - self.c)]):
            pl.semaphore_signal(self.bar, inc=1, device_id=dev, device_id_type=MESH)

    def meet(self):
        pl.semaphore_wait(self.bar, 7)

    def w_rows(self, first, count, cols):
        return self.e.w.at[self.c, pl.ds(pl.multiple_of(first * ROWS, count * ROWS), count * ROWS), cols]

    def mine(self, k, cols):
        return self.e.g.at[self.c, :, self.across[k], :, cols]

    def route(self, kind, *key):
        e = self.e
        if kind in self.fixed:
            return self.fixed[kind][key[0]] + ("t",)
        if kind in ("z", "zz", "x", "y", "d", "xy", "yx", "t"):
            piece, d = key
            cols = slice(*PIECES[piece])
            first, second = halves(*PIECES[piece])
            if kind == "z":
                at, to = self.w_rows(self.f, 1, cols), d
            elif kind == "zz":
                at, to = self.w_rows(self.zi * 4, 4, cols), d
            elif kind == "t":
                at, to = self.w_rows(self.z_from(d) * 4, 4, cols), "t"
            elif kind == "xy":
                at, to = self.w_rows(self.z_from(d) * 4 + self.across["x"], 1, first), "y"
            elif kind == "yx":
                at, to = self.w_rows(self.z_from(d) * 4 + self.across["y"], 1, second), "x"
            else:
                at, to = self.w_rows(self.z_from(d) * 4 + self.xy, 1, cols), kind
            return at, at, to
        if kind == "n":
            n = key[0]
            return e.gs.at[0 if n == 0 else 1 if n < 4 else 2], e.gr.at[n], "t" if n == 0 else "xyd"[n - 1] if n < 4 else n - 3
        piece = key[0]
        if kind == "gt":
            lo, hi = GPIECES[piece] if piece < 3 else (0, OO)
            return e.g.at[1 - self.c, :, :, :, lo:hi], e.other.at[:, :, :, lo:hi], "t"
        cols = slice(*GPIECES[piece])
        if kind == "gz":
            d = key[1]
            return e.zs.at[d, :, cols], e.rz.at[d - 1, :, cols], d
        to = kind[1]
        if len(key) > 1:
            cols = halves(*GPIECES[piece])[key[1]]
            if kind == "gd":
                to = "xy"[key[1]]
        return self.mine(kind[1], cols), e.rx.at["xyd".index(kind[1]), :, :, cols], to

    def copy(self, key):
        src, dst, to = self.route(*key)
        if isinstance(to, int):
            dev = (self.z_at(to) * 4 + self.xy, self.c)
        elif to == "t":
            dev = (self.f, 1 - self.c)
        else:
            dev = (self.zi * 4 + self.across[to], self.c)
        sent = self.sent.index(key) % NSEND if key in self.sent else 0
        return pltpu.make_async_remote_copy(
            src_ref=src, dst_ref=dst, send_sem=self.sems[0].at[sent],
            recv_sem=self.sems[1].at[self.arrival.setdefault(key, len(self.arrival))], device_id=dev, device_id_type=MESH)

    def send(self, *key):
        self.sent.append(key)
        if len(self.sent) > NSEND:
            self.copy(self.sent[-1 - NSEND]).wait_send()
        self.copy(key).start()

    def arrived(self, *key):
        self.copy(key).wait_recv()

    def finish(self):
        assert len(self.sent) == len(self.arrival) == NSEM, len(self.sent)
        for key in self.sent[-NSEND:]:
            self.copy(key).wait_send()

    def own_z(self, piece):
        for d in (1, 2, 3):
            self.send("z", piece, d)

    def own_plane(self, piece):
        self.to_plane(piece, 0)

    def to_plane(self, piece, d):
        for k in "xyd" if piece < 3 else "xy":
            self.send(k, piece, d)

    def plane(self, piece, d):
        self.arrived("z", piece, d)
        self.to_plane(piece, d)

    def corner(self, piece, d):
        self.arrived("x", piece, d)
        self.send("xy", piece, d)
        self.arrived("y", piece, d)
        self.send("yx", piece, d)

    def pair(self, piece, d):
        for k in ("x", "y", "d") if piece < 2 else ("xy", "yx"):
            self.arrived(k, piece, d)
        self.send("t", piece, d)

    def turn(self, piece):
        for k in "xyd":
            self.arrived(k, piece, 0)
        for d in (1, 2, 3):
            self.send("zz", piece, d)
        self.send("t", piece, 0)

    def turned(self, piece):
        for d in (1, 2, 3):
            self.arrived("zz", piece, d)
            self.send("t", piece, d)

    def gathered(self, piece):
        for d in range(4):
            self.arrived("t", piece, d)

    def grads_pair(self, piece):
        self.send("gt", piece)

    def grads_plane(self, piece):
        for k in "xyd":
            self.send("g" + k, piece)

    def grads_part(self, piece):
        self.send("gd", piece, 0)
        self.send("gd", piece, 1)
        self.send("gx", piece, 0)
        self.send("gy", piece, 1)

    def grads_join(self, piece):
        first, second = halves(*GPIECES[piece])
        for n, k, cols in ((0, "y", first), (1, "x", second)):
            self.arrived("gd", piece, n)
            at = self.mine(k, cols)
            at[...] = (at[...].astype(F32) + self.e.rx[2, :, :, cols].astype(F32)).astype(BF)
            self.send("g" + k, piece, n)

    def grads_line(self, piece, direct):
        e = self.e
        cols = slice(*GPIECES[piece])
        if direct:
            for k in "xyd":
                self.arrived("g" + k, piece)
        else:
            for k in "xy":
                for n in range(2):
                    self.arrived("g" + k, piece, n)
        for d in (1, 2, 3, 0):
            z = self.z_at(d)
            total = e.g[self.c, z, self.xy, :, cols].astype(F32)
            for n in range(3 if direct else 2):
                total = total + e.rx[n, z, :, cols].astype(F32)
            if d:
                e.zs[d, :, cols] = total.astype(BF)
                self.send("gz", piece, d)
            else:
                self.out[:, cols] = total

    def grads_in(self, piece):
        cols = slice(*GPIECES[piece])
        for n in range(3):
            self.arrived("gz", piece, n + 1)
        total = self.out[:, cols]
        for n in range(3):
            total = total + self.e.rz[n, :, cols].astype(F32)
        self.out[:, cols] = total

    def gains_sum(self, step):
        e = self.e
        if step == 0:
            self.send("n", 0)
        if step == 1:
            self.arrived("n", 0)
            e.gs[1] = e.gs[0] + e.gr[0]
            for n in (1, 2, 3):
                self.send("n", n)
        if step == 2:
            for n in (1, 2, 3):
                self.arrived("n", n)
            e.gs[2] = e.gs[1] + e.gr[1] + e.gr[2] + e.gr[3]
            for n in (4, 5, 6):
                self.send("n", n)
        if step == 3:
            for n in (4, 5, 6):
                self.arrived("n", n)
            return e.gs[2] + e.gr[4] + e.gr[5] + e.gr[6]


NSEM = 154
NSEND = 24


def step_kernel(tokens, cotangent, gain_attn, gain_ffn, wq, wk, wv, wo, wi, wd, seg, result, gtok, gout, gains, *scr):
    ns, ne = len(SCRATCH), len(EXCHANGE)
    s = stage_names(scr[:ns])
    e = Names()
    for n, r in zip(EXCHANGE, scr[ns:ns + ne]):
        setattr(e, n, r)
    send_sem, recv_sem, local = scr[ns + ne:]
    link = Links(e, (send_sem, recv_sem))
    link.out = gout
    c, f, w, g = link.c, link.f, e.w, e.g
    half = T // 2
    mine = pl.ds(pl.multiple_of(c * half, half), half)
    theirs = pl.ds(pl.multiple_of((1 - c) * half, half), half)
    four, three = range(4), (1, 2, 3)

    link.fixed = {"in": [(tokens.at[1 - c], e.tok.at[mine, :]), (cotangent.at[1 - c], e.cot.at[mine, :])],
                  "out": [(e.cot.at[theirs, :], gtok.at[c]), (e.tok.at[theirs, :], result.at[c])]}
    loads = [pltpu.make_async_copy(tokens.at[c], e.tok.at[mine, :], local.at[0]),
             pltpu.make_async_copy(cotangent.at[c], e.cot.at[mine, :], local.at[1])]
    for cp in loads:
        cp.start()
    link.greet()
    w[c, pl.ds(pl.multiple_of(f * ROWS, ROWS), ROWS), :] = join_cols(wq[...], wk[...], wv[...], wo[...], wi[...], wd[...])
    link.meet()
    link.own_z(0)
    link.own_plane(0)
    link.send("in", 0)
    link.send("in", 1)
    link.own_z(1)
    link.own_plane(1)
    link.own_plane(2)
    loads[0].wait()
    link.arrived("in", 0)
    st_tokens(s, e.tok, gain_attn)
    loads[1].wait()
    link.arrived("in", 1)
    st_cot(s, e.cot)
    transpose_into(s.nmt, s.nm)
    for d in three:
        link.plane(0, d)
    link.own_z(3)
    transpose_into(s.cott, s.cotp)
    st_bias(s)
    for d in three:
        link.plane(1, d)
    link.own_plane(3)
    link.turn(2)
    for d in four:
        link.pair(0, d)
    link.own_z(4)
    st_query_key(s, w, c)
    link.gathered(0)
    st_query_key(s, w, 1 - c)
    link.plane(3, 1)
    link.plane(3, 2)

    def halfway():
        for d in four:
            link.pair(1, d)
        link.plane(3, 3)
    st_sinkhorn(s, seg.at[pl.ds(c, 1), :], halfway)
    link.gathered(1)
    st_values(s, w)
    link.corner(3, 0)
    link.corner(3, 1)
    st_sort(s)
    link.corner(3, 2)
    link.corner(3, 3)
    link.own_plane(4)
    st_attend(s, 0)
    link.pair(3, 0)
    link.pair(3, 1)
    link.turned(2)
    link.plane(4, 1)
    link.plane(4, 2)
    link.plane(4, 3)
    st_attend(s, 1)
    link.pair(3, 2)
    link.pair(3, 3)
    link.corner(4, 0)
    link.gathered(2)
    st_out(s, w, gain_ffn)
    transpose_into(s.nft, s.nf)
    link.gathered(3)

    def ffn(u):
        early, late = u == 0, u == 1
        @pl.when(late)
        def _():
            link.gathered(4)

        st_ffn(s, w, 1 - c, u, None)

        @pl.when(early)
        def _():
            for d in three:
                link.corner(4, d)
        st_ffn_grads(s, g, None, 1 - c, u, False)
        for n in range(2):
            pl.when(u == n)(functools.partial(link.grads_pair, n))
        st_ffn(s, w, c, u, e.tok)

        @pl.when(early)
        def _():
            for d in four:
                link.pair(4, d)
            link.arrived("gt", 0)

        @pl.when(late)
        def _():
            link.grads_join(0)
            link.arrived("gt", 1)
        st_ffn_grads(s, g, e.other, c, u, True)
        for n in range(2):
            pl.when(u == n)(functools.partial(link.grads_part, n))
    loop(2, ffn)
    st_mid_back(s, w, gain_ffn)
    st_out_grads(s, g, None, 1 - c, False)
    link.grads_pair(2)

    def attend0():
        link.arrived("gt", 2)
        st_out_grads(s, g, e.other, c, True)
        link.grads_plane(2)
        link.grads_line(0, False)

    def sort0():
        link.grads_join(1)

    def first():
        link.grads_pair(3)

    def pair():
        link.arrived("gt", 3)

    def queries():
        link.grads_plane(4)
        link.grads_line(1, False)

    def values():
        link.grads_part(3)
        link.grads_line(2, True)

    def last():
        link.grads_plane(5)

    attention_backward(s, w, g, e.other, c, gain_attn, e.cot, {
        "attend0": attend0, "sort0": sort0, "first": first, "pair": pair, "queries": queries, "values": values, "last": last})
    link.grads_join(3)
    e.gs[0] = s.gg[...]
    link.gains_sum(0)
    stores = []
    for n, (buf, out) in enumerate(((e.cot, gtok), (e.tok, result))):
        st_restore(buf)
        stores.append(pltpu.make_async_copy(buf.at[mine, :], out.at[c], local.at[2 + n]))
        stores[n].start()
        link.send("out", n)
    link.grads_line(4, True)
    link.gains_sum(1)
    link.grads_in(0)
    link.grads_in(2)
    link.grads_line(5, True)
    link.gains_sum(2)
    link.grads_line(3, False)
    link.grads_in(1)
    link.grads_in(4)
    link.grads_in(3)
    link.arrived("out", 0)
    link.arrived("out", 1)
    for cp in stores:
        cp.wait()
    total = link.gains_sum(3)
    width = D // 32
    pick = (iota((D, 128), 0) == iota((D, 128), 1) + (2 * f + c) * width).astype(F32)
    gains[...] = nn(total, pick, precision=HI)
    link.grads_in(5)
    link.finish()


def by_kernel(tokens, gain_attn, gain_ffn, w_query, w_key, w_value, w_out, w_in, w_down, segment_ids, cotangent):
    vm, hbm = pl.BlockSpec(memory_space=pltpu.VMEM), pl.BlockSpec(memory_space=pl.ANY)
    shapes = list(SCRATCH.values()) + list(EXCHANGE.values())
    res, gtok, grads, gains = pl.pallas_call(
        step_kernel,
        out_shape=(jax.ShapeDtypeStruct(tokens.shape, BF), jax.ShapeDtypeStruct(tokens.shape, BF),
                   jax.ShapeDtypeStruct((ROWS, COLS), F32), jax.ShapeDtypeStruct((8, 128), F32)),
        in_specs=[hbm] * 2 + [vm] * 9, out_specs=(hbm, hbm, vm, vm),
        scratch_shapes=[pltpu.VMEM(*v) for v in shapes] + [
            pltpu.SemaphoreType.DMA((NSEND,)), pltpu.SemaphoreType.DMA((NSEM,)), pltpu.SemaphoreType.DMA((4,))],
        compiler_params=pltpu.CompilerParams(collective_id=0, has_side_effects=True, vmem_limit_bytes=63 << 20),
    )(tokens, cotangent, gain_attn[None], gain_ffn[None], w_query, w_key, w_value, w_out.T, w_in, w_down.T, segment_ids)
    return finish(res, gtok, grads, gains, D // 32)


def solution(mesh):
    body = by_kernel if mesh.shape["fsdp"] == 16 else by_collectives
    return jax.shard_map(
        body,
        mesh=mesh,
        in_specs=(P(None, ("fsdp", "tp"), None), P(), P(), P("fsdp", "tp"), P("fsdp", "tp"), P("fsdp", "tp"),
                  P("tp", "fsdp"), P("fsdp", "tp"), P("tp", "fsdp"), P(None, "fsdp"), P(None, ("fsdp", "tp"), None)),
        out_specs=(P(None, ("fsdp", "tp"), None), P(None, ("fsdp", "tp"), None), P(("fsdp", "tp")), P(("fsdp", "tp")),
                   P("fsdp", "tp"), P("fsdp", "tp"), P("fsdp", "tp"), P("tp", "fsdp"), P("fsdp", "tp"), P("tp", "fsdp")),
        check_vma=False,
    )
```
